32 devices in a mesh: blk: 8 (over z, y), aux: 4 (over x, core).
Axes of the slice: x: 2, y: 2, z: 4, core: 2. Of those that a mesh axis runs over, the one named last changes fastest.
Arguments:
- adjoint: bfloat16 [1024, 1024], P(('blk', 'aux')), may hold values from -0.1875 to 0.1875
- three_centre: bfloat16 [128, 32, 32, 1024], P(('blk', 'aux')), may hold values from -1 to 1
- occ_density: bfloat16 [64, 1024], P('blk'), may hold values from -1 to 1
- vir_density: bfloat16 [64, 1024], P('blk'), may hold values from -1 to 1
- block_sizes: int32 [64], P('blk'), may hold values from 16 to 32
- tile_rows: int32 [128], P(('blk', 'aux')), may hold values from 0 to 7
- col_owner: int32 [128, 1], P(('blk', 'aux')), may hold values from 0 to 7; in each aligned block of 16 rows (0 to 15, 16 to 31, ...) at most 4 rows name the same one
- col_block: int32 [128], P(('blk', 'aux')), may hold values from 0 to 7
Outputs:
- occ_grad: float32 [64, 1024], P(('blk', 'aux'))
- vir_grad: float32 [64, 1024], P(('blk', 'aux'))
The draws below stay inside these ranges and needn't reach their ends.
Inputs may be any that keep to these rules, and one draw needn't show every extreme that they name: `col_owner`: among the 16 tiles of one blk index (aligned blocks of 16 tiles), at most 4 name the same owner, and some blk index reaches 4.
All inputs are finite; a program needn't handle non-finite values.
Results may differ from the reference program's by a relative error of at most 0.0041.
Values may be sent and summed in bfloat16 or wider, within the bound.
A program may use at most 128 MiB of HBM per device.

```python
import math
import jax
import jax.numpy as jnp
import numpy as np
from jax import lax

BS = 32
NAUX = 1024
BLK_DEV = 8
TILE_DEV = 4
TILES_ROW = 16
CAP = 4
NB = 64
NTILE = 128
N_BLK = 8


def plant(values, stream_key, smallest, top_value):
    longest = values.shape.index(max(values.shape))
    spots = []
    for shift in (0, 1):
        where = [jax.random.randint(jax.random.fold_in(stream_key, axis), (), 0, length) for axis, length in enumerate(values.shape)]
        where[longest] = (where[longest] + shift) % values.shape[longest]
        spots.append(tuple(where))
    return values.at[spots[0]].set(smallest).at[spots[1]].set(top_value)


def block_scale(key, dims, shards, low, high):
    def one(axis_at, parts):
        heights = jax.random.uniform(jax.random.fold_in(jax.random.fold_in(key, 6), axis_at), (parts,), jnp.float32, low / len(shards), high / len(shards))
        return jnp.repeat(jnp.exp(heights), dims[axis_at] // parts).reshape((-1,) + (1,) * (len(dims) - axis_at - 1))

    level = one(*shards[0])
    for cut in shards[1:]:
        level = level * one(*cut)
    return level


def assign_block(rng, own, number, rows, amount, top, most, slope):
    order = jax.random.permutation(rng, amount)
    packed, ordinary = portions_of(amount, rows * top, most, slope, True), portions_of(amount, rows * top, most, slope, False)
    places = jnp.arange(amount)

    def named(tallies, rotation):
        used = int((tallies > 0).sum())
        fixed = max(1, used // 4)
        shifted = fixed + (places - fixed + rotation * (used - fixed)) % max(1, amount - fixed)
        return jnp.zeros((amount,), jnp.int32).at[order[jnp.where(places < fixed, places, shifted)]].set(jnp.asarray(tallies, jnp.int32))

    tallies = jnp.where(number % 4 == 0, named(packed, number // 4), named(ordinary, number - number // 4 - 1))
    mixed = jax.random.permutation(jax.random.fold_in(own, 3), amount)
    source_of, taker = mixed[0:amount // 2 * 2:2], mixed[1:amount // 2 * 2:2]
    slack = jnp.minimum(tallies[source_of] - 1, most - tallies[taker]) // 2
    slack = jnp.where((source_of == order[0]) | (taker == order[0]) | (tallies[taker] == 0), 0, jnp.maximum(slack, 0))
    shifted = jax.random.randint(jax.random.fold_in(own, 4), (amount // 2,), 0, 1 << 20) % (slack + 1)
    tallies = tallies.at[source_of].add(-shifted).at[taker].add(shifted)
    items = jnp.searchsorted(jnp.cumsum(tallies), jnp.arange(rows * top), side="right").astype(jnp.int32)
    listing = items.reshape(top, rows).T
    listing = listing[jax.random.permutation(jax.random.fold_in(own, 1), rows)]
    rotation = jax.random.randint(jax.random.fold_in(own, 2), (rows, 1), 0, top)
    return jnp.take_along_axis(listing, (jnp.arange(top)[None, :] + rotation) % top, axis=1)


def portions_of(count, total, limit, slope, full):
    portions = [(1 << 20) // math.isqrt(rank ** slope) + 1 for rank in range(1, count + 1)]
    largest = limit if full else min(limit, max(-(-total // count), total * portions[0] // sum(portions)))
    least = 1 if total - largest >= count - 1 else 0
    counts, spare = [largest] + [least] * (count - 1), total - largest - least * (count - 1)
    while spare > 0:
        movable = [i for i in range(1, count) if counts[i] < largest] or [i for i in range(1, count) if counts[i] < limit]
        pool, budget = sum([portions[i] for i in movable]), spare
        for i in movable:
            extra = min(limit - counts[i], max(1, budget * portions[i] // pool), spare)
            counts[i] = counts[i] + extra
            spare = spare - extra
    return np.array(counts)


def bell_draw(stream_key, dims, width, bound, split=(), held_as=jnp.bfloat16):
    level = block_scale(stream_key, dims, split, -0.22, 0.18) if split else 1.0
    entries = jax.random.normal(stream_key, dims, jnp.float32) * width * level
    return jnp.minimum(jnp.maximum(entries, -bound), bound).astype(held_as)


def setup_inputs(seed: int = 0) -> dict:
    key_of = jax.random.split(jax.random.key(seed), 9)
    adjoint = bell_draw(key_of[0], (NAUX, NAUX), NAUX ** -0.5, 0.1875, ((0, 32),))
    three_centre = bell_draw(key_of[1], (NTILE, BS, BS, NAUX), BS ** -0.5, 1.0, ((0, 32),))
    occ_density = bell_draw(key_of[2], (NB, BS * BS), BS ** -0.5, 1.0, ((0, 8),))
    vir_density = bell_draw(key_of[3], (NB, BS * BS), BS ** -0.5, 1.0, ((0, 8),))
    block_sizes = plant(jax.random.randint(key_of[4], (NB,), BS // 2, BS + 1), jax.random.fold_in(key_of[4], 1), BS // 2, BS).astype(jnp.int32)
    tile_rows = plant(jax.random.randint(key_of[5], (NTILE,), 0, BLK_DEV), jax.random.fold_in(key_of[5], 1), 0, BLK_DEV - 1).astype(jnp.int32)
    col_owner_keys = jax.random.split(jax.random.fold_in(key_of[6], 1), NTILE // TILES_ROW)
    col_owner_turns = jax.random.permutation(jax.random.fold_in(key_of[6], 3), NTILE // TILES_ROW)
    col_owner = jax.vmap(lambda own, number: assign_block(jax.random.fold_in(key_of[6], 2), own, number, TILES_ROW, N_BLK, 1, CAP, 2))(col_owner_keys, col_owner_turns).reshape((NTILE, 1))
    col_block = plant(jax.random.randint(key_of[7], (NTILE,), 0, BLK_DEV), jax.random.fold_in(key_of[7], 1), 0, BLK_DEV - 1).astype(jnp.int32)
    return dict(adjoint=adjoint, three_centre=three_centre, occ_density=occ_density, vir_density=vir_density, block_sizes=block_sizes, tile_rows=tile_rows, col_owner=col_owner, col_block=col_block)


def reference(adjoint, three_centre, occ_density, vir_density, block_sizes, tile_rows, col_owner, col_block):
    func_index = jnp.arange(BS, dtype=jnp.int32)
    live_funcs = (func_index[None, :] < block_sizes[:, None]).astype(jnp.float32)
    live_pairs = (live_funcs[:, :, None] * live_funcs[:, None, :]).reshape(NB, BS * BS)
    occ_masked = (occ_density.astype(jnp.float32) * live_pairs).astype(jnp.bfloat16)
    vir_masked = (vir_density.astype(jnp.float32) * live_pairs).astype(jnp.bfloat16)
    tile_ids = jnp.arange(NTILE, dtype=jnp.int32)
    row_ids = ((tile_ids // TILES_ROW) * BLK_DEV + tile_rows).astype(jnp.int32)
    col_ids = (col_owner[:, 0] * BLK_DEV + col_block).astype(jnp.int32)
    adjoint_t = adjoint.T

    def one_group(totals, group_id):
        occ_acc, vir_acc = totals
        first = (group_id * TILE_DEV).astype(jnp.int32)
        tile_group = lax.dynamic_slice_in_dim(three_centre, first, TILE_DEV, 0)
        group_rows = lax.dynamic_slice_in_dim(row_ids, first, TILE_DEV, 0)
        group_cols = lax.dynamic_slice_in_dim(col_ids, first, TILE_DEV, 0)
        tile_flat = tile_group.reshape(TILE_DEV * BS * BS, NAUX)
        contracted = jnp.dot(tile_flat, adjoint_t, preferred_element_type=jnp.float32).astype(jnp.bfloat16)
        contracted = contracted.reshape(TILE_DEV, BS, BS, NAUX).astype(jnp.float32)
        vir_tile_d = vir_masked[group_cols].reshape(TILE_DEV, BS, BS).astype(jnp.float32)
        occ_tile_d = occ_masked[group_rows].reshape(TILE_DEV, BS, BS).astype(jnp.float32)
        tiles_f = tile_group.astype(jnp.float32)
        weighted = jnp.einsum('tjk,tijq->tikq', vir_tile_d, contracted).astype(jnp.bfloat16).astype(jnp.float32)
        occ_tile = jnp.einsum('tikq,tlkq->til', weighted, tiles_f)
        rotated = jnp.einsum('tij,tjkq->tikq', occ_tile_d, tiles_f).astype(jnp.bfloat16).astype(jnp.float32)
        vir_tile = jnp.einsum('tijq,tikq->tjk', contracted, rotated)
        occ_acc = occ_acc.at[group_rows].add(occ_tile.reshape(TILE_DEV, BS * BS))
        vir_acc = vir_acc.at[group_cols].add(vir_tile.reshape(TILE_DEV, BS * BS))
        return (occ_acc, vir_acc), None

    zeros = jnp.zeros((NB, BS * BS), jnp.float32)
    (occ_acc, vir_acc), _ = lax.scan(one_group, (zeros, zeros), jnp.arange(NTILE // TILE_DEV, dtype=jnp.int32))
    norm_factor = NAUX ** -0.5
    return occ_acc * live_pairs * norm_factor, vir_acc * live_pairs * norm_factor
```

```python
import functools

import jax
import jax.numpy as jnp
from jax import lax
from jax.experimental import pallas as pl
from jax.experimental.pallas import tpu as pltpu
from jax.sharding import PartitionSpec as P

BS = 32
SUB = 8
CHUNK = 256
MESH = pl.DeviceIdType.MESH
F32 = jnp.float32
BF16 = jnp.bfloat16


def iota(shape, dim):
    return lax.broadcasted_iota(jnp.int32, shape, dim)


def dot(left, right):
    return jnp.dot(left, right, preferred_element_type=F32)


def dot_nt(left, right):
    return lax.dot_general(left, right, (((1,), (1,)), ((), ())), preferred_element_type=F32)


def fold(rows, lanes, row_key, lane_key):
    return (row_key(iota((rows, lanes), 0)) == lane_key(iota((rows, lanes), 1))).astype(BF16)


def exact(mat, folding):
    high = mat.astype(BF16)
    low = (mat - high.astype(F32)).astype(BF16)
    return dot(high, folding) + dot(low, folding)


def minor(index):
    return index % BS


def inner(index):
    return index // (SUB * SUB) * SUB + index % SUB


def outer(index):
    return index // SUB


def fused_kernel(
    n_blk, n_aux, norm,
    sizes, rows, owners, blocks, adj_hbm, occ_ref, vir_ref, t_hbm,
    out_ref,
    got, tbuf, cbuf, rbuf, ybuf, vir_send, vir_got, occ_send, occ_got,
    adj_sem, t_sem, near_sem, recv_sem, send_sem, trade_sem,
):
    n_dev = n_blk * n_aux
    depth = n_blk // 2
    count, groups, _, _, naux = tbuf.shape
    pairs = BS * BS
    wide = BS * SUB
    own = out_ref.shape[1]
    arows = adj_hbm.shape[0]
    half = arows // 2
    span = naux // depth
    per_plane = n_dev // depth
    b = lax.axis_index("blk")
    a = lax.axis_index("aux")
    z, y, x, c = b // 2, b % 2, a // 2, a % 2
    col, sides, corner, mates = range(4)
    over_x = (b, (1 - x) * 2 + c)
    over_y = (z * 2 + 1 - y, a)
    mate = (b, x * 2 + 1 - c)
    above, below = (b + 2, a), (b - 2, a)
    has_up, has_down = z < depth - 1, z > 0
    me = b * n_aux + a

    def ident(xx, yy, zz, cc):
        return ((zz * 2 + yy) * 2 + xx) * 2 + cc

    barrier = pltpu.get_barrier_semaphore()

    def tell(sem, device):
        pl.semaphore_signal(sem, inc=1, device_id=device, device_id_type=MESH)

    for device in (over_x, over_y, mate):
        tell(barrier, device)
    pl.when(has_up)(lambda: tell(barrier, above))
    pl.when(has_down)(lambda: tell(barrier, below))

    adj_copy = pltpu.make_async_copy(adj_hbm, got.at[me, pl.ds(0, arows)], adj_sem)
    adj_copy.start()
    for t in range(count):
        for g in range(groups):
            pltpu.make_async_copy(t_hbm.at[t, :, g], tbuf.at[t, g], t_sem.at[t]).start()

    lane = iota((1, pairs), 1)
    diag = iota((BS, pairs), 1) // BS == iota((BS, pairs), 0)

    def live(size):
        return (lane // BS < size) & (lane % BS < size)

    def pick(all_rows, at):
        return jnp.sum(jnp.where(iota(all_rows.shape, 0) == at, all_rows, 0.0), axis=0, keepdims=True)

    vir_all = vir_ref[...].astype(F32)
    mine = [jnp.where(live(sizes[a * own + r]), pick(vir_all, a * own + r), 0.0) for r in range(own)]
    got[me, arows:, :] = jnp.concatenate(mine, axis=0).astype(BF16)

    adj_copy.wait()
    pl.semaphore_wait(barrier, 3 + has_up.astype(jnp.int32) + has_down.astype(jnp.int32))

    def send(block, device, kind, zz, part=None):
        ref = got.at[block] if part is None else got.at[block, part]
        pltpu.make_async_remote_copy(
            src_ref=ref,
            dst_ref=ref,
            send_sem=send_sem,
            recv_sem=recv_sem.at[kind, zz],
            device_id=device,
            device_id_type=MESH,
        ).start()

    def arrive(kind, zz, number):
        part = got.at[pl.ds(0, number)]
        pltpu.make_async_copy(part, part, recv_sem.at[kind, zz]).wait()

    for device in (over_x, over_y):
        send(me, device, sides, z)
    pl.when(has_up)(lambda: send(me, above, col, z))
    pl.when(has_down)(lambda: send(me, below, col, z))
    send(me, mate, mates, z)

    def reach(hop):
        pl.when(has_down & (z + hop < depth))(lambda: tell(near_sem.at[0], below))
        pl.when(has_up & (z - hop >= 0))(lambda: tell(near_sem.at[1], above))

        @pl.when(z + hop + 1 < depth)
        def _():
            pl.semaphore_wait(near_sem.at[0], 1)
            send(me, (b + 2 * (hop + 1), a), col, z)

        @pl.when(z - hop - 1 >= 0)
        def _():
            pl.semaphore_wait(near_sem.at[1], 1)
            send(me, (b - 2 * (hop + 1), a), col, z)

    def relay_col(zz):
        block = ident(x, y, zz, c)
        arrive(col, zz, 1)
        send(block, over_x, sides, zz)
        send(block, over_y, sides, zz)
        send(block, mate, mates, zz)

    def relay_sides(zz):
        arrive(sides, zz, 2)
        block_x, block_y = ident(1 - x, y, zz, c), ident(x, 1 - y, zz, c)
        send(block_x, over_y, corner, zz, pl.ds(0, half))
        send(block_y, over_x, corner, zz, pl.ds(half, arows + own - half))
        send(block_x, mate, mates, zz)
        send(block_y, mate, mates, zz)

    def relay_corner(zz):
        arrive(corner, zz, 1)
        send(ident(1 - x, 1 - y, zz, c), mate, mates, zz)

    low = z < depth // 2
    zl = jnp.where(low, z, depth - 1 - z)

    def plane(k):
        near = zl + k // 2 if k % 2 == 0 else zl - (k + 1) // 2
        at = jnp.where(k <= 2 * zl, near, k)
        return jnp.where(low, at, depth - 1 - at)

    order = [plane(k) for k in range(depth)]

    occ_all = occ_ref[...].astype(F32)
    parts = []
    for t in range(count):
        row = jnp.where(live(sizes[rows[t]]), pick(occ_all, rows[t]), 0.0)
        parts.append(jnp.where(diag, row, 0.0))
    square = dot(jnp.concatenate(parts, axis=0).astype(BF16), fold(pairs, wide, minor, outer))
    same_sub = iota((wide, wide), 0) % SUB == iota((wide, wide), 1) % SUB

    def rotate(t):
        spread = jnp.broadcast_to(square[t * BS : (t + 1) * BS][:, None, :], (BS, SUB, wide)).reshape(wide, wide)
        left = jnp.where(same_sub, spread, 0.0).astype(BF16)
        pltpu.make_async_copy(tbuf.at[t], tbuf.at[t], t_sem.at[t]).wait()
        for g in range(groups):
            rbuf[t, g] = dot(left, tbuf[t, g].reshape(wide, naux)).astype(BF16).reshape(BS, SUB, naux)

    def contract(k, t):
        zz = order[k]
        part = got[pl.ds(zz * per_plane, per_plane), :arows, :].reshape(span, naux)
        columns = pl.ds(pl.multiple_of(zz * span, span), span)
        new = dot_nt(tbuf[t].reshape(pairs, naux), part).astype(BF16)
        cbuf[t, :, :, :, columns] = new.reshape(groups, BS, SUB, span)

    events = {
        (0, 1): [lambda: relay_sides(order[1])],
        (0, 3): [lambda: relay_col(order[3])],
        (1, 0): [lambda: relay_sides(order[2]), lambda: relay_corner(order[1]), lambda: arrive(mates, order[1], 4)],
        (1, 1): [lambda: relay_corner(order[2])],
        (1, 3): [lambda: relay_sides(order[3])],
        (2, 0): [lambda: arrive(mates, order[2], 4)],
        (2, 2): [lambda: relay_corner(order[3])],
        (3, 0): [lambda: arrive(mates, order[3], 4)],
    }

    rotate(0)
    reach(1)
    rotate(1)
    reach(2)
    rotate(2)
    rotate(3)
    relay_sides(order[0])
    relay_col(order[1])
    relay_corner(order[0])
    relay_col(order[2])
    arrive(mates, order[0], 4)
    for k in range(depth):
        for t in range(count):
            for event in events.get((k, t), []):
                event()
            contract(k, t)

    same_row = iota((SUB, SUB, wide), 0) == iota((SUB, SUB, wide), 2) % (SUB * SUB) // SUB
    lanes_of = iota((SUB, 128), 1) // BS

    def compact(square):
        total = jnp.zeros((SUB, 128), F32)
        for g in range(groups):
            total = jnp.where(lanes_of == g, square[g * SUB : (g + 1) * SUB], total)
        return total

    parts = []
    for t in range(count):
        acc = jnp.zeros((wide, wide), F32)
        for at in range(0, BS, SUB):
            left = cbuf[t, :, at : at + SUB].reshape(wide, naux)
            acc = acc + dot_nt(left, rbuf[t, :, at : at + SUB].reshape(wide, naux))
        acc = jnp.where(same_row, acc.reshape(groups, SUB, SUB, wide), 0.0)
        parts.append(jnp.sum(acc, axis=1).reshape(BS, wide))
    both = exact(jnp.concatenate(parts, axis=0), fold(wide, 128, inner, minor))
    terms = [compact(both[t * BS : (t + 1) * BS]) for t in range(count)]
    for p in range(n_dev):
        slots = []
        for r in range(own):
            total = jnp.zeros((SUB, 128), F32)
            for t in range(count):
                here = owners[t] * (n_aux * own) + blocks[t] == p * own + r
                total = total + jnp.where(here, terms[t], 0.0)
            slots.append(total)
        vir_send[p] = jnp.concatenate(slots, axis=0).astype(BF16)
    vir_got[me] = vir_send[me]

    def send_vir(k, carry):
        p = lax.rem(me + k, n_dev)
        pltpu.make_async_remote_copy(
            src_ref=vir_send.at[p],
            dst_ref=vir_got.at[me],
            send_sem=trade_sem.at[0],
            recv_sem=trade_sem.at[1],
            device_id=(p // n_aux, p % n_aux),
            device_id_type=MESH,
        ).start()
        return carry

    lax.fori_loop(1, n_dev, send_vir, 0)

    parts = []
    for t in range(count):
        home = owners[t] * n_aux + blocks[t] // own
        row = pick(got[home, arows:, :].astype(F32), blocks[t] % own)
        parts.append(jnp.where(diag, row, 0.0))
    square_v = dot(jnp.concatenate(parts, axis=0).astype(BF16), fold(pairs, wide, minor, inner))
    for t in range(count):
        spread = square_v[t * BS : (t + 1) * BS].reshape(groups, 1, SUB, wide)
        spread = jnp.broadcast_to(spread, (groups, SUB, SUB, wide))
        left = jnp.where(same_row, spread, 0.0).reshape(wide, wide).astype(BF16)
        for at in range(0, BS, SUB):
            new = dot(left, tbuf[t, :, at : at + SUB].reshape(wide, naux)).astype(BF16)
            ybuf[t, :, at : at + SUB] = new.reshape(groups, SUB, SUB, naux)

    gather = fold(BS, wide, lambda index: index, outer)
    parts = []
    for t in range(count):
        acc = jnp.zeros((wide, wide), F32)
        for g in range(groups):
            acc = acc + dot_nt(cbuf[t, g].reshape(wide, naux), ybuf[t, g].reshape(wide, naux))
        acc = jnp.where(same_sub, acc, 0.0)
        high = acc.astype(BF16)
        parts.append(dot(gather, high) + dot(gather, (acc - high.astype(F32)).astype(BF16)))
    both = exact(jnp.concatenate(parts, axis=0), fold(wide, 128, outer, minor))
    terms = [compact(both[t * BS : (t + 1) * BS]) for t in range(count)]
    for q in range(n_aux):
        slots = []
        for r in range(own):
            total = jnp.zeros((SUB, 128), F32)
            for t in range(count):
                total = total + jnp.where(rows[t] == q * own + r, terms[t], 0.0)
            slots.append(total)
        occ_send[q] = jnp.concatenate(slots, axis=0)
    occ_got[a] = occ_send[a]
    for k in range(1, n_aux):
        q = lax.rem(a + k, n_aux)
        pltpu.make_async_remote_copy(
            src_ref=occ_send.at[q],
            dst_ref=occ_got.at[a],
            send_sem=trade_sem.at[2],
            recv_sem=trade_sem.at[3],
            device_id=(b, q),
            device_id_type=MESH,
        ).start()

    def done(ref, sem):
        pltpu.make_async_copy(ref, ref, sem).wait()

    done(vir_got.at[pl.ds(0, n_dev - 1)], trade_sem.at[1])
    vir_sum = jnp.sum(vir_got[...].astype(F32), axis=0)
    done(occ_got.at[pl.ds(0, n_aux - 1)], trade_sem.at[3])
    occ_sum = jnp.sum(occ_got[...], axis=0)

    sums = jnp.concatenate([occ_sum, vir_sum], axis=0)
    lanes_all = iota(sums.shape, 1) // BS
    parts = [jnp.where(lanes_all == g, sums, 0.0) for g in range(groups)]
    both = exact(jnp.concatenate(parts, axis=0), fold(128, 128, minor, minor))
    both = both.reshape(groups, 2 * own, SUB, 128)
    per_tile = 128 // BS
    lines = []
    for m in range(pairs // 128):
        first = m * per_tile
        here = iota((SUB, 128), 0) == first % SUB + lanes_of
        lines.append(jnp.sum(jnp.where(here, both[first // SUB], 0.0), axis=1))
    flat = jnp.concatenate(lines, axis=1)
    for r in range(own):
        scale = jnp.where(live(sizes[a * own + r]), norm, 0.0).astype(F32)
        out_ref[0, r : r + 1, :] = flat[r : r + 1, :] * scale
        out_ref[1, r : r + 1, :] = flat[own + r : own + r + 1, :] * scale

    done(vir_send.at[pl.ds(0, n_dev - 1)], trade_sem.at[0])
    done(occ_send.at[pl.ds(0, n_aux - 1)], trade_sem.at[2])
    done(got.at[pl.ds(0, depth - 1 + 7 * depth)], send_sem)


def fused(sizes, rows, owners, blocks, adj, occ, vir, three, n_blk, n_aux, norm):
    n_dev = n_blk * n_aux
    count, naux = three.shape[0], three.shape[3]
    own = occ.shape[0] // n_aux
    groups = BS // SUB
    smem = pl.BlockSpec(memory_space=pltpu.SMEM)
    vmem = pl.BlockSpec(memory_space=pltpu.VMEM)
    hbm = pl.BlockSpec(memory_space=pl.ANY)
    tile = pltpu.VMEM((count, groups, BS, SUB, naux), BF16)
    return pl.pallas_call(
        functools.partial(fused_kernel, n_blk, n_aux, norm),
        out_shape=jax.ShapeDtypeStruct((2, own, BS * BS), F32),
        in_specs=[smem] * 4 + [hbm, vmem, vmem, hbm],
        out_specs=vmem,
        scratch_shapes=[
            pltpu.VMEM((n_dev, adj.shape[0] + own, naux), BF16),
            tile,
            tile,
            tile,
            tile,
            pltpu.VMEM((n_dev, own * SUB, 128), BF16),
            pltpu.VMEM((n_dev, own * SUB, 128), BF16),
            pltpu.VMEM((n_aux, own * SUB, 128), F32),
            pltpu.VMEM((n_aux, own * SUB, 128), F32),
            pltpu.SemaphoreType.DMA,
            pltpu.SemaphoreType.DMA((count,)),
            pltpu.SemaphoreType.REGULAR((2,)),
            pltpu.SemaphoreType.DMA((4, n_blk // 2)),
            pltpu.SemaphoreType.DMA,
            pltpu.SemaphoreType.DMA((4,)),
        ],
        compiler_params=pltpu.CompilerParams(
            collective_id=0, has_side_effects=True, vmem_limit_bytes=67043328
        ),
        name="fused",
    )(sizes, rows, owners, blocks, adj, occ, vir, three.reshape(count, BS, groups, SUB, naux))


def tile_kernel(
    n_aux, own, sizes, rows, owners, blocks, occ_ref, vir_ref, adj_ref, t_ref, occ_out, vir_out, vir_acc
):
    t = pl.program_id(0)
    pairs = BS * BS
    naux = adj_ref.shape[0]

    @pl.when(t == 0)
    def _():
        occ_out[...] = jnp.zeros_like(occ_out)
        vir_acc[...] = jnp.zeros_like(vir_acc)

    row, owner, block = rows[t], owners[t], blocks[t]
    size = sizes[row]
    lane = iota((1, pairs), 1)
    inside = (lane // BS < size) & (lane % BS < size)
    occ_all = occ_ref[...].astype(F32)
    occ_row = jnp.sum(jnp.where(iota(occ_all.shape, 0) == row, occ_all, 0.0), axis=0, keepdims=True)
    occ_row = jnp.where(inside, occ_row, 0.0)
    home = owner * n_aux + block // own
    vir_all = vir_ref[home].astype(F32)
    vir_row = jnp.sum(jnp.where(iota(vir_all.shape, 0) == block % own, vir_all, 0.0), axis=0, keepdims=True)
    diag = iota((BS, pairs), 1) // BS == iota((BS, pairs), 0)
    fold_minor = (iota((pairs, 128), 0) % BS == iota((pairs, 128), 1) % BS).astype(BF16)
    fold_major = (iota((pairs, 128), 0) // BS == iota((pairs, 128), 1) % BS).astype(BF16)
    spread = (iota((128, pairs), 0) == iota((128, pairs), 1) // BS).astype(BF16)
    repeat = pairs // 128

    def square(flat):
        return jnp.dot(jnp.where(diag, flat, 0.0).astype(BF16), fold_minor, preferred_element_type=F32)

    occ_rep = jnp.dot(square(occ_row).astype(BF16), spread, preferred_element_type=F32)
    vir_rep = jnp.concatenate([square(vir_row)] * repeat, axis=1)

    nt = (((1,), (1,)), ((), ()))
    acc = jnp.zeros((BS, pairs), F32)
    lines = []
    for first in range(0, pairs, CHUNK):
        part = lax.dot_general(t_ref[0, first : first + CHUNK, :], adj_ref[...], nt, preferred_element_type=F32)
        gram = lax.dot_general(part.astype(BF16), t_ref[0], nt, preferred_element_type=F32)
        for at in range(CHUNK // BS):
            i = first // BS + at
            block_i = gram[at * BS : (at + 1) * BS, :]
            acc = acc + block_i * occ_rep[i : i + 1, :]
            lines.append(jnp.sum(block_i * vir_rep, axis=0, keepdims=True))
    zmat = jnp.concatenate(lines, axis=0)

    def flatten(mat, fold):
        high = mat.astype(BF16)
        low = (mat - high.astype(F32)).astype(BF16)
        both = jnp.dot(high, fold, preferred_element_type=F32) + jnp.dot(low, fold, preferred_element_type=F32)
        wide = jnp.concatenate([both] * repeat, axis=1)
        return jnp.sum(jnp.where(diag, wide, 0.0), axis=0, keepdims=True)

    occ_flat = flatten(zmat, fold_major)
    vir_flat = flatten(acc, fold_minor)
    slot = iota((own, pairs), 0)
    occ_out[row // own] = occ_out[row // own] + jnp.where(slot == row % own, occ_flat, 0.0)
    vir_acc[home] = vir_acc[home] + jnp.where(slot == block % own, vir_flat, 0.0)

    @pl.when(t == pl.num_programs(0) - 1)
    def _():
        vir_out[...] = vir_acc[...].astype(vir_out.dtype)


def tiles(sizes, rows, owners, blocks, occ, vir, adj, three, n_dev, n_aux):
    count, pairs, naux = three.shape
    own = occ.shape[0] // n_aux
    smem = pl.BlockSpec(memory_space=pltpu.SMEM)
    vmem = pl.BlockSpec(memory_space=pltpu.VMEM)
    return pl.pallas_call(
        functools.partial(tile_kernel, n_aux, own),
        grid=(count,),
        out_shape=(
            jax.ShapeDtypeStruct((n_aux, own, pairs), F32),
            jax.ShapeDtypeStruct((n_dev, own, pairs), BF16),
        ),
        in_specs=[smem] * 4 + [vmem] * 3 + [pl.BlockSpec((1, pairs, naux), lambda t: (t, 0, 0))],
        out_specs=(vmem, vmem),
        scratch_shapes=[pltpu.VMEM((n_dev, own, pairs), F32)],
        compiler_params=pltpu.CompilerParams(vmem_limit_bytes=48 * 1024 * 1024),
        name="tiles",
    )(sizes, rows, owners, blocks, occ, vir, adj, three)


def exchange_kernel(
    n_blk, n_aux, norm, sizes, occ_ref, vir_ref, occ_out, vir_out, occ_got, vir_got, occ_sems, vir_sems
):
    n_dev = n_blk * n_aux
    b = lax.axis_index("blk")
    a = lax.axis_index("aux")
    me = b * n_aux + a
    barrier = pltpu.get_barrier_semaphore()

    def greet(k, carry):
        p = lax.rem(me + k, n_dev)
        pl.semaphore_signal(barrier, inc=1, device_id=(p // n_aux, p % n_aux), device_id_type=MESH)
        return carry

    lax.fori_loop(1, n_dev, greet, 0)
    pl.semaphore_wait(barrier, n_dev - 1)

    trade(n_blk, n_aux, norm, sizes, occ_ref, vir_ref, occ_out, vir_out, occ_got, vir_got, occ_sems, vir_sems)


def trade(n_blk, n_aux, norm, sizes, occ_ref, vir_ref, occ_out, vir_out, occ_got, vir_got, occ_sems, vir_sems):
    n_dev = n_blk * n_aux
    b = lax.axis_index("blk")
    a = lax.axis_index("aux")
    me = b * n_aux + a
    own, pairs = occ_out.shape

    def vir_copy(k, source):
        p = lax.rem(me + k, n_dev)
        return pltpu.make_async_remote_copy(
            src_ref=vir_ref.at[p],
            dst_ref=vir_got.at[source],
            send_sem=vir_sems.at[0, k],
            recv_sem=vir_sems.at[1, source],
            device_id=(p // n_aux, p % n_aux),
            device_id_type=MESH,
        )

    def occ_copy(k, source):
        q = lax.rem(a + k, n_aux)
        return pltpu.make_async_remote_copy(
            src_ref=occ_ref.at[q],
            dst_ref=occ_got.at[source],
            send_sem=occ_sems.at[0, k],
            recv_sem=occ_sems.at[1, source],
            device_id=(b, q),
            device_id_type=MESH,
        )

    def start_vir(k, carry):
        vir_copy(k, me).start()
        return carry

    def start_occ(k, carry):
        occ_copy(k, a).start()
        return carry

    lax.fori_loop(1, n_dev, start_vir, 0)
    lax.fori_loop(1, n_aux, start_occ, 0)

    def take_vir(k, total):
        source = lax.rem(me + k, n_dev)
        vir_copy(k, source).wait_recv()
        return total + vir_got[source].astype(F32)

    def take_occ(k, total):
        source = lax.rem(a + k, n_aux)
        occ_copy(k, source).wait_recv()
        return total + occ_got[source]

    occ_sum = lax.fori_loop(1, n_aux, take_occ, occ_ref[a])
    vir_sum = lax.fori_loop(1, n_dev, take_vir, vir_ref[me].astype(F32))
    lane = iota((1, pairs), 1)
    for r in range(own):
        size = sizes[a * own + r]
        scale = jnp.where((lane // BS < size) & (lane % BS < size), norm, 0.0).astype(F32)
        occ_out[r : r + 1, :] = occ_sum[r : r + 1, :] * scale
        vir_out[r : r + 1, :] = vir_sum[r : r + 1, :] * scale

    def end_vir(k, carry):
        vir_copy(k, me).wait_send()
        return carry

    def end_occ(k, carry):
        occ_copy(k, a).wait_send()
        return carry

    lax.fori_loop(1, n_dev, end_vir, 0)
    lax.fori_loop(1, n_aux, end_occ, 0)


def exchange(sizes, occ, vir, n_blk, n_aux, norm):
    n_dev, own, pairs = vir.shape
    vmem = pl.BlockSpec(memory_space=pltpu.VMEM)
    out = jax.ShapeDtypeStruct((own, pairs), F32)
    return pl.pallas_call(
        functools.partial(exchange_kernel, n_blk, n_aux, norm),
        out_shape=(out, out),
        in_specs=[pl.BlockSpec(memory_space=pltpu.SMEM), vmem, vmem],
        out_specs=(vmem, vmem),
        scratch_shapes=[
            pltpu.VMEM(occ.shape, occ.dtype),
            pltpu.VMEM(vir.shape, vir.dtype),
            pltpu.SemaphoreType.DMA((2, n_aux)),
            pltpu.SemaphoreType.DMA((2, n_dev)),
        ],
        compiler_params=pltpu.CompilerParams(collective_id=1, has_side_effects=True),
        name="exchange",
    )(sizes, occ, vir)


def shards(
    n_blk, n_aux, adjoint, three_centre, occ_density, vir_density, block_sizes, tile_rows, col_owner, col_block
):
    n_dev = n_blk * n_aux
    count = three_centre.shape[0]
    naux = three_centre.shape[3]
    own = occ_density.shape[0] // n_aux
    depth = adjoint.shape[0]
    three = three_centre.reshape(count, BS * BS, naux)
    if n_aux == 4 and n_blk == 8:
        both = fused(
            block_sizes, tile_rows, col_owner.reshape(count), col_block, adjoint, occ_density, vir_density,
            three_centre, n_blk, n_aux, naux ** -0.5,
        )
        return both[0], both[1]
    aux_here = lax.axis_index("aux")
    own_sizes = lax.dynamic_slice_in_dim(block_sizes, aux_here * own, own, 0)
    own_vir = lax.dynamic_slice_in_dim(vir_density, aux_here * own, own, 0)
    lane = jnp.arange(BS * BS, dtype=jnp.int32)[None, :]
    inside = (lane // BS < own_sizes[:, None]) & (lane % BS < own_sizes[:, None])
    own_vir = jnp.where(inside, own_vir, jnp.zeros_like(own_vir))
    got = lax.all_gather(jnp.concatenate((adjoint, own_vir), axis=0), ("blk", "aux"), axis=0)
    adj = got[:, :depth, :].reshape(naux, naux)
    vir = got[:, depth:, :]
    occ_terms, vir_terms = tiles(
        block_sizes, tile_rows, col_owner.reshape(count), col_block, occ_density, vir, adj,
        three, n_dev, n_aux,
    )
    return exchange(block_sizes, occ_terms, vir_terms, n_blk, n_aux, naux ** -0.5)


def solution(mesh):
    in_specs = (
        P(("blk", "aux"), None),
        P(("blk", "aux"), None, None, None),
        P("blk", None),
        P("blk", None),
        P("blk"),
        P(("blk", "aux")),
        P(("blk", "aux"), None),
        P(("blk", "aux")),
    )
    out_specs = (P(("blk", "aux"), None), P(("blk", "aux"), None))
    body = functools.partial(shards, mesh.shape["blk"], mesh.shape["aux"])
    return jax.shard_map(body, mesh=mesh, in_specs=in_specs, out_specs=out_specs, check_vma=False)
```

```python
import functools

import jax
import jax.numpy as jnp
from jax import lax
from jax.experimental import pallas as pl
from jax.experimental.pallas import tpu as pltpu
from jax.sharding import PartitionSpec as P

BS = 32
SUB = 8
CHUNK = 256
MESH = pl.DeviceIdType.MESH
F32 = jnp.float32
BF16 = jnp.bfloat16


def iota(shape, dim):
    return lax.broadcasted_iota(jnp.int32, shape, dim)


def dot(left, right):
    return jnp.dot(left, right, preferred_element_type=F32)


def dot_nt(left, right):
    return lax.dot_general(left, right, (((1,), (1,)), ((), ())), preferred_element_type=F32)


def fold(rows, lanes, row_key, lane_key):
    return (row_key(iota((rows, lanes), 0)) == lane_key(iota((rows, lanes), 1))).astype(BF16)


def exact(mat, folding):
    high = mat.astype(BF16)
    low = (mat - high.astype(F32)).astype(BF16)
    return dot(high, folding) + dot(low, folding)


def minor(index):
    return index % BS


def inner(index):
    return index // (SUB * SUB) * SUB + index % SUB


def outer(index):
    return index // SUB


def fused_kernel(
    n_blk, n_aux, norm,
    sizes_hbm, rows_hbm, owners_hbm, blocks_hbm, adj_hbm, occ_hbm, vir_hbm, t_hbm,
    out_ref,
    sizes, rows, owners, blocks, occ_ref, vir_ref, got, tbuf, cbuf, rbuf, ybuf, vir_send, vir_got, occ_send, occ_got,
    in_sem, t_sem, near_sem, recv_sem, send_sem, trade_sem,
):
    n_dev = n_blk * n_aux
    depth = n_blk // 2
    count, groups, _, _, naux = tbuf.shape
    pairs = BS * BS
    wide = BS * SUB
    own = out_ref.shape[1]
    arows = adj_hbm.shape[0]
    half = arows // 2
    span = naux // depth
    per_plane = n_dev // depth
    b = lax.axis_index("blk")
    a = lax.axis_index("aux")
    z, y, x, c = b // 2, b % 2, a // 2, a % 2
    col, sides, corner, mates = range(4)
    over_x = (b, (1 - x) * 2 + c)
    over_y = (z * 2 + 1 - y, a)
    mate = (b, x * 2 + 1 - c)
    above, below = (b + 2, a), (b - 2, a)
    has_up, has_down = z < depth - 1, z > 0
    me = b * n_aux + a

    def ident(xx, yy, zz, cc):
        return ((zz * 2 + yy) * 2 + xx) * 2 + cc

    barrier = pltpu.get_barrier_semaphore()

    def tell(sem, device):
        pl.semaphore_signal(sem, inc=1, device_id=device, device_id_type=MESH)

    for device in (over_x, over_y, mate):
        tell(barrier, device)
    pl.when(has_up)(lambda: tell(barrier, above))
    pl.when(has_down)(lambda: tell(barrier, below))

    pairs_in = (
        (vir_hbm, vir_ref), (sizes_hbm, sizes), (adj_hbm, got.at[me, pl.ds(0, arows)]),
        (rows_hbm, rows), (occ_hbm, occ_ref), (owners_hbm, owners), (blocks_hbm, blocks),
    )
    fetches = [pltpu.make_async_copy(src, dst, in_sem.at[i]) for i, (src, dst) in enumerate(pairs_in)]
    for fetch in fetches:
        fetch.start()

    lane = iota((1, pairs), 1)
    diag = iota((BS, pairs), 1) // BS == iota((BS, pairs), 0)

    def live(size):
        return (lane // BS < size) & (lane % BS < size)

    def pick(all_rows, at):
        return jnp.sum(jnp.where(iota(all_rows.shape, 0) == at, all_rows, 0.0), axis=0, keepdims=True)

    for fetch in fetches:
        fetch.wait()
    for t in range(count):
        for g in range(groups):
            pltpu.make_async_copy(t_hbm.at[t, :, g], tbuf.at[t, g], t_sem.at[t]).start()
    vir_all = vir_ref[...].astype(F32)
    mine = [jnp.where(live(sizes[a * own + r]), pick(vir_all, a * own + r), 0.0) for r in range(own)]
    got[me, arows:, :] = jnp.concatenate(mine, axis=0).astype(BF16)

    pl.semaphore_wait(barrier, 3 + has_up.astype(jnp.int32) + has_down.astype(jnp.int32))

    def send(block, device, kind, zz, part=None):
        ref = got.at[block] if part is None else got.at[block, part]
        pltpu.make_async_remote_copy(
            src_ref=ref,
            dst_ref=ref,
            send_sem=send_sem,
            recv_sem=recv_sem.at[kind, zz],
            device_id=device,
            device_id_type=MESH,
        ).start()

    def arrive(kind, zz, number):
        part = got.at[pl.ds(0, number)]
        pltpu.make_async_copy(part, part, recv_sem.at[kind, zz]).wait()

    for device in (over_x, over_y):
        send(me, device, sides, z)
    pl.when(has_up)(lambda: send(me, above, col, z))
    pl.when(has_down)(lambda: send(me, below, col, z))
    send(me, mate, mates, z)

    def report(hop):
        pl.when(has_down & (z + hop < depth))(lambda: tell(near_sem.at[0], below))
        pl.when(has_up & (z - hop >= 0))(lambda: tell(near_sem.at[1], above))

    def reach(hop):
        @pl.when(z + hop + 1 < depth)
        def _():
            pl.semaphore_wait(near_sem.at[0], 1)
            send(me, (b + 2 * (hop + 1), a), col, z)

        @pl.when(z - hop - 1 >= 0)
        def _():
            pl.semaphore_wait(near_sem.at[1], 1)
            send(me, (b - 2 * (hop + 1), a), col, z)

    def relay_col(zz):
        block = ident(x, y, zz, c)
        arrive(col, zz, 1)
        send(block, over_x, sides, zz)
        send(block, over_y, sides, zz)
        send(block, mate, mates, zz)

    def relay_sides(zz):
        arrive(sides, zz, 2)
        block_x, block_y = ident(1 - x, y, zz, c), ident(x, 1 - y, zz, c)
        send(block_x, over_y, corner, zz, pl.ds(0, half))
        send(block_y, over_x, corner, zz, pl.ds(half, arows + own - half))
        send(block_x, mate, mates, zz)
        send(block_y, mate, mates, zz)

    def relay_corner(zz):
        arrive(corner, zz, 1)
        send(ident(1 - x, 1 - y, zz, c), mate, mates, zz)

    low = z < depth // 2
    zl = jnp.where(low, z, depth - 1 - z)

    def plane(k):
        near = zl + k // 2 if k % 2 == 0 else zl - (k + 1) // 2
        at = jnp.where(k <= 2 * zl, near, k)
        return jnp.where(low, at, depth - 1 - at)

    order = [plane(k) for k in range(depth)]

    report(1)
    occ_all = occ_ref[...].astype(F32)
    parts = []
    for t in range(count):
        row = jnp.where(live(sizes[rows[t]]), pick(occ_all, rows[t]), 0.0)
        parts.append(jnp.where(diag, row, 0.0))
    square = dot(jnp.concatenate(parts, axis=0).astype(BF16), fold(pairs, wide, minor, outer))
    same_sub = iota((wide, wide), 0) % SUB == iota((wide, wide), 1) % SUB

    def rotate(t):
        spread = jnp.broadcast_to(square[t * BS : (t + 1) * BS][:, None, :], (BS, SUB, wide)).reshape(wide, wide)
        left = jnp.where(same_sub, spread, 0.0).astype(BF16)
        pltpu.make_async_copy(tbuf.at[t], tbuf.at[t], t_sem.at[t]).wait()
        for g in range(groups):
            rbuf[t, g] = dot(left, tbuf[t, g].reshape(wide, naux)).astype(BF16).reshape(BS, SUB, naux)

    def contract(k, t):
        zz = order[k]
        part = got[pl.ds(zz * per_plane, per_plane), :arows, :].reshape(span, naux)
        new = dot_nt(tbuf[t].reshape(pairs, naux), part).astype(BF16)
        cbuf[t, zz] = new.reshape(groups, BS, SUB, span)

    events = {
        (0, 1): [lambda: relay_sides(order[1])],
        (0, 3): [lambda: relay_col(order[3])],
        (1, 0): [lambda: relay_sides(order[2]), lambda: relay_corner(order[1]), lambda: arrive(mates, order[1], 4)],
        (1, 1): [lambda: relay_corner(order[2])],
        (1, 3): [lambda: relay_sides(order[3])],
        (2, 0): [lambda: arrive(mates, order[2], 4)],
        (2, 2): [lambda: relay_corner(order[3])],
        (3, 0): [lambda: arrive(mates, order[3], 4)],
    }

    rotate(0)
    reach(1)
    report(2)
    rotate(1)
    rotate(2)
    reach(2)
    rotate(3)
    relay_sides(order[0])
    relay_col(order[1])
    relay_corner(order[0])
    relay_col(order[2])
    arrive(mates, order[0], 4)
    for k in range(depth):
        for t in range(count):
            for event in events.get((k, t), []):
                event()
            contract(k, t)

    same_row = iota((SUB, SUB, wide), 0) == iota((SUB, SUB, wide), 2) % (SUB * SUB) // SUB
    lanes_of = iota((SUB, 128), 1) // BS

    def compact(square):
        total = jnp.zeros((SUB, 128), F32)
        for g in range(groups):
            total = jnp.where(lanes_of == g, square[g * SUB : (g + 1) * SUB], total)
        return total

    parts = []
    for t in range(count):
        acc = jnp.zeros((wide, wide), F32)
        for at in range(0, BS, SUB):
            left = jnp.concatenate([cbuf[t, zz, :, at : at + SUB].reshape(wide, span) for zz in range(depth)], axis=1)
            acc = acc + dot_nt(left, rbuf[t, :, at : at + SUB].reshape(wide, naux))
        acc = jnp.where(same_row, acc.reshape(groups, SUB, SUB, wide), 0.0)
        parts.append(jnp.sum(acc, axis=1).reshape(BS, wide))
    both = exact(jnp.concatenate(parts, axis=0), fold(wide, 128, inner, minor))
    terms = [compact(both[t * BS : (t + 1) * BS]) for t in range(count)]
    for p in range(n_dev):
        slots = []
        for r in range(own):
            total = jnp.zeros((SUB, 128), F32)
            for t in range(count):
                here = owners[t] * (n_aux * own) + blocks[t] == p * own + r
                total = total + jnp.where(here, terms[t], 0.0)
            slots.append(total)
        vir_send[p] = jnp.concatenate(slots, axis=0).astype(BF16)
    vir_got[me] = vir_send[me]

    def send_vir(k, carry):
        p = lax.rem(me + k, n_dev)
        pltpu.make_async_remote_copy(
            src_ref=vir_send.at[p],
            dst_ref=vir_got.at[me],
            send_sem=trade_sem.at[0],
            recv_sem=trade_sem.at[1],
            device_id=(p // n_aux, p % n_aux),
            device_id_type=MESH,
        ).start()
        return carry

    lax.fori_loop(1, n_dev, send_vir, 0)

    parts = []
    for t in range(count):
        home = owners[t] * n_aux + blocks[t] // own
        row = pick(got[home, arows:, :].astype(F32), blocks[t] % own)
        parts.append(jnp.where(diag, row, 0.0))
    square_v = dot(jnp.concatenate(parts, axis=0).astype(BF16), fold(pairs, wide, minor, inner))
    for t in range(count):
        spread = square_v[t * BS : (t + 1) * BS].reshape(groups, 1, SUB, wide)
        spread = jnp.broadcast_to(spread, (groups, SUB, SUB, wide))
        left = jnp.where(same_row, spread, 0.0).reshape(wide, wide).astype(BF16)
        for at in range(0, BS, SUB):
            new = dot(left, tbuf[t, :, at : at + SUB].reshape(wide, naux)).astype(BF16)
            ybuf[t, :, at : at + SUB] = new.reshape(groups, SUB, SUB, naux)

    parts = []
    for t in range(count):
        acc = jnp.zeros((wide, wide), F32)
        for g in range(groups):
            left = jnp.concatenate([cbuf[t, zz, g].reshape(wide, span) for zz in range(depth)], axis=1)
            acc = acc + dot_nt(left, ybuf[t, g].reshape(wide, naux))
        parts.append(jnp.where(same_sub, acc, 0.0))
    both = exact(jnp.concatenate(parts, axis=0), fold(wide, 128, outer, minor)).reshape(count, groups, SUB, SUB, 128)
    terms = []
    for t in range(count):
        total = jnp.zeros((SUB, SUB, 128), F32)
        for g in range(groups):
            total = jnp.where(lanes_of == g, both[t, g], total)
        terms.append(jnp.sum(total, axis=1))
    for q in range(n_aux):
        slots = []
        for r in range(own):
            total = jnp.zeros((SUB, 128), F32)
            for t in range(count):
                total = total + jnp.where(rows[t] == q * own + r, terms[t], 0.0)
            slots.append(total)
        occ_send[q] = jnp.concatenate(slots, axis=0)
    occ_got[a] = occ_send[a]
    for k in range(1, n_aux):
        q = lax.rem(a + k, n_aux)
        pltpu.make_async_remote_copy(
            src_ref=occ_send.at[q],
            dst_ref=occ_got.at[a],
            send_sem=trade_sem.at[2],
            recv_sem=trade_sem.at[3],
            device_id=(b, q),
            device_id_type=MESH,
        ).start()

    def done(ref, sem):
        pltpu.make_async_copy(ref, ref, sem).wait()

    done(vir_got.at[pl.ds(0, n_dev - 1)], trade_sem.at[1])
    vir_sum = jnp.sum(vir_got[...].astype(F32), axis=0)
    done(occ_got.at[pl.ds(0, n_aux - 1)], trade_sem.at[3])
    occ_sum = jnp.sum(occ_got[...], axis=0)

    sums = jnp.concatenate([occ_sum, vir_sum], axis=0)
    lanes_all = iota(sums.shape, 1) // BS
    parts = [jnp.where(lanes_all == g, sums, 0.0) for g in range(groups)]
    both = exact(jnp.concatenate(parts, axis=0), fold(128, 128, minor, minor))
    both = both.reshape(groups, 2 * own, SUB, 128)
    per_tile = 128 // BS
    lines = []
    for m in range(pairs // 128):
        first = m * per_tile
        here = iota((SUB, 128), 0) == first % SUB + lanes_of
        lines.append(jnp.sum(jnp.where(here, both[first // SUB], 0.0), axis=1))
    flat = jnp.concatenate(lines, axis=1)
    for r in range(own):
        scale = jnp.where(live(sizes[a * own + r]), norm, 0.0).astype(F32)
        out_ref[0, r : r + 1, :] = flat[r : r + 1, :] * scale
        out_ref[1, r : r + 1, :] = flat[own + r : own + r + 1, :] * scale

    done(vir_send.at[pl.ds(0, n_dev - 1)], trade_sem.at[0])
    done(occ_send.at[pl.ds(0, n_aux - 1)], trade_sem.at[2])
    done(got.at[pl.ds(0, depth - 1 + 7 * depth)], send_sem)


def fused(sizes, rows, owners, blocks, adj, occ, vir, three, n_blk, n_aux, norm):
    n_dev = n_blk * n_aux
    count, naux = three.shape[0], three.shape[3]
    own = occ.shape[0] // n_aux
    groups = BS // SUB
    vmem = pl.BlockSpec(memory_space=pltpu.VMEM)
    hbm = pl.BlockSpec(memory_space=pl.ANY)
    tile = pltpu.VMEM((count, groups, BS, SUB, naux), BF16)
    return pl.pallas_call(
        functools.partial(fused_kernel, n_blk, n_aux, norm),
        out_shape=jax.ShapeDtypeStruct((2, own, BS * BS), F32),
        in_specs=[hbm] * 8,
        out_specs=vmem,
        scratch_shapes=[
            *(pltpu.SMEM(scalars.shape, scalars.dtype) for scalars in (sizes, rows, owners, blocks)),
            pltpu.VMEM(occ.shape, BF16),
            pltpu.VMEM(vir.shape, BF16),
            pltpu.VMEM((n_dev, adj.shape[0] + own, naux), BF16),
            tile,
            pltpu.VMEM((count, n_blk // 2, groups, BS, SUB, naux // (n_blk // 2)), BF16),
            tile,
            tile,
            pltpu.VMEM((n_dev, own * SUB, 128), BF16),
            pltpu.VMEM((n_dev, own * SUB, 128), BF16),
            pltpu.VMEM((n_aux, own * SUB, 128), F32),
            pltpu.VMEM((n_aux, own * SUB, 128), F32),
            pltpu.SemaphoreType.DMA((7,)),
            pltpu.SemaphoreType.DMA((count,)),
            pltpu.SemaphoreType.REGULAR((2,)),
            pltpu.SemaphoreType.DMA((4, n_blk // 2)),
            pltpu.SemaphoreType.DMA,
            pltpu.SemaphoreType.DMA((4,)),
        ],
        compiler_params=pltpu.CompilerParams(
            collective_id=0, has_side_effects=True, vmem_limit_bytes=67043328
        ),
        name="fused",
    )(sizes, rows, owners, blocks, adj, occ, vir, three.reshape(count, BS, groups, SUB, naux))


def tile_kernel(
    n_aux, own, sizes, rows, owners, blocks, occ_ref, vir_ref, adj_ref, t_ref, occ_out, vir_out, vir_acc
):
    t = pl.program_id(0)
    pairs = BS * BS
    naux = adj_ref.shape[0]

    @pl.when(t == 0)
    def _():
        occ_out[...] = jnp.zeros_like(occ_out)
        vir_acc[...] = jnp.zeros_like(vir_acc)

    row, owner, block = rows[t], owners[t], blocks[t]
    size = sizes[row]
    lane = iota((1, pairs), 1)
    inside = (lane // BS < size) & (lane % BS < size)
    occ_all = occ_ref[...].astype(F32)
    occ_row = jnp.sum(jnp.where(iota(occ_all.shape, 0) == row, occ_all, 0.0), axis=0, keepdims=True)
    occ_row = jnp.where(inside, occ_row, 0.0)
    home = owner * n_aux + block // own
    vir_all = vir_ref[home].astype(F32)
    vir_row = jnp.sum(jnp.where(iota(vir_all.shape, 0) == block % own, vir_all, 0.0), axis=0, keepdims=True)
    diag = iota((BS, pairs), 1) // BS == iota((BS, pairs), 0)
    fold_minor = (iota((pairs, 128), 0) % BS == iota((pairs, 128), 1) % BS).astype(BF16)
    fold_major = (iota((pairs, 128), 0) // BS == iota((pairs, 128), 1) % BS).astype(BF16)
    spread = (iota((128, pairs), 0) == iota((128, pairs), 1) // BS).astype(BF16)
    repeat = pairs // 128

    def square(flat):
        return jnp.dot(jnp.where(diag, flat, 0.0).astype(BF16), fold_minor, preferred_element_type=F32)

    occ_rep = jnp.dot(square(occ_row).astype(BF16), spread, preferred_element_type=F32)
    vir_rep = jnp.concatenate([square(vir_row)] * repeat, axis=1)

    nt = (((1,), (1,)), ((), ()))
    acc = jnp.zeros((BS, pairs), F32)
    lines = []
    for first in range(0, pairs, CHUNK):
        part = lax.dot_general(t_ref[0, first : first + CHUNK, :], adj_ref[...], nt, preferred_element_type=F32)
        gram = lax.dot_general(part.astype(BF16), t_ref[0], nt, preferred_element_type=F32)
        for at in range(CHUNK // BS):
            i = first // BS + at
            block_i = gram[at * BS : (at + 1) * BS, :]
            acc = acc + block_i * occ_rep[i : i + 1, :]
            lines.append(jnp.sum(block_i * vir_rep, axis=0, keepdims=True))
    zmat = jnp.concatenate(lines, axis=0)

    def flatten(mat, fold):
        high = mat.astype(BF16)
        low = (mat - high.astype(F32)).astype(BF16)
        both = jnp.dot(high, fold, preferred_element_type=F32) + jnp.dot(low, fold, preferred_element_type=F32)
        wide = jnp.concatenate([both] * repeat, axis=1)
        return jnp.sum(jnp.where(diag, wide, 0.0), axis=0, keepdims=True)

    occ_flat = flatten(zmat, fold_major)
    vir_flat = flatten(acc, fold_minor)
    slot = iota((own, pairs), 0)
    occ_out[row // own] = occ_out[row // own] + jnp.where(slot == row % own, occ_flat, 0.0)
    vir_acc[home] = vir_acc[home] + jnp.where(slot == block % own, vir_flat, 0.0)

    @pl.when(t == pl.num_programs(0) - 1)
    def _():
        vir_out[...] = vir_acc[...].astype(vir_out.dtype)


def tiles(sizes, rows, owners, blocks, occ, vir, adj, three, n_dev, n_aux):
    count, pairs, naux = three.shape
    own = occ.shape[0] // n_aux
    smem = pl.BlockSpec(memory_space=pltpu.SMEM)
    vmem = pl.BlockSpec(memory_space=pltpu.VMEM)
    return pl.pallas_call(
        functools.partial(tile_kernel, n_aux, own),
        grid=(count,),
        out_shape=(
            jax.ShapeDtypeStruct((n_aux, own, pairs), F32),
            jax.ShapeDtypeStruct((n_dev, own, pairs), BF16),
        ),
        in_specs=[smem] * 4 + [vmem] * 3 + [pl.BlockSpec((1, pairs, naux), lambda t: (t, 0, 0))],
        out_specs=(vmem, vmem),
        scratch_shapes=[pltpu.VMEM((n_dev, own, pairs), F32)],
        compiler_params=pltpu.CompilerParams(vmem_limit_bytes=48 * 1024 * 1024),
        name="tiles",
    )(sizes, rows, owners, blocks, occ, vir, adj, three)


def exchange_kernel(
    n_blk, n_aux, norm, sizes, occ_ref, vir_ref, occ_out, vir_out, occ_got, vir_got, occ_sems, vir_sems
):
    n_dev = n_blk * n_aux
    b = lax.axis_index("blk")
    a = lax.axis_index("aux")
    me = b * n_aux + a
    barrier = pltpu.get_barrier_semaphore()

    def greet(k, carry):
        p = lax.rem(me + k, n_dev)
        pl.semaphore_signal(barrier, inc=1, device_id=(p // n_aux, p % n_aux), device_id_type=MESH)
        return carry

    lax.fori_loop(1, n_dev, greet, 0)
    pl.semaphore_wait(barrier, n_dev - 1)

    trade(n_blk, n_aux, norm, sizes, occ_ref, vir_ref, occ_out, vir_out, occ_got, vir_got, occ_sems, vir_sems)


def trade(n_blk, n_aux, norm, sizes, occ_ref, vir_ref, occ_out, vir_out, occ_got, vir_got, occ_sems, vir_sems):
    n_dev = n_blk * n_aux
    b = lax.axis_index("blk")
    a = lax.axis_index("aux")
    me = b * n_aux + a
    own, pairs = occ_out.shape

    def vir_copy(k, source):
        p = lax.rem(me + k, n_dev)
        return pltpu.make_async_remote_copy(
            src_ref=vir_ref.at[p],
            dst_ref=vir_got.at[source],
            send_sem=vir_sems.at[0, k],
            recv_sem=vir_sems.at[1, source],
            device_id=(p // n_aux, p % n_aux),
            device_id_type=MESH,
        )

    def occ_copy(k, source):
        q = lax.rem(a + k, n_aux)
        return pltpu.make_async_remote_copy(
            src_ref=occ_ref.at[q],
            dst_ref=occ_got.at[source],
            send_sem=occ_sems.at[0, k],
            recv_sem=occ_sems.at[1, source],
            device_id=(b, q),
            device_id_type=MESH,
        )

    def start_vir(k, carry):
        vir_copy(k, me).start()
        return carry

    def start_occ(k, carry):
        occ_copy(k, a).start()
        return carry

    lax.fori_loop(1, n_dev, start_vir, 0)
    lax.fori_loop(1, n_aux, start_occ, 0)

    def take_vir(k, total):
        source = lax.rem(me + k, n_dev)
        vir_copy(k, source).wait_recv()
        return total + vir_got[source].astype(F32)

    def take_occ(k, total):
        source = lax.rem(a + k, n_aux)
        occ_copy(k, source).wait_recv()
        return total + occ_got[source]

    occ_sum = lax.fori_loop(1, n_aux, take_occ, occ_ref[a])
    vir_sum = lax.fori_loop(1, n_dev, take_vir, vir_ref[me].astype(F32))
    lane = iota((1, pairs), 1)
    for r in range(own):
        size = sizes[a * own + r]
        scale = jnp.where((lane // BS < size) & (lane % BS < size), norm, 0.0).astype(F32)
        occ_out[r : r + 1, :] = occ_sum[r : r + 1, :] * scale
        vir_out[r : r + 1, :] = vir_sum[r : r + 1, :] * scale

    def end_vir(k, carry):
        vir_copy(k, me).wait_send()
        return carry

    def end_occ(k, carry):
        occ_copy(k, a).wait_send()
        return carry

    lax.fori_loop(1, n_dev, end_vir, 0)
    lax.fori_loop(1, n_aux, end_occ, 0)


def exchange(sizes, occ, vir, n_blk, n_aux, norm):
    n_dev, own, pairs = vir.shape
    vmem = pl.BlockSpec(memory_space=pltpu.VMEM)
    out = jax.ShapeDtypeStruct((own, pairs), F32)
    return pl.pallas_call(
        functools.partial(exchange_kernel, n_blk, n_aux, norm),
        out_shape=(out, out),
        in_specs=[pl.BlockSpec(memory_space=pltpu.SMEM), vmem, vmem],
        out_specs=(vmem, vmem),
        scratch_shapes=[
            pltpu.VMEM(occ.shape, occ.dtype),
            pltpu.VMEM(vir.shape, vir.dtype),
            pltpu.SemaphoreType.DMA((2, n_aux)),
            pltpu.SemaphoreType.DMA((2, n_dev)),
        ],
        compiler_params=pltpu.CompilerParams(collective_id=1, has_side_effects=True),
        name="exchange",
    )(sizes, occ, vir)


def shards(
    n_blk, n_aux, adjoint, three_centre, occ_density, vir_density, block_sizes, tile_rows, col_owner, col_block
):
    n_dev = n_blk * n_aux
    count = three_centre.shape[0]
    naux = three_centre.shape[3]
    own = occ_density.shape[0] // n_aux
    depth = adjoint.shape[0]
    three = three_centre.reshape(count, BS * BS, naux)
    if n_aux == 4 and n_blk == 8:
        both = fused(
            block_sizes, tile_rows, col_owner.reshape(count), col_block, adjoint, occ_density, vir_density,
            three_centre, n_blk, n_aux, naux ** -0.5,
        )
        return both[0], both[1]
    aux_here = lax.axis_index("aux")
    own_sizes = lax.dynamic_slice_in_dim(block_sizes, aux_here * own, own, 0)
    own_vir = lax.dynamic_slice_in_dim(vir_density, aux_here * own, own, 0)
    lane = jnp.arange(BS * BS, dtype=jnp.int32)[None, :]
    inside = (lane // BS < own_sizes[:, None]) & (lane % BS < own_sizes[:, None])
    own_vir = jnp.where(inside, own_vir, jnp.zeros_like(own_vir))
    got = lax.all_gather(jnp.concatenate((adjoint, own_vir), axis=0), ("blk", "aux"), axis=0)
    adj = got[:, :depth, :].reshape(naux, naux)
    vir = got[:, depth:, :]
    occ_terms, vir_terms = tiles(
        block_sizes, tile_rows, col_owner.reshape(count), col_block, occ_density, vir, adj,
        three, n_dev, n_aux,
    )
    return exchange(block_sizes, occ_terms, vir_terms, n_blk, n_aux, naux ** -0.5)


def solution(mesh):
    in_specs = (
        P(("blk", "aux"), None),
        P(("blk", "aux"), None, None, None),
        P("blk", None),
        P("blk", None),
        P("blk"),
        P(("blk", "aux")),
        P(("blk", "aux"), None),
        P(("blk", "aux")),
    )
    out_specs = (P(("blk", "aux"), None), P(("blk", "aux"), None))
    body = functools.partial(shards, mesh.shape["blk"], mesh.shape["aux"])
    return jax.shard_map(body, mesh=mesh, in_specs=in_specs, out_specs=out_specs, check_vma=False)
```

```python
import functools

import jax
import jax.numpy as jnp
from jax import lax
from jax.experimental import pallas as pl
from jax.experimental.pallas import tpu as pltpu
from jax.sharding import PartitionSpec as P

BS = 32
SUB = 8
CHUNK = 256
MESH = pl.DeviceIdType.MESH
F32 = jnp.float32
BF16 = jnp.bfloat16


def iota(shape, dim):
    return lax.broadcasted_iota(jnp.int32, shape, dim)


def dot(left, right):
    return jnp.dot(left, right, preferred_element_type=F32)


def dot_nt(left, right):
    return lax.dot_general(left, right, (((1,), (1,)), ((), ())), preferred_element_type=F32)


def fold(rows, lanes, row_key, lane_key):
    return (row_key(iota((rows, lanes), 0)) == lane_key(iota((rows, lanes), 1))).astype(BF16)


def exact(mat, folding):
    high = mat.astype(BF16)
    low = (mat - high.astype(F32)).astype(BF16)
    return dot(high, folding) + dot(low, folding)


def minor(index):
    return index % BS


def inner(index):
    return index // (SUB * SUB) * SUB + index % SUB


def outer(index):
    return index // SUB


def fused_kernel(
    n_blk, n_aux, norm,
    sizes_hbm, rows_hbm, owners_hbm, blocks_hbm, adj_hbm, occ_hbm, vir_hbm, t_hbm,
    out_ref,
    sizes, rows, owners, blocks, occ_ref, vir_ref, got, tbuf, cbuf, rbuf, ybuf, vir_send, vir_got, occ_send, occ_got,
    in_sem, t_sem, near_sem, recv_sem, send_sem, trade_sem,
):
    n_dev = n_blk * n_aux
    depth = n_blk // 2
    count, groups, _, _, naux = tbuf.shape
    pairs = BS * BS
    wide = BS * SUB
    own = out_ref.shape[1]
    arows = adj_hbm.shape[0]
    half = arows // 2
    span = naux // depth
    per_plane = n_dev // depth
    b = lax.axis_index("blk")
    a = lax.axis_index("aux")
    z, y, x, c = b // 2, b % 2, a // 2, a % 2
    col, sides, corner, mates = range(4)
    over_x = (b, (1 - x) * 2 + c)
    over_y = (z * 2 + 1 - y, a)
    across = (z * 2 + 1 - y, (1 - x) * 2 + c)
    mate = (b, x * 2 + 1 - c)
    above, below = (b + 2, a), (b - 2, a)
    has_up, has_down = z < depth - 1, z > 0
    me = b * n_aux + a

    def ident(xx, yy, zz, cc):
        return ((zz * 2 + yy) * 2 + xx) * 2 + cc

    barrier = pltpu.get_barrier_semaphore()

    def tell(sem, device):
        pl.semaphore_signal(sem, inc=1, device_id=device, device_id_type=MESH)

    for device in (over_x, over_y, across, mate):
        tell(barrier, device)
    pl.when(has_up)(lambda: tell(barrier, above))
    pl.when(has_down)(lambda: tell(barrier, below))

    pairs_in = (
        (vir_hbm, vir_ref), (sizes_hbm, sizes), (adj_hbm, got.at[me, pl.ds(0, arows)]),
        (rows_hbm, rows), (occ_hbm, occ_ref), (owners_hbm, owners), (blocks_hbm, blocks),
    )
    fetches = [pltpu.make_async_copy(src, dst, in_sem.at[i]) for i, (src, dst) in enumerate(pairs_in)]
    for fetch in fetches:
        fetch.start()

    lane = iota((1, pairs), 1)
    diag = iota((BS, pairs), 1) // BS == iota((BS, pairs), 0)

    def live(size):
        return (lane // BS < size) & (lane % BS < size)

    def pick(all_rows, at):
        return jnp.sum(jnp.where(iota(all_rows.shape, 0) == at, all_rows, 0.0), axis=0, keepdims=True)

    for fetch in fetches:
        fetch.wait()
    for t in range(count):
        for g in range(groups):
            pltpu.make_async_copy(t_hbm.at[t, :, g], tbuf.at[t, g], t_sem.at[t]).start()
    vir_all = vir_ref[...].astype(F32)
    mine = [jnp.where(live(sizes[a * own + r]), pick(vir_all, a * own + r), 0.0) for r in range(own)]
    got[me, arows:, :] = jnp.concatenate(mine, axis=0).astype(BF16)

    pl.semaphore_wait(barrier, 4 + has_up.astype(jnp.int32) + has_down.astype(jnp.int32))

    def send(block, device, kind, zz, part=None):
        ref = got.at[block] if part is None else got.at[block, part]
        pltpu.make_async_remote_copy(
            src_ref=ref,
            dst_ref=ref,
            send_sem=send_sem,
            recv_sem=recv_sem.at[kind, zz],
            device_id=device,
            device_id_type=MESH,
        ).start()

    def arrive(kind, zz, number):
        part = got.at[pl.ds(0, number)]
        pltpu.make_async_copy(part, part, recv_sem.at[kind, zz]).wait()

    for device in (over_x, over_y):
        send(me, device, sides, z)
    pl.when(has_up)(lambda: send(me, above, col, z))
    pl.when(has_down)(lambda: send(me, below, col, z))
    send(me, across, corner, z)
    send(me, mate, mates, z)

    def report(hop):
        pl.when(has_down & (z + hop < depth))(lambda: tell(near_sem.at[0], below))
        pl.when(has_up & (z - hop >= 0))(lambda: tell(near_sem.at[1], above))

    def reach(hop):
        @pl.when(z + hop + 1 < depth)
        def _():
            pl.semaphore_wait(near_sem.at[0], 1)
            send(me, (b + 2 * (hop + 1), a), col, z)

        @pl.when(z - hop - 1 >= 0)
        def _():
            pl.semaphore_wait(near_sem.at[1], 1)
            send(me, (b - 2 * (hop + 1), a), col, z)

    def relay_col(zz):
        block = ident(x, y, zz, c)
        arrive(col, zz, 1)
        send(block, over_x, sides, zz)
        send(block, over_y, sides, zz)
        send(block, mate, mates, zz)

    def relay_sides(zz, halves=True):
        arrive(sides, zz, 2)
        block_x, block_y = ident(1 - x, y, zz, c), ident(x, 1 - y, zz, c)
        if halves:
            send(block_x, over_y, corner, zz, pl.ds(0, half))
            send(block_y, over_x, corner, zz, pl.ds(half, arows + own - half))
        send(block_x, mate, mates, zz)
        send(block_y, mate, mates, zz)

    def relay_corner(zz):
        arrive(corner, zz, 1)
        send(ident(1 - x, 1 - y, zz, c), mate, mates, zz)

    def ready(zz):
        arrive(mates, zz, 4)

    low = z < depth // 2
    zl = jnp.where(low, z, depth - 1 - z)

    def plane(k):
        near = zl + k // 2 if k % 2 == 0 else zl - (k + 1) // 2
        at = jnp.where(k <= 2 * zl, near, k)
        return jnp.where(low, at, depth - 1 - at)

    order = [plane(k) for k in range(depth)]

    report(1)
    occ_all = occ_ref[...].astype(F32)
    parts = []
    for t in range(count):
        row = jnp.where(live(sizes[rows[t]]), pick(occ_all, rows[t]), 0.0)
        parts.append(jnp.where(diag, row, 0.0))
    square = dot(jnp.concatenate(parts, axis=0).astype(BF16), fold(pairs, wide, minor, outer))
    same_sub = iota((wide, wide), 0) % SUB == iota((wide, wide), 1) % SUB

    def rotate(t):
        spread = jnp.broadcast_to(square[t * BS : (t + 1) * BS][:, None, :], (BS, SUB, wide)).reshape(wide, wide)
        left = jnp.where(same_sub, spread, 0.0).astype(BF16)
        pltpu.make_async_copy(tbuf.at[t], tbuf.at[t], t_sem.at[t]).wait()
        for g in range(groups):
            rbuf[t, g] = dot(left, tbuf[t, g].reshape(wide, naux)).astype(BF16).reshape(BS, SUB, naux)

    def contract(k, t):
        zz = order[k]
        part = got[pl.ds(zz * per_plane, per_plane), :arows, :].reshape(span, naux)
        for first in range(0, groups, groups // 2):
            rows_of = pl.ds(first, groups // 2)
            new = dot_nt(tbuf[t, rows_of].reshape(pairs // 2, naux), part).astype(BF16)
            cbuf[t, zz, rows_of] = new.reshape(groups // 2, BS, SUB, span)

    reach(1)
    report(2)
    rotate(0)
    reach(2)
    rotate(1)
    relay_sides(z, halves=False)
    relay_col(order[1])
    rotate(2)
    rotate(3)
    relay_corner(z)
    relay_col(order[2])
    relay_sides(order[1])
    arrive(mates, z, 4)
    events = {
        (0, 1): [(relay_col, 3)],
        (1, 0): [(relay_corner, 1), (relay_sides, 2), (ready, 1)],
        (1, 1): [(relay_corner, 2), (relay_sides, 3)],
        (2, 0): [(ready, 2)],
        (2, 1): [(relay_corner, 3)],
        (3, 0): [(ready, 3)],
    }
    for k in range(depth):
        for part in range(2):
            for event, which in events.get((k, part), []):
                event(order[which])
            for t in range(part * count // 2, (part + 1) * count // 2):
                contract(k, t)

    same_row = iota((SUB, SUB, wide), 0) == iota((SUB, SUB, wide), 2) % (SUB * SUB) // SUB
    lanes_of = iota((SUB, 128), 1) // BS

    def compact(square):
        total = jnp.zeros((SUB, 128), F32)
        for g in range(groups):
            total = jnp.where(lanes_of == g, square[g * SUB : (g + 1) * SUB], total)
        return total

    parts = []
    for t in range(count):
        acc = jnp.zeros((wide, wide), F32)
        for at in range(0, BS, SUB):
            left = jnp.concatenate([cbuf[t, zz, :, at : at + SUB].reshape(wide, span) for zz in range(depth)], axis=1)
            acc = acc + dot_nt(left, rbuf[t, :, at : at + SUB].reshape(wide, naux))
        acc = jnp.where(same_row, acc.reshape(groups, SUB, SUB, wide), 0.0)
        parts.append(jnp.sum(acc, axis=1).reshape(BS, wide))
    both = exact(jnp.concatenate(parts, axis=0), fold(wide, 128, inner, minor))
    terms = [compact(both[t * BS : (t + 1) * BS]) for t in range(count)]
    for p in range(n_dev):
        slots = []
        for r in range(own):
            total = jnp.zeros((SUB, 128), F32)
            for t in range(count):
                here = owners[t] * (n_aux * own) + blocks[t] == p * own + r
                total = total + jnp.where(here, terms[t], 0.0)
            slots.append(total)
        vir_send[p] = jnp.concatenate(slots, axis=0).astype(BF16)
    vir_got[me] = vir_send[me]

    def send_vir(k, carry):
        p = lax.rem(me + k, n_dev)
        pltpu.make_async_remote_copy(
            src_ref=vir_send.at[p],
            dst_ref=vir_got.at[me],
            send_sem=trade_sem.at[0],
            recv_sem=trade_sem.at[1],
            device_id=(p // n_aux, p % n_aux),
            device_id_type=MESH,
        ).start()
        return carry

    lax.fori_loop(1, n_dev, send_vir, 0)

    parts = []
    for t in range(count):
        home = owners[t] * n_aux + blocks[t] // own
        row = pick(got[home, arows:, :].astype(F32), blocks[t] % own)
        parts.append(jnp.where(diag, row, 0.0))
    square_v = dot(jnp.concatenate(parts, axis=0).astype(BF16), fold(pairs, wide, minor, inner))
    for t in range(count):
        spread = square_v[t * BS : (t + 1) * BS].reshape(groups, 1, SUB, wide)
        spread = jnp.broadcast_to(spread, (groups, SUB, SUB, wide))
        left = jnp.where(same_row, spread, 0.0).reshape(wide, wide).astype(BF16)
        for at in range(0, BS, SUB):
            new = dot(left, tbuf[t, :, at : at + SUB].reshape(wide, naux)).astype(BF16)
            ybuf[t, :, at : at + SUB] = new.reshape(groups, SUB, SUB, naux)

    parts = []
    for t in range(count):
        acc = jnp.zeros((wide, wide), F32)
        for g in range(groups):
            left = jnp.concatenate([cbuf[t, zz, g].reshape(wide, span) for zz in range(depth)], axis=1)
            acc = acc + dot_nt(left, ybuf[t, g].reshape(wide, naux))
        parts.append(jnp.where(same_sub, acc, 0.0))
    both = exact(jnp.concatenate(parts, axis=0), fold(wide, 128, outer, minor)).reshape(count, groups, SUB, SUB, 128)
    terms = []
    for t in range(count):
        total = jnp.zeros((SUB, SUB, 128), F32)
        for g in range(groups):
            total = jnp.where(lanes_of == g, both[t, g], total)
        terms.append(jnp.sum(total, axis=1))
    for q in range(n_aux):
        slots = []
        for r in range(own):
            total = jnp.zeros((SUB, 128), F32)
            for t in range(count):
                total = total + jnp.where(rows[t] == q * own + r, terms[t], 0.0)
            slots.append(total)
        occ_send[q] = jnp.concatenate(slots, axis=0)
    occ_got[a] = occ_send[a]
    for k in range(1, n_aux):
        q = lax.rem(a + k, n_aux)
        pltpu.make_async_remote_copy(
            src_ref=occ_send.at[q],
            dst_ref=occ_got.at[a],
            send_sem=trade_sem.at[2],
            recv_sem=trade_sem.at[3],
            device_id=(b, q),
            device_id_type=MESH,
        ).start()

    def done(ref, sem):
        pltpu.make_async_copy(ref, ref, sem).wait()

    done(vir_got.at[pl.ds(0, n_dev - 1)], trade_sem.at[1])
    vir_sum = jnp.sum(vir_got[...].astype(F32), axis=0)
    done(occ_got.at[pl.ds(0, n_aux - 1)], trade_sem.at[3])
    occ_sum = jnp.sum(occ_got[...], axis=0)

    sums = jnp.concatenate([occ_sum, vir_sum], axis=0)
    lanes_all = iota(sums.shape, 1) // BS
    parts = [jnp.where(lanes_all == g, sums, 0.0) for g in range(groups)]
    both = exact(jnp.concatenate(parts, axis=0), fold(128, 128, minor, minor))
    both = both.reshape(groups, 2 * own, SUB, 128)
    per_tile = 128 // BS
    lines = []
    for m in range(pairs // 128):
        first = m * per_tile
        here = iota((SUB, 128), 0) == first % SUB + lanes_of
        lines.append(jnp.sum(jnp.where(here, both[first // SUB], 0.0), axis=1))
    flat = jnp.concatenate(lines, axis=1)
    for r in range(own):
        scale = jnp.where(live(sizes[a * own + r]), norm, 0.0).astype(F32)
        out_ref[0, r : r + 1, :] = flat[r : r + 1, :] * scale
        out_ref[1, r : r + 1, :] = flat[own + r : own + r + 1, :] * scale

    done(vir_send.at[pl.ds(0, n_dev - 1)], trade_sem.at[0])
    done(occ_send.at[pl.ds(0, n_aux - 1)], trade_sem.at[2])
    done(got.at[pl.ds(0, depth - 1 + 7 * depth)], send_sem)


def fused(sizes, rows, owners, blocks, adj, occ, vir, three, n_blk, n_aux, norm):
    n_dev = n_blk * n_aux
    count, naux = three.shape[0], three.shape[3]
    own = occ.shape[0] // n_aux
    groups = BS // SUB
    vmem = pl.BlockSpec(memory_space=pltpu.VMEM)
    hbm = pl.BlockSpec(memory_space=pl.ANY)
    tile = pltpu.VMEM((count, groups, BS, SUB, naux), BF16)
    return pl.pallas_call(
        functools.partial(fused_kernel, n_blk, n_aux, norm),
        out_shape=jax.ShapeDtypeStruct((2, own, BS * BS), F32),
        in_specs=[hbm] * 8,
        out_specs=vmem,
        scratch_shapes=[
            *(pltpu.SMEM(scalars.shape, scalars.dtype) for scalars in (sizes, rows, owners, blocks)),
            pltpu.VMEM(occ.shape, BF16),
            pltpu.VMEM(vir.shape, BF16),
            pltpu.VMEM((n_dev, adj.shape[0] + own, naux), BF16),
            tile,
            pltpu.VMEM((count, n_blk // 2, groups, BS, SUB, naux // (n_blk // 2)), BF16),
            tile,
            tile,
            pltpu.VMEM((n_dev, own * SUB, 128), BF16),
            pltpu.VMEM((n_dev, own * SUB, 128), BF16),
            pltpu.VMEM((n_aux, own * SUB, 128), F32),
            pltpu.VMEM((n_aux, own * SUB, 128), F32),
            pltpu.SemaphoreType.DMA((7,)),
            pltpu.SemaphoreType.DMA((count,)),
            pltpu.SemaphoreType.REGULAR((2,)),
            pltpu.SemaphoreType.DMA((4, n_blk // 2)),
            pltpu.SemaphoreType.DMA,
            pltpu.SemaphoreType.DMA((4,)),
        ],
        compiler_params=pltpu.CompilerParams(
            collective_id=0, has_side_effects=True, vmem_limit_bytes=67043328
        ),
        name="fused",
    )(sizes, rows, owners, blocks, adj, occ, vir, three.reshape(count, BS, groups, SUB, naux))


def tile_kernel(
    n_aux, own, sizes, rows, owners, blocks, occ_ref, vir_ref, adj_ref, t_ref, occ_out, vir_out, vir_acc
):
    t = pl.program_id(0)
    pairs = BS * BS
    naux = adj_ref.shape[0]

    @pl.when(t == 0)
    def _():
        occ_out[...] = jnp.zeros_like(occ_out)
        vir_acc[...] = jnp.zeros_like(vir_acc)

    row, owner, block = rows[t], owners[t], blocks[t]
    size = sizes[row]
    lane = iota((1, pairs), 1)
    inside = (lane // BS < size) & (lane % BS < size)
    occ_all = occ_ref[...].astype(F32)
    occ_row = jnp.sum(jnp.where(iota(occ_all.shape, 0) == row, occ_all, 0.0), axis=0, keepdims=True)
    occ_row = jnp.where(inside, occ_row, 0.0)
    home = owner * n_aux + block // own
    vir_all = vir_ref[home].astype(F32)
    vir_row = jnp.sum(jnp.where(iota(vir_all.shape, 0) == block % own, vir_all, 0.0), axis=0, keepdims=True)
    diag = iota((BS, pairs), 1) // BS == iota((BS, pairs), 0)
    fold_minor = (iota((pairs, 128), 0) % BS == iota((pairs, 128), 1) % BS).astype(BF16)
    fold_major = (iota((pairs, 128), 0) // BS == iota((pairs, 128), 1) % BS).astype(BF16)
    spread = (iota((128, pairs), 0) == iota((128, pairs), 1) // BS).astype(BF16)
    repeat = pairs // 128

    def square(flat):
        return jnp.dot(jnp.where(diag, flat, 0.0).astype(BF16), fold_minor, preferred_element_type=F32)

    occ_rep = jnp.dot(square(occ_row).astype(BF16), spread, preferred_element_type=F32)
    vir_rep = jnp.concatenate([square(vir_row)] * repeat, axis=1)

    nt = (((1,), (1,)), ((), ()))
    acc = jnp.zeros((BS, pairs), F32)
    lines = []
    for first in range(0, pairs, CHUNK):
        part = lax.dot_general(t_ref[0, first : first + CHUNK, :], adj_ref[...], nt, preferred_element_type=F32)
        gram = lax.dot_general(part.astype(BF16), t_ref[0], nt, preferred_element_type=F32)
        for at in range(CHUNK // BS):
            i = first // BS + at
            block_i = gram[at * BS : (at + 1) * BS, :]
            acc = acc + block_i * occ_rep[i : i + 1, :]
            lines.append(jnp.sum(block_i * vir_rep, axis=0, keepdims=True))
    zmat = jnp.concatenate(lines, axis=0)

    def flatten(mat, fold):
        high = mat.astype(BF16)
        low = (mat - high.astype(F32)).astype(BF16)
        both = jnp.dot(high, fold, preferred_element_type=F32) + jnp.dot(low, fold, preferred_element_type=F32)
        wide = jnp.concatenate([both] * repeat, axis=1)
        return jnp.sum(jnp.where(diag, wide, 0.0), axis=0, keepdims=True)

    occ_flat = flatten(zmat, fold_major)
    vir_flat = flatten(acc, fold_minor)
    slot = iota((own, pairs), 0)
    occ_out[row // own] = occ_out[row // own] + jnp.where(slot == row % own, occ_flat, 0.0)
    vir_acc[home] = vir_acc[home] + jnp.where(slot == block % own, vir_flat, 0.0)

    @pl.when(t == pl.num_programs(0) - 1)
    def _():
        vir_out[...] = vir_acc[...].astype(vir_out.dtype)


def tiles(sizes, rows, owners, blocks, occ, vir, adj, three, n_dev, n_aux):
    count, pairs, naux = three.shape
    own = occ.shape[0] // n_aux
    smem = pl.BlockSpec(memory_space=pltpu.SMEM)
    vmem = pl.BlockSpec(memory_space=pltpu.VMEM)
    return pl.pallas_call(
        functools.partial(tile_kernel, n_aux, own),
        grid=(count,),
        out_shape=(
            jax.ShapeDtypeStruct((n_aux, own, pairs), F32),
            jax.ShapeDtypeStruct((n_dev, own, pairs), BF16),
        ),
        in_specs=[smem] * 4 + [vmem] * 3 + [pl.BlockSpec((1, pairs, naux), lambda t: (t, 0, 0))],
        out_specs=(vmem, vmem),
        scratch_shapes=[pltpu.VMEM((n_dev, own, pairs), F32)],
        compiler_params=pltpu.CompilerParams(vmem_limit_bytes=48 * 1024 * 1024),
        name="tiles",
    )(sizes, rows, owners, blocks, occ, vir, adj, three)


def exchange_kernel(
    n_blk, n_aux, norm, sizes, occ_ref, vir_ref, occ_out, vir_out, occ_got, vir_got, occ_sems, vir_sems
):
    n_dev = n_blk * n_aux
    b = lax.axis_index("blk")
    a = lax.axis_index("aux")
    me = b * n_aux + a
    barrier = pltpu.get_barrier_semaphore()

    def greet(k, carry):
        p = lax.rem(me + k, n_dev)
        pl.semaphore_signal(barrier, inc=1, device_id=(p // n_aux, p % n_aux), device_id_type=MESH)
        return carry

    lax.fori_loop(1, n_dev, greet, 0)
    pl.semaphore_wait(barrier, n_dev - 1)

    trade(n_blk, n_aux, norm, sizes, occ_ref, vir_ref, occ_out, vir_out, occ_got, vir_got, occ_sems, vir_sems)


def trade(n_blk, n_aux, norm, sizes, occ_ref, vir_ref, occ_out, vir_out, occ_got, vir_got, occ_sems, vir_sems):
    n_dev = n_blk * n_aux
    b = lax.axis_index("blk")
    a = lax.axis_index("aux")
    me = b * n_aux + a
    own, pairs = occ_out.shape

    def vir_copy(k, source):
        p = lax.rem(me + k, n_dev)
        return pltpu.make_async_remote_copy(
            src_ref=vir_ref.at[p],
            dst_ref=vir_got.at[source],
            send_sem=vir_sems.at[0, k],
            recv_sem=vir_sems.at[1, source],
            device_id=(p // n_aux, p % n_aux),
            device_id_type=MESH,
        )

    def occ_copy(k, source):
        q = lax.rem(a + k, n_aux)
        return pltpu.make_async_remote_copy(
            src_ref=occ_ref.at[q],
            dst_ref=occ_got.at[source],
            send_sem=occ_sems.at[0, k],
            recv_sem=occ_sems.at[1, source],
            device_id=(b, q),
            device_id_type=MESH,
        )

    def start_vir(k, carry):
        vir_copy(k, me).start()
        return carry

    def start_occ(k, carry):
        occ_copy(k, a).start()
        return carry

    lax.fori_loop(1, n_dev, start_vir, 0)
    lax.fori_loop(1, n_aux, start_occ, 0)

    def take_vir(k, total):
        source = lax.rem(me + k, n_dev)
        vir_copy(k, source).wait_recv()
        return total + vir_got[source].astype(F32)

    def take_occ(k, total):
        source = lax.rem(a + k, n_aux)
        occ_copy(k, source).wait_recv()
        return total + occ_got[source]

    occ_sum = lax.fori_loop(1, n_aux, take_occ, occ_ref[a])
    vir_sum = lax.fori_loop(1, n_dev, take_vir, vir_ref[me].astype(F32))
    lane = iota((1, pairs), 1)
    for r in range(own):
        size = sizes[a * own + r]
        scale = jnp.where((lane // BS < size) & (lane % BS < size), norm, 0.0).astype(F32)
        occ_out[r : r + 1, :] = occ_sum[r : r + 1, :] * scale
        vir_out[r : r + 1, :] = vir_sum[r : r + 1, :] * scale

    def end_vir(k, carry):
        vir_copy(k, me).wait_send()
        return carry

    def end_occ(k, carry):
        occ_copy(k, a).wait_send()
        return carry

    lax.fori_loop(1, n_dev, end_vir, 0)
    lax.fori_loop(1, n_aux, end_occ, 0)


def exchange(sizes, occ, vir, n_blk, n_aux, norm):
    n_dev, own, pairs = vir.shape
    vmem = pl.BlockSpec(memory_space=pltpu.VMEM)
    out = jax.ShapeDtypeStruct((own, pairs), F32)
    return pl.pallas_call(
        functools.partial(exchange_kernel, n_blk, n_aux, norm),
        out_shape=(out, out),
        in_specs=[pl.BlockSpec(memory_space=pltpu.SMEM), vmem, vmem],
        out_specs=(vmem, vmem),
        scratch_shapes=[
            pltpu.VMEM(occ.shape, occ.dtype),
            pltpu.VMEM(vir.shape, vir.dtype),
            pltpu.SemaphoreType.DMA((2, n_aux)),
            pltpu.SemaphoreType.DMA((2, n_dev)),
        ],
        compiler_params=pltpu.CompilerParams(collective_id=1, has_side_effects=True),
        name="exchange",
    )(sizes, occ, vir)


def shards(
    n_blk, n_aux, adjoint, three_centre, occ_density, vir_density, block_sizes, tile_rows, col_owner, col_block
):
    n_dev = n_blk * n_aux
    count = three_centre.shape[0]
    naux = three_centre.shape[3]
    own = occ_density.shape[0] // n_aux
    depth = adjoint.shape[0]
    three = three_centre.reshape(count, BS * BS, naux)
    if n_aux == 4 and n_blk == 8:
        both = fused(
            block_sizes, tile_rows, col_owner.reshape(count), col_block, adjoint, occ_density, vir_density,
            three_centre, n_blk, n_aux, naux ** -0.5,
        )
        return both[0], both[1]
    aux_here = lax.axis_index("aux")
    own_sizes = lax.dynamic_slice_in_dim(block_sizes, aux_here * own, own, 0)
    own_vir = lax.dynamic_slice_in_dim(vir_density, aux_here * own, own, 0)
    lane = jnp.arange(BS * BS, dtype=jnp.int32)[None, :]
    inside = (lane // BS < own_sizes[:, None]) & (lane % BS < own_sizes[:, None])
    own_vir = jnp.where(inside, own_vir, jnp.zeros_like(own_vir))
    got = lax.all_gather(jnp.concatenate((adjoint, own_vir), axis=0), ("blk", "aux"), axis=0)
    adj = got[:, :depth, :].reshape(naux, naux)
    vir = got[:, depth:, :]
    occ_terms, vir_terms = tiles(
        block_sizes, tile_rows, col_owner.reshape(count), col_block, occ_density, vir, adj,
        three, n_dev, n_aux,
    )
    return exchange(block_sizes, occ_terms, vir_terms, n_blk, n_aux, naux ** -0.5)


def solution(mesh):
    in_specs = (
        P(("blk", "aux"), None),
        P(("blk", "aux"), None, None, None),
        P("blk", None),
        P("blk", None),
        P("blk"),
        P(("blk", "aux")),
        P(("blk", "aux"), None),
        P(("blk", "aux")),
    )
    out_specs = (P(("blk", "aux"), None), P(("blk", "aux"), None))
    body = functools.partial(shards, mesh.shape["blk"], mesh.shape["aux"])
    return jax.shard_map(body, mesh=mesh, in_specs=in_specs, out_specs=out_specs, check_vma=False)
```

```python
import functools

import jax
import jax.numpy as jnp
from jax import lax
from jax.experimental import pallas as pl
from jax.experimental.pallas import tpu as pltpu
from jax.sharding import PartitionSpec as P

BS = 32
SUB = 8
CHUNK = 256
MESH = pl.DeviceIdType.MESH
F32 = jnp.float32
BF16 = jnp.bfloat16


def iota(shape, dim):
    return lax.broadcasted_iota(jnp.int32, shape, dim)


def dot(left, right):
    return jnp.dot(left, right, preferred_element_type=F32)


def dot_nt(left, right):
    return lax.dot_general(left, right, (((1,), (1,)), ((), ())), preferred_element_type=F32)


def fold(rows, lanes, row_key, lane_key):
    return (row_key(iota((rows, lanes), 0)) == lane_key(iota((rows, lanes), 1))).astype(BF16)


def exact(mat, folding):
    high = mat.astype(BF16)
    low = (mat - high.astype(F32)).astype(BF16)
    return dot(high, folding) + dot(low, folding)


def minor(index):
    return index % BS


def inner(index):
    return index // (SUB * SUB) * SUB + index % SUB


def outer(index):
    return index // SUB


def fused_kernel(
    n_blk, n_aux, norm,
    sizes_hbm, rows_hbm, owners_hbm, blocks_hbm, adj_hbm, occ_hbm, vir_hbm, t_hbm,
    out_ref,
    sizes, rows, owners, blocks, occ_ref, vir_ref, got, tbuf, cbuf, rbuf, ybuf, vir_acc, vir_send, vir_got, occ_send, occ_got,
    in_sem, t_sem, near_sem, recv_sem, send_sem, trade_sem,
):
    n_dev = n_blk * n_aux
    depth = n_blk // 2
    count, groups, _, _, naux = tbuf.shape
    pairs = BS * BS
    wide = BS * SUB
    own = out_ref.shape[1]
    arows = adj_hbm.shape[0]
    span = naux // depth
    per_plane = n_dev // depth
    b = lax.axis_index("blk")
    a = lax.axis_index("aux")
    z, y, x, c = b // 2, b % 2, a // 2, a % 2
    col, sides, corner, mates = range(4)
    over_x = (b, (1 - x) * 2 + c)
    over_y = (z * 2 + 1 - y, a)
    across = (z * 2 + 1 - y, (1 - x) * 2 + c)
    mate = (b, x * 2 + 1 - c)
    above, below = (b + 2, a), (b - 2, a)
    has_up, has_down = z < depth - 1, z > 0
    inner_plane = has_up & has_down
    me = b * n_aux + a

    def ident(xx, yy, zz, cc):
        return ((zz * 2 + yy) * 2 + xx) * 2 + cc

    barrier = pltpu.get_barrier_semaphore()

    def tell(sem, device):
        pl.semaphore_signal(sem, inc=1, device_id=device, device_id_type=MESH)

    for device in (over_x, over_y, across, mate):
        tell(barrier, device)
    pl.when(has_up)(lambda: tell(barrier, above))
    pl.when(has_down)(lambda: tell(barrier, below))

    pairs_in = (
        (vir_hbm, vir_ref), (sizes_hbm, sizes), (adj_hbm, got.at[me, pl.ds(0, arows)]),
        (rows_hbm, rows), (occ_hbm, occ_ref), (owners_hbm, owners), (blocks_hbm, blocks),
    )
    fetches = [pltpu.make_async_copy(src, dst, in_sem.at[i]) for i, (src, dst) in enumerate(pairs_in)]
    for fetch in fetches:
        fetch.start()

    lane = iota((1, pairs), 1)
    diag = iota((BS, pairs), 1) // BS == iota((BS, pairs), 0)

    def live(size):
        return (lane // BS < size) & (lane % BS < size)

    def pick(all_rows, at):
        return jnp.sum(jnp.where(iota(all_rows.shape, 0) == at, all_rows, 0.0), axis=0, keepdims=True)

    for fetch in fetches:
        fetch.wait()
    for t in range(count):
        for g in range(groups):
            pltpu.make_async_copy(t_hbm.at[t, :, g], tbuf.at[t, g], t_sem.at[t]).start()
    vir_all = vir_ref[...].astype(F32)
    mine = [jnp.where(live(sizes[a * own + r]), pick(vir_all, a * own + r), 0.0) for r in range(own)]
    got[me, arows:, :] = jnp.concatenate(mine, axis=0).astype(BF16)

    pl.semaphore_wait(barrier, 4 + has_up.astype(jnp.int32) + has_down.astype(jnp.int32))

    def send(block, device, kind, zz, part=None):
        ref = got.at[block] if part is None else got.at[block, part]
        pltpu.make_async_remote_copy(
            src_ref=ref,
            dst_ref=ref,
            send_sem=send_sem,
            recv_sem=recv_sem.at[kind, zz],
            device_id=device,
            device_id_type=MESH,
        ).start()

    def arrive(kind, zz, number):
        part = got.at[pl.ds(0, number)]
        pltpu.make_async_copy(part, part, recv_sem.at[kind, zz]).wait()

    def turn(even, odd):
        return tuple(jnp.where(c == 0, i, j) for i, j in zip(even, odd))

    near_one, near_two = turn(over_x, over_y), turn(over_y, over_x)
    send(me, near_one, sides, z)
    send(me, near_two, sides, z)
    pl.when(has_up)(lambda: send(me, above, col, z))
    pl.when(has_down)(lambda: send(me, below, col, z))
    send(me, across, corner, z)
    send(me, mate, mates, z)

    def report(hop):
        pl.when(has_down & (z + hop < depth))(lambda: tell(near_sem.at[0], below))
        pl.when(has_up & (z - hop >= 0))(lambda: tell(near_sem.at[1], above))

    def reach(hop):
        pl.when(z + hop + 1 < depth)(lambda: pl.semaphore_wait(near_sem.at[0], 1))
        pl.when(z - hop - 1 >= 0)(lambda: pl.semaphore_wait(near_sem.at[1], 1))

    def send_far(hop):
        pl.when(z + hop < depth)(lambda: send(me, (b + 2 * hop, a), col, z))
        pl.when(z - hop >= 0)(lambda: send(me, (b - 2 * hop, a), col, z))

    def relay_col(zz):
        block = ident(x, y, zz, c)
        arrive(col, zz, 1)
        pl.when((zz == z - 1) & has_up)(lambda: send(block, above, col, zz))
        pl.when((zz == z + 1) & has_down)(lambda: send(block, below, col, zz))
        send(block, near_one, sides, zz)
        send(block, near_two, sides, zz)
        send(block, across, corner, zz)
        send(block, mate, mates, zz)

    def relay_sides(zz):
        arrive(sides, zz, 2)
        send(ident(1 - x, y, zz, c), mate, mates, zz)
        send(ident(x, 1 - y, zz, c), mate, mates, zz)

    def relay_corner(zz):
        arrive(corner, zz, 1)
        send(ident(1 - x, 1 - y, zz, c), mate, mates, zz)

    def relay_outer(zz):
        pl.when(jnp.logical_not(inner_plane))(lambda: relay_col(zz))

    def ready(zz):
        arrive(mates, zz, 4)

    low = z < depth // 2
    zl = jnp.where(low, z, depth - 1 - z)

    def plane(k):
        near = zl + k // 2 if k % 2 == 0 else zl - (k + 1) // 2
        at = jnp.where(k <= 2 * zl, near, k)
        return jnp.where(low, at, depth - 1 - at)

    order = [plane(k) for k in range(depth)]

    report(1)
    occ_all = occ_ref[...].astype(F32)
    parts = []
    for t in range(count):
        row = jnp.where(live(sizes[rows[t]]), pick(occ_all, rows[t]), 0.0)
        parts.append(jnp.where(diag, row, 0.0))
    square = dot(jnp.concatenate(parts, axis=0).astype(BF16), fold(pairs, wide, minor, outer))
    same_sub = iota((wide, wide), 0) % SUB == iota((wide, wide), 1) % SUB

    def rotate(t):
        spread = jnp.broadcast_to(square[t * BS : (t + 1) * BS][:, None, :], (BS, SUB, wide)).reshape(wide, wide)
        left = jnp.where(same_sub, spread, 0.0).astype(BF16)
        pltpu.make_async_copy(tbuf.at[t], tbuf.at[t], t_sem.at[t]).wait()
        for g in range(groups):
            new = dot(left, tbuf[t, g].reshape(wide, naux)).astype(BF16)
            for zz in range(depth):
                rbuf[t, zz, g] = new[:, zz * span : (zz + 1) * span].reshape(BS, SUB, span)

    def contract(k, t):
        zz = order[k]
        part = got[pl.ds(zz * per_plane, per_plane), :arows, :].reshape(span, naux)
        for first in range(0, groups, groups // 2):
            rows_of = pl.ds(first, groups // 2)
            new = dot_nt(tbuf[t, rows_of].reshape(pairs // 2, naux), part).astype(BF16)
            cbuf[t, zz, rows_of] = new.reshape(groups // 2, BS, SUB, span)

    def column_term(k, t):
        zz = order[k]
        acc = jnp.zeros((wide, wide), F32) if k == 0 else vir_acc[t]
        for at in range(0, BS, SUB):
            left = cbuf[t, zz, :, at : at + SUB].reshape(wide, span)
            acc = acc + dot_nt(left, rbuf[t, zz, :, at : at + SUB].reshape(wide, span))
        return acc

    reach(1)
    report(2)
    rotate(0)
    reach(2)
    rotate(1)
    relay_col(order[1])
    pl.when(inner_plane)(lambda: relay_col(order[2]))
    rotate(2)
    relay_sides(z)
    rotate(3)
    send_far(3)
    relay_corner(z)
    ready(z)
    events = {
        (0, 1): [(relay_sides, 1), (relay_outer, 2), (relay_corner, 1)],
        (1, 0): [(relay_col, 3), (ready, 1)],
        (1, 1): [(relay_sides, 2), (relay_corner, 2)],
        (2, 0): [(ready, 2)],
        (2, 1): [(relay_sides, 3), (relay_corner, 3)],
        (3, 0): [(ready, 3)],
    }
    for k in range(depth):
        for part in range(2):
            for event, which in events.get((k, part), []):
                event(order[which])
            tiles_here = range(part * count // 2, (part + 1) * count // 2)
            for t in tiles_here:
                contract(k, t)
            if k < depth - 1:
                for t in tiles_here:
                    vir_acc[t] = column_term(k, t)

    same_row = iota((SUB, SUB, wide), 0) == iota((SUB, SUB, wide), 2) % (SUB * SUB) // SUB
    lanes_of = iota((SUB, 128), 1) // BS

    def compact(square):
        total = jnp.zeros((SUB, 128), F32)
        for g in range(groups):
            total = jnp.where(lanes_of == g, square[g * SUB : (g + 1) * SUB], total)
        return total

    parts = []
    for t in range(count):
        acc = column_term(depth - 1, t)
        acc = jnp.where(same_row, acc.reshape(groups, SUB, SUB, wide), 0.0)
        parts.append(jnp.sum(acc, axis=1).reshape(BS, wide))
    both = exact(jnp.concatenate(parts, axis=0), fold(wide, 128, inner, minor))
    terms = [compact(both[t * BS : (t + 1) * BS]) for t in range(count)]
    for p in range(n_dev):
        slots = []
        for r in range(own):
            total = jnp.zeros((SUB, 128), F32)
            for t in range(count):
                here = owners[t] * (n_aux * own) + blocks[t] == p * own + r
                total = total + jnp.where(here, terms[t], 0.0)
            slots.append(total)
        vir_send[p] = jnp.concatenate(slots, axis=0).astype(BF16)
    vir_got[me] = vir_send[me]

    def send_vir(k, carry):
        p = lax.rem(me + k, n_dev)
        pltpu.make_async_remote_copy(
            src_ref=vir_send.at[p],
            dst_ref=vir_got.at[me],
            send_sem=trade_sem.at[0],
            recv_sem=trade_sem.at[1],
            device_id=(p // n_aux, p % n_aux),
            device_id_type=MESH,
        ).start()
        return carry

    lax.fori_loop(1, n_dev, send_vir, 0)

    parts = []
    for t in range(count):
        home = owners[t] * n_aux + blocks[t] // own
        row = pick(got[home, arows:, :].astype(F32), blocks[t] % own)
        parts.append(jnp.where(diag, row, 0.0))
    square_v = dot(jnp.concatenate(parts, axis=0).astype(BF16), fold(pairs, wide, minor, inner))
    for t in range(count):
        spread = square_v[t * BS : (t + 1) * BS].reshape(groups, 1, SUB, wide)
        spread = jnp.broadcast_to(spread, (groups, SUB, SUB, wide))
        left = jnp.where(same_row, spread, 0.0).reshape(wide, wide).astype(BF16)
        for at in range(0, BS, SUB):
            new = dot(left, tbuf[t, :, at : at + SUB].reshape(wide, naux)).astype(BF16)
            ybuf[t, :, at : at + SUB] = new.reshape(groups, SUB, SUB, naux)

    parts = []
    for t in range(count):
        acc = jnp.zeros((wide, wide), F32)
        for g in range(groups):
            left = jnp.concatenate([cbuf[t, zz, g].reshape(wide, span) for zz in range(depth)], axis=1)
            acc = acc + dot_nt(left, ybuf[t, g].reshape(wide, naux))
        parts.append(jnp.where(same_sub, acc, 0.0))
    both = exact(jnp.concatenate(parts, axis=0), fold(wide, 128, outer, minor)).reshape(count, groups, SUB, SUB, 128)
    terms = []
    for t in range(count):
        total = jnp.zeros((SUB, SUB, 128), F32)
        for g in range(groups):
            total = jnp.where(lanes_of == g, both[t, g], total)
        terms.append(jnp.sum(total, axis=1))
    for q in range(n_aux):
        slots = []
        for r in range(own):
            total = jnp.zeros((SUB, 128), F32)
            for t in range(count):
                total = total + jnp.where(rows[t] == q * own + r, terms[t], 0.0)
            slots.append(total)
        occ_send[q] = jnp.concatenate(slots, axis=0)
    occ_got[a] = occ_send[a]
    for k in range(1, n_aux):
        q = lax.rem(a + k, n_aux)
        pltpu.make_async_remote_copy(
            src_ref=occ_send.at[q],
            dst_ref=occ_got.at[a],
            send_sem=trade_sem.at[2],
            recv_sem=trade_sem.at[3],
            device_id=(b, q),
            device_id_type=MESH,
        ).start()

    def done(ref, sem):
        pltpu.make_async_copy(ref, ref, sem).wait()

    done(vir_got.at[pl.ds(0, n_dev - 1)], trade_sem.at[1])
    vir_sum = jnp.sum(vir_got[...].astype(F32), axis=0)
    done(occ_got.at[pl.ds(0, n_aux - 1)], trade_sem.at[3])
    occ_sum = jnp.sum(occ_got[...], axis=0)

    sums = jnp.concatenate([occ_sum, vir_sum], axis=0)
    lanes_all = iota(sums.shape, 1) // BS
    parts = [jnp.where(lanes_all == g, sums, 0.0) for g in range(groups)]
    both = exact(jnp.concatenate(parts, axis=0), fold(128, 128, minor, minor))
    both = both.reshape(groups, 2 * own, SUB, 128)
    per_tile = 128 // BS
    lines = []
    for m in range(pairs // 128):
        first = m * per_tile
        here = iota((SUB, 128), 0) == first % SUB + lanes_of
        lines.append(jnp.sum(jnp.where(here, both[first // SUB], 0.0), axis=1))
    flat = jnp.concatenate(lines, axis=1)
    for r in range(own):
        scale = jnp.where(live(sizes[a * own + r]), norm, 0.0).astype(F32)
        out_ref[0, r : r + 1, :] = flat[r : r + 1, :] * scale
        out_ref[1, r : r + 1, :] = flat[own + r : own + r + 1, :] * scale

    done(vir_send.at[pl.ds(0, n_dev - 1)], trade_sem.at[0])
    done(occ_send.at[pl.ds(0, n_aux - 1)], trade_sem.at[2])
    pl.when(inner_plane)(lambda: done(got.at[pl.ds(0, 7 * depth + 4)], send_sem))
    pl.when(jnp.logical_not(inner_plane))(lambda: done(got.at[pl.ds(0, 7 * depth + 2)], send_sem))


def fused(sizes, rows, owners, blocks, adj, occ, vir, three, n_blk, n_aux, norm):
    n_dev = n_blk * n_aux
    count, naux = three.shape[0], three.shape[3]
    own = occ.shape[0] // n_aux
    groups = BS // SUB
    vmem = pl.BlockSpec(memory_space=pltpu.VMEM)
    hbm = pl.BlockSpec(memory_space=pl.ANY)
    tile = pltpu.VMEM((count, groups, BS, SUB, naux), BF16)
    by_plane = pltpu.VMEM((count, n_blk // 2, groups, BS, SUB, naux // (n_blk // 2)), BF16)
    return pl.pallas_call(
        functools.partial(fused_kernel, n_blk, n_aux, norm),
        out_shape=jax.ShapeDtypeStruct((2, own, BS * BS), F32),
        in_specs=[hbm] * 8,
        out_specs=vmem,
        scratch_shapes=[
            *(pltpu.SMEM(scalars.shape, scalars.dtype) for scalars in (sizes, rows, owners, blocks)),
            pltpu.VMEM(occ.shape, BF16),
            pltpu.VMEM(vir.shape, BF16),
            pltpu.VMEM((n_dev, adj.shape[0] + own, naux), BF16),
            tile,
            by_plane,
            by_plane,
            tile,
            pltpu.VMEM((count, BS * SUB, BS * SUB), F32),
            pltpu.VMEM((n_dev, own * SUB, 128), BF16),
            pltpu.VMEM((n_dev, own * SUB, 128), BF16),
            pltpu.VMEM((n_aux, own * SUB, 128), F32),
            pltpu.VMEM((n_aux, own * SUB, 128), F32),
            pltpu.SemaphoreType.DMA((7,)),
            pltpu.SemaphoreType.DMA((count,)),
            pltpu.SemaphoreType.REGULAR((2,)),
            pltpu.SemaphoreType.DMA((4, n_blk // 2)),
            pltpu.SemaphoreType.DMA,
            pltpu.SemaphoreType.DMA((4,)),
        ],
        compiler_params=pltpu.CompilerParams(
            collective_id=0, has_side_effects=True, vmem_limit_bytes=67043328
        ),
        name="fused",
    )(sizes, rows, owners, blocks, adj, occ, vir, three.reshape(count, BS, groups, SUB, naux))


def tile_kernel(
    n_aux, own, sizes, rows, owners, blocks, occ_ref, vir_ref, adj_ref, t_ref, occ_out, vir_out, vir_acc
):
    t = pl.program_id(0)
    pairs = BS * BS
    naux = adj_ref.shape[0]

    @pl.when(t == 0)
    def _():
        occ_out[...] = jnp.zeros_like(occ_out)
        vir_acc[...] = jnp.zeros_like(vir_acc)

    row, owner, block = rows[t], owners[t], blocks[t]
    size = sizes[row]
    lane = iota((1, pairs), 1)
    inside = (lane // BS < size) & (lane % BS < size)
    occ_all = occ_ref[...].astype(F32)
    occ_row = jnp.sum(jnp.where(iota(occ_all.shape, 0) == row, occ_all, 0.0), axis=0, keepdims=True)
    occ_row = jnp.where(inside, occ_row, 0.0)
    home = owner * n_aux + block // own
    vir_all = vir_ref[home].astype(F32)
    vir_row = jnp.sum(jnp.where(iota(vir_all.shape, 0) == block % own, vir_all, 0.0), axis=0, keepdims=True)
    diag = iota((BS, pairs), 1) // BS == iota((BS, pairs), 0)
    fold_minor = (iota((pairs, 128), 0) % BS == iota((pairs, 128), 1) % BS).astype(BF16)
    fold_major = (iota((pairs, 128), 0) // BS == iota((pairs, 128), 1) % BS).astype(BF16)
    spread = (iota((128, pairs), 0) == iota((128, pairs), 1) // BS).astype(BF16)
    repeat = pairs // 128

    def square(flat):
        return jnp.dot(jnp.where(diag, flat, 0.0).astype(BF16), fold_minor, preferred_element_type=F32)

    occ_rep = jnp.dot(square(occ_row).astype(BF16), spread, preferred_element_type=F32)
    vir_rep = jnp.concatenate([square(vir_row)] * repeat, axis=1)

    nt = (((1,), (1,)), ((), ()))
    acc = jnp.zeros((BS, pairs), F32)
    lines = []
    for first in range(0, pairs, CHUNK):
        part = lax.dot_general(t_ref[0, first : first + CHUNK, :], adj_ref[...], nt, preferred_element_type=F32)
        gram = lax.dot_general(part.astype(BF16), t_ref[0], nt, preferred_element_type=F32)
        for at in range(CHUNK // BS):
            i = first // BS + at
            block_i = gram[at * BS : (at + 1) * BS, :]
            acc = acc + block_i * occ_rep[i : i + 1, :]
            lines.append(jnp.sum(block_i * vir_rep, axis=0, keepdims=True))
    zmat = jnp.concatenate(lines, axis=0)

    def flatten(mat, fold):
        high = mat.astype(BF16)
        low = (mat - high.astype(F32)).astype(BF16)
        both = jnp.dot(high, fold, preferred_element_type=F32) + jnp.dot(low, fold, preferred_element_type=F32)
        wide = jnp.concatenate([both] * repeat, axis=1)
        return jnp.sum(jnp.where(diag, wide, 0.0), axis=0, keepdims=True)

    occ_flat = flatten(zmat, fold_major)
    vir_flat = flatten(acc, fold_minor)
    slot = iota((own, pairs), 0)
    occ_out[row // own] = occ_out[row // own] + jnp.where(slot == row % own, occ_flat, 0.0)
    vir_acc[home] = vir_acc[home] + jnp.where(slot == block % own, vir_flat, 0.0)

    @pl.when(t == pl.num_programs(0) - 1)
    def _():
        vir_out[...] = vir_acc[...].astype(vir_out.dtype)


def tiles(sizes, rows, owners, blocks, occ, vir, adj, three, n_dev, n_aux):
    count, pairs, naux = three.shape
    own = occ.shape[0] // n_aux
    smem = pl.BlockSpec(memory_space=pltpu.SMEM)
    vmem = pl.BlockSpec(memory_space=pltpu.VMEM)
    return pl.pallas_call(
        functools.partial(tile_kernel, n_aux, own),
        grid=(count,),
        out_shape=(
            jax.ShapeDtypeStruct((n_aux, own, pairs), F32),
            jax.ShapeDtypeStruct((n_dev, own, pairs), BF16),
        ),
        in_specs=[smem] * 4 + [vmem] * 3 + [pl.BlockSpec((1, pairs, naux), lambda t: (t, 0, 0))],
        out_specs=(vmem, vmem),
        scratch_shapes=[pltpu.VMEM((n_dev, own, pairs), F32)],
        compiler_params=pltpu.CompilerParams(vmem_limit_bytes=48 * 1024 * 1024),
        name="tiles",
    )(sizes, rows, owners, blocks, occ, vir, adj, three)


def exchange_kernel(
    n_blk, n_aux, norm, sizes, occ_ref, vir_ref, occ_out, vir_out, occ_got, vir_got, occ_sems, vir_sems
):
    n_dev = n_blk * n_aux
    b = lax.axis_index("blk")
    a = lax.axis_index("aux")
    me = b * n_aux + a
    barrier = pltpu.get_barrier_semaphore()

    def greet(k, carry):
        p = lax.rem(me + k, n_dev)
        pl.semaphore_signal(barrier, inc=1, device_id=(p // n_aux, p % n_aux), device_id_type=MESH)
        return carry

    lax.fori_loop(1, n_dev, greet, 0)
    pl.semaphore_wait(barrier, n_dev - 1)

    trade(n_blk, n_aux, norm, sizes, occ_ref, vir_ref, occ_out, vir_out, occ_got, vir_got, occ_sems, vir_sems)


def trade(n_blk, n_aux, norm, sizes, occ_ref, vir_ref, occ_out, vir_out, occ_got, vir_got, occ_sems, vir_sems):
    n_dev = n_blk * n_aux
    b = lax.axis_index("blk")
    a = lax.axis_index("aux")
    me = b * n_aux + a
    own, pairs = occ_out.shape

    def vir_copy(k, source):
        p = lax.rem(me + k, n_dev)
        return pltpu.make_async_remote_copy(
            src_ref=vir_ref.at[p],
            dst_ref=vir_got.at[source],
            send_sem=vir_sems.at[0, k],
            recv_sem=vir_sems.at[1, source],
            device_id=(p // n_aux, p % n_aux),
            device_id_type=MESH,
        )

    def occ_copy(k, source):
        q = lax.rem(a + k, n_aux)
        return pltpu.make_async_remote_copy(
            src_ref=occ_ref.at[q],
            dst_ref=occ_got.at[source],
            send_sem=occ_sems.at[0, k],
            recv_sem=occ_sems.at[1, source],
            device_id=(b, q),
            device_id_type=MESH,
        )

    def start_vir(k, carry):
        vir_copy(k, me).start()
        return carry

    def start_occ(k, carry):
        occ_copy(k, a).start()
        return carry

    lax.fori_loop(1, n_dev, start_vir, 0)
    lax.fori_loop(1, n_aux, start_occ, 0)

    def take_vir(k, total):
        source = lax.rem(me + k, n_dev)
        vir_copy(k, source).wait_recv()
        return total + vir_got[source].astype(F32)

    def take_occ(k, total):
        source = lax.rem(a + k, n_aux)
        occ_copy(k, source).wait_recv()
        return total + occ_got[source]

    occ_sum = lax.fori_loop(1, n_aux, take_occ, occ_ref[a])
    vir_sum = lax.fori_loop(1, n_dev, take_vir, vir_ref[me].astype(F32))
    lane = iota((1, pairs), 1)
    for r in range(own):
        size = sizes[a * own + r]
        scale = jnp.where((lane // BS < size) & (lane % BS < size), norm, 0.0).astype(F32)
        occ_out[r : r + 1, :] = occ_sum[r : r + 1, :] * scale
        vir_out[r : r + 1, :] = vir_sum[r : r + 1, :] * scale

    def end_vir(k, carry):
        vir_copy(k, me).wait_send()
        return carry

    def end_occ(k, carry):
        occ_copy(k, a).wait_send()
        return carry

    lax.fori_loop(1, n_dev, end_vir, 0)
    lax.fori_loop(1, n_aux, end_occ, 0)


def exchange(sizes, occ, vir, n_blk, n_aux, norm):
    n_dev, own, pairs = vir.shape
    vmem = pl.BlockSpec(memory_space=pltpu.VMEM)
    out = jax.ShapeDtypeStruct((own, pairs), F32)
    return pl.pallas_call(
        functools.partial(exchange_kernel, n_blk, n_aux, norm),
        out_shape=(out, out),
        in_specs=[pl.BlockSpec(memory_space=pltpu.SMEM), vmem, vmem],
        out_specs=(vmem, vmem),
        scratch_shapes=[
            pltpu.VMEM(occ.shape, occ.dtype),
            pltpu.VMEM(vir.shape, vir.dtype),
            pltpu.SemaphoreType.DMA((2, n_aux)),
            pltpu.SemaphoreType.DMA((2, n_dev)),
        ],
        compiler_params=pltpu.CompilerParams(collective_id=1, has_side_effects=True),
        name="exchange",
    )(sizes, occ, vir)


def shards(
    n_blk, n_aux, adjoint, three_centre, occ_density, vir_density, block_sizes, tile_rows, col_owner, col_block
):
    n_dev = n_blk * n_aux
    count = three_centre.shape[0]
    naux = three_centre.shape[3]
    own = occ_density.shape[0] // n_aux
    depth = adjoint.shape[0]
    three = three_centre.reshape(count, BS * BS, naux)
    if n_aux == 4 and n_blk == 8:
        both = fused(
            block_sizes, tile_rows, col_owner.reshape(count), col_block, adjoint, occ_density, vir_density,
            three_centre, n_blk, n_aux, naux ** -0.5,
        )
        return both[0], both[1]
    aux_here = lax.axis_index("aux")
    own_sizes = lax.dynamic_slice_in_dim(block_sizes, aux_here * own, own, 0)
    own_vir = lax.dynamic_slice_in_dim(vir_density, aux_here * own, own, 0)
    lane = jnp.arange(BS * BS, dtype=jnp.int32)[None, :]
    inside = (lane // BS < own_sizes[:, None]) & (lane % BS < own_sizes[:, None])
    own_vir = jnp.where(inside, own_vir, jnp.zeros_like(own_vir))
    got = lax.all_gather(jnp.concatenate((adjoint, own_vir), axis=0), ("blk", "aux"), axis=0)
    adj = got[:, :depth, :].reshape(naux, naux)
    vir = got[:, depth:, :]
    occ_terms, vir_terms = tiles(
        block_sizes, tile_rows, col_owner.reshape(count), col_block, occ_density, vir, adj,
        three, n_dev, n_aux,
    )
    return exchange(block_sizes, occ_terms, vir_terms, n_blk, n_aux, naux ** -0.5)


def solution(mesh):
    in_specs = (
        P(("blk", "aux"), None),
        P(("blk", "aux"), None, None, None),
        P("blk", None),
        P("blk", None),
        P("blk"),
        P(("blk", "aux")),
        P(("blk", "aux"), None),
        P(("blk", "aux")),
    )
    out_specs = (P(("blk", "aux"), None), P(("blk", "aux"), None))
    body = functools.partial(shards, mesh.shape["blk"], mesh.shape["aux"])
    return jax.shard_map(body, mesh=mesh, in_specs=in_specs, out_specs=out_specs, check_vma=False)
```

```python
import functools

import jax
import jax.numpy as jnp
from jax import lax
from jax.experimental import pallas as pl
from jax.experimental.pallas import tpu as pltpu
from jax.sharding import PartitionSpec as P

BS = 32
SUB = 8
CHUNK = 256
MESH = pl.DeviceIdType.MESH
F32 = jnp.float32
BF16 = jnp.bfloat16


def iota(shape, dim):
    return lax.broadcasted_iota(jnp.int32, shape, dim)


def dot(left, right):
    return jnp.dot(left, right, preferred_element_type=F32)


def dot_nt(left, right):
    return lax.dot_general(left, right, (((1,), (1,)), ((), ())), preferred_element_type=F32)


def fold(rows, lanes, row_key, lane_key):
    return (row_key(iota((rows, lanes), 0)) == lane_key(iota((rows, lanes), 1))).astype(BF16)


def exact(mat, folding):
    high = mat.astype(BF16)
    low = (mat - high.astype(F32)).astype(BF16)
    return dot(high, folding) + dot(low, folding)


def minor(index):
    return index % BS


def inner(index):
    return index // (SUB * SUB) * SUB + index % SUB


def outer(index):
    return index // SUB


def fused_kernel(
    n_blk, n_aux, norm,
    sizes_hbm, rows_hbm, owners_hbm, blocks_hbm, adj_hbm, occ_hbm, vir_hbm, t_hbm,
    out_ref,
    sizes, rows, owners, blocks, occ_ref, vir_ref, got, tbuf, cbuf, rbuf, ybuf, vir_acc, vir_send, vir_got, occ_send, occ_got,
    in_sem, t_sem, near_sem, recv_sem, send_sem, trade_sem,
):
    n_dev = n_blk * n_aux
    depth = n_blk // 2
    count, groups, _, _, naux = tbuf.shape
    pairs = BS * BS
    wide = BS * SUB
    own = out_ref.shape[1]
    arows = adj_hbm.shape[0]
    span = naux // depth
    per_plane = n_dev // depth
    b = lax.axis_index("blk")
    a = lax.axis_index("aux")
    z, y, x, c = b // 2, b % 2, a // 2, a % 2
    col, sides, corner, mates = range(4)
    over_x = (b, (1 - x) * 2 + c)
    over_y = (z * 2 + 1 - y, a)
    across = (z * 2 + 1 - y, (1 - x) * 2 + c)
    mate = (b, x * 2 + 1 - c)
    above, below = (b + 2, a), (b - 2, a)
    has_up, has_down = z < depth - 1, z > 0
    inner_plane = has_up & has_down
    me = b * n_aux + a

    def ident(xx, yy, zz, cc):
        return ((zz * 2 + yy) * 2 + xx) * 2 + cc

    barrier = pltpu.get_barrier_semaphore()

    def tell(sem, device):
        pl.semaphore_signal(sem, inc=1, device_id=device, device_id_type=MESH)

    for device in (over_x, over_y, across, mate):
        tell(barrier, device)
    pl.when(has_up)(lambda: tell(barrier, above))
    pl.when(has_down)(lambda: tell(barrier, below))

    pairs_in = (
        (vir_hbm, vir_ref), (sizes_hbm, sizes), (adj_hbm, got.at[me, pl.ds(0, arows)]),
        (rows_hbm, rows), (occ_hbm, occ_ref), (owners_hbm, owners), (blocks_hbm, blocks),
    )
    fetches = [pltpu.make_async_copy(src, dst, in_sem.at[i]) for i, (src, dst) in enumerate(pairs_in)]
    for fetch in fetches:
        fetch.start()

    lane = iota((1, pairs), 1)
    diag = iota((BS, pairs), 1) // BS == iota((BS, pairs), 0)

    def live(size):
        return (lane // BS < size) & (lane % BS < size)

    def pick(all_rows, at):
        return jnp.sum(jnp.where(iota(all_rows.shape, 0) == at, all_rows, 0.0), axis=0, keepdims=True)

    for fetch in fetches:
        fetch.wait()
    for t in range(count):
        for g in range(groups):
            pltpu.make_async_copy(t_hbm.at[t, :, g], tbuf.at[t, g], t_sem.at[t]).start()
    vir_all = vir_ref[...].astype(F32)
    mine = [jnp.where(live(sizes[a * own + r]), pick(vir_all, a * own + r), 0.0) for r in range(own)]
    got[me, arows:, :] = jnp.concatenate(mine, axis=0).astype(BF16)

    pl.semaphore_wait(barrier, 4 + has_up.astype(jnp.int32) + has_down.astype(jnp.int32))

    def send(block, device, kind, zz):
        ref = got.at[block]
        pltpu.make_async_remote_copy(
            src_ref=ref,
            dst_ref=ref,
            send_sem=send_sem,
            recv_sem=recv_sem.at[kind, zz],
            device_id=device,
            device_id_type=MESH,
        ).start()

    def arrive(kind, zz, number):
        part = got.at[pl.ds(0, number)]
        pltpu.make_async_copy(part, part, recv_sem.at[kind, zz]).wait()

    def turn(even, odd):
        return tuple(jnp.where(c == 0, i, j) for i, j in zip(even, odd))

    near_one, near_two = turn(over_x, over_y), turn(over_y, over_x)
    send(me, across, corner, z)
    send(me, near_one, sides, z)
    send(me, near_two, sides, z)
    pl.when(has_up)(lambda: send(me, above, col, z))
    pl.when(has_down)(lambda: send(me, below, col, z))
    send(me, mate, mates, z)

    def report(hop):
        pl.when(has_down & (z + hop < depth))(lambda: tell(near_sem.at[0], below))
        pl.when(has_up & (z - hop >= 0))(lambda: tell(near_sem.at[1], above))

    def reach(hop):
        pl.when(z + hop + 1 < depth)(lambda: pl.semaphore_wait(near_sem.at[0], 1))
        pl.when(z - hop - 1 >= 0)(lambda: pl.semaphore_wait(near_sem.at[1], 1))

    def send_far(hop):
        pl.when(z + hop < depth)(lambda: send(me, (b + 2 * hop, a), col, z))
        pl.when(z - hop >= 0)(lambda: send(me, (b - 2 * hop, a), col, z))

    def relay_col(zz):
        block = ident(x, y, zz, c)
        arrive(col, zz, 1)
        pl.when((zz == z - 1) & has_up)(lambda: send(block, above, col, zz))
        pl.when((zz == z + 1) & has_down)(lambda: send(block, below, col, zz))
        send(block, across, corner, zz)
        send(block, near_one, sides, zz)
        send(block, near_two, sides, zz)
        send(block, mate, mates, zz)

    def relay_sides(zz):
        arrive(sides, zz, 2)
        send(ident(1 - x, y, zz, c), mate, mates, zz)
        send(ident(x, 1 - y, zz, c), mate, mates, zz)

    def relay_corner(zz):
        arrive(corner, zz, 1)
        send(ident(1 - x, 1 - y, zz, c), mate, mates, zz)

    def relay_outer(zz):
        pl.when(jnp.logical_not(inner_plane))(lambda: relay_col(zz))

    def ready(zz):
        arrive(mates, zz, 4)

    low = z < depth // 2
    zl = jnp.where(low, z, depth - 1 - z)

    def plane(k):
        near = zl + k // 2 if k % 2 == 0 else zl - (k + 1) // 2
        at = jnp.where(k <= 2 * zl, near, k)
        return jnp.where(low, at, depth - 1 - at)

    order = [plane(k) for k in range(depth)]

    report(1)
    occ_all = occ_ref[...].astype(F32)
    parts = []
    for t in range(count):
        row = jnp.where(live(sizes[rows[t]]), pick(occ_all, rows[t]), 0.0)
        parts.append(jnp.where(diag, row, 0.0))
    square = dot(jnp.concatenate(parts, axis=0).astype(BF16), fold(pairs, wide, minor, outer))
    same_sub = iota((wide, wide), 0) % SUB == iota((wide, wide), 1) % SUB

    def rotate(t):
        spread = jnp.broadcast_to(square[t * BS : (t + 1) * BS][:, None, :], (BS, SUB, wide)).reshape(wide, wide)
        left = jnp.where(same_sub, spread, 0.0).astype(BF16)
        pltpu.make_async_copy(tbuf.at[t], tbuf.at[t], t_sem.at[t]).wait()
        for g in range(groups):
            new = dot(left, tbuf[t, g].reshape(wide, naux)).astype(BF16)
            for zz in range(depth):
                rbuf[t, zz, g] = new[:, zz * span : (zz + 1) * span].reshape(BS, SUB, span)

    def contract(k, t):
        zz = order[k]
        part = got[pl.ds(zz * per_plane, per_plane), :arows, :].reshape(span, naux)
        for first in range(0, groups, groups // 2):
            rows_of = pl.ds(first, groups // 2)
            new = dot_nt(tbuf[t, rows_of].reshape(pairs // 2, naux), part).astype(BF16)
            cbuf[t, zz, rows_of] = new.reshape(groups // 2, BS, SUB, span)

    def column_term(k, t):
        zz = order[k]
        acc = jnp.zeros((wide, wide), F32) if k == 0 else vir_acc[t]
        for at in range(0, BS, SUB):
            left = cbuf[t, zz, :, at : at + SUB].reshape(wide, span)
            acc = acc + dot_nt(left, rbuf[t, zz, :, at : at + SUB].reshape(wide, span))
        return acc

    reach(1)
    report(2)
    rotate(0)
    reach(2)
    rotate(1)
    relay_col(order[1])
    pl.when(inner_plane)(lambda: relay_col(order[2]))
    send_far(3)
    rotate(2)
    relay_sides(z)
    rotate(3)
    relay_corner(z)
    ready(z)
    events = {
        (0, 1): [(relay_sides, 1), (relay_outer, 2), (relay_corner, 1)],
        (1, 0): [(relay_col, 3), (ready, 1)],
        (1, 1): [(relay_sides, 2), (relay_corner, 2)],
        (2, 0): [(ready, 2)],
        (2, 1): [(relay_sides, 3), (relay_corner, 3)],
        (3, 0): [(ready, 3)],
    }
    for k in range(depth):
        for part in range(2):
            for event, which in events.get((k, part), []):
                event(order[which])
            tiles_here = range(part * count // 2, (part + 1) * count // 2)
            for t in tiles_here:
                contract(k, t)
            if k < depth - 1:
                for t in tiles_here:
                    vir_acc[t] = column_term(k, t)

    same_row = iota((SUB, SUB, wide), 0) == iota((SUB, SUB, wide), 2) % (SUB * SUB) // SUB
    lanes_of = iota((SUB, 128), 1) // BS

    def compact(square):
        total = jnp.zeros((SUB, 128), F32)
        for g in range(groups):
            total = jnp.where(lanes_of == g, square[g * SUB : (g + 1) * SUB], total)
        return total

    parts = []
    for t in range(count):
        acc = column_term(depth - 1, t)
        acc = jnp.where(same_row, acc.reshape(groups, SUB, SUB, wide), 0.0)
        parts.append(jnp.sum(acc, axis=1).reshape(BS, wide))
    both = exact(jnp.concatenate(parts, axis=0), fold(wide, 128, inner, minor))
    terms = [compact(both[t * BS : (t + 1) * BS]) for t in range(count)]
    for p in range(n_dev):
        slots = []
        for r in range(own):
            total = jnp.zeros((SUB, 128), F32)
            for t in range(count):
                here = owners[t] * (n_aux * own) + blocks[t] == p * own + r
                total = total + jnp.where(here, terms[t], 0.0)
            slots.append(total)
        vir_send[p] = jnp.concatenate(slots, axis=0).astype(BF16)
    vir_got[me] = vir_send[me]

    def send_vir(k):
        p = lax.rem(me + k, n_dev)
        pltpu.make_async_remote_copy(
            src_ref=vir_send.at[p],
            dst_ref=vir_got.at[me],
            send_sem=trade_sem.at[0],
            recv_sem=trade_sem.at[1],
            device_id=(p // n_aux, p % n_aux),
            device_id_type=MESH,
        ).start()

    parts = []
    for t in range(count):
        home = owners[t] * n_aux + blocks[t] // own
        row = pick(got[home, arows:, :].astype(F32), blocks[t] % own)
        parts.append(jnp.where(diag, row, 0.0))
    square_v = dot(jnp.concatenate(parts, axis=0).astype(BF16), fold(pairs, wide, minor, inner))
    for t in range(count):
        spread = square_v[t * BS : (t + 1) * BS].reshape(groups, 1, SUB, wide)
        spread = jnp.broadcast_to(spread, (groups, SUB, SUB, wide))
        left = jnp.where(same_row, spread, 0.0).reshape(wide, wide).astype(BF16)
        for k in range(max(1, t * n_dev // count), (t + 1) * n_dev // count):
            send_vir(k)
        for at in range(0, BS, SUB):
            new = dot(left, tbuf[t, :, at : at + SUB].reshape(wide, naux)).astype(BF16)
            ybuf[t, :, at : at + SUB] = new.reshape(groups, SUB, SUB, naux)

    parts = []
    for t in range(count):
        acc = jnp.zeros((wide, wide), F32)
        for g in range(groups):
            left = jnp.concatenate([cbuf[t, zz, g].reshape(wide, span) for zz in range(depth)], axis=1)
            acc = acc + dot_nt(left, ybuf[t, g].reshape(wide, naux))
        parts.append(jnp.where(same_sub, acc, 0.0))
    both = exact(jnp.concatenate(parts, axis=0), fold(wide, 128, outer, minor)).reshape(count, groups, SUB, SUB, 128)
    terms = []
    for t in range(count):
        total = jnp.zeros((SUB, SUB, 128), F32)
        for g in range(groups):
            total = jnp.where(lanes_of == g, both[t, g], total)
        terms.append(jnp.sum(total, axis=1))
    for q in range(n_aux):
        slots = []
        for r in range(own):
            total = jnp.zeros((SUB, 128), F32)
            for t in range(count):
                total = total + jnp.where(rows[t] == q * own + r, terms[t], 0.0)
            slots.append(total)
        occ_send[q] = jnp.concatenate(slots, axis=0)
    occ_got[a] = occ_send[a]
    for k in range(1, n_aux):
        q = lax.rem(a + k, n_aux)
        pltpu.make_async_remote_copy(
            src_ref=occ_send.at[q],
            dst_ref=occ_got.at[a],
            send_sem=trade_sem.at[2],
            recv_sem=trade_sem.at[3],
            device_id=(b, q),
            device_id_type=MESH,
        ).start()

    def done(ref, sem):
        pltpu.make_async_copy(ref, ref, sem).wait()

    done(vir_got.at[pl.ds(0, n_dev - 1)], trade_sem.at[1])
    vir_sum = jnp.sum(vir_got[...].astype(F32), axis=0)
    done(occ_got.at[pl.ds(0, n_aux - 1)], trade_sem.at[3])
    occ_sum = jnp.sum(occ_got[...], axis=0)

    sums = jnp.concatenate([occ_sum, vir_sum], axis=0)
    lanes_all = iota(sums.shape, 1) // BS
    parts = [jnp.where(lanes_all == g, sums, 0.0) for g in range(groups)]
    both = exact(jnp.concatenate(parts, axis=0), fold(128, 128, minor, minor))
    both = both.reshape(groups, 2 * own, SUB, 128)
    per_tile = 128 // BS
    lines = []
    for m in range(pairs // 128):
        first = m * per_tile
        here = iota((SUB, 128), 0) == first % SUB + lanes_of
        lines.append(jnp.sum(jnp.where(here, both[first // SUB], 0.0), axis=1))
    flat = jnp.concatenate(lines, axis=1)
    for r in range(own):
        scale = jnp.where(live(sizes[a * own + r]), norm, 0.0).astype(F32)
        out_ref[0, r : r + 1, :] = flat[r : r + 1, :] * scale
        out_ref[1, r : r + 1, :] = flat[own + r : own + r + 1, :] * scale

    done(vir_send.at[pl.ds(0, n_dev - 1)], trade_sem.at[0])
    done(occ_send.at[pl.ds(0, n_aux - 1)], trade_sem.at[2])
    pl.when(inner_plane)(lambda: done(got.at[pl.ds(0, 7 * depth + 4)], send_sem))
    pl.when(jnp.logical_not(inner_plane))(lambda: done(got.at[pl.ds(0, 7 * depth + 2)], send_sem))


def fused(sizes, rows, owners, blocks, adj, occ, vir, three, n_blk, n_aux, norm):
    n_dev = n_blk * n_aux
    count, naux = three.shape[0], three.shape[3]
    own = occ.shape[0] // n_aux
    groups = BS // SUB
    vmem = pl.BlockSpec(memory_space=pltpu.VMEM)
    hbm = pl.BlockSpec(memory_space=pltpu.HBM)
    tile = pltpu.VMEM((count, groups, BS, SUB, naux), BF16)
    by_plane = pltpu.VMEM((count, n_blk // 2, groups, BS, SUB, naux // (n_blk // 2)), BF16)
    return pl.pallas_call(
        functools.partial(fused_kernel, n_blk, n_aux, norm),
        out_shape=pltpu.VMEM((2, own, BS * BS), F32),
        in_specs=[hbm] * 8,
        out_specs=vmem,
        scratch_shapes=[
            *(pltpu.SMEM(scalars.shape, scalars.dtype) for scalars in (sizes, rows, owners, blocks)),
            pltpu.VMEM(occ.shape, BF16),
            pltpu.VMEM(vir.shape, BF16),
            pltpu.VMEM((n_dev, adj.shape[0] + own, naux), BF16),
            tile,
            by_plane,
            by_plane,
            tile,
            pltpu.VMEM((count, BS * SUB, BS * SUB), F32),
            pltpu.VMEM((n_dev, own * SUB, 128), BF16),
            pltpu.VMEM((n_dev, own * SUB, 128), BF16),
            pltpu.VMEM((n_aux, own * SUB, 128), F32),
            pltpu.VMEM((n_aux, own * SUB, 128), F32),
            pltpu.SemaphoreType.DMA((7,)),
            pltpu.SemaphoreType.DMA((count,)),
            pltpu.SemaphoreType.REGULAR((2,)),
            pltpu.SemaphoreType.DMA((4, n_blk // 2)),
            pltpu.SemaphoreType.DMA,
            pltpu.SemaphoreType.DMA((4,)),
        ],
        compiler_params=pltpu.CompilerParams(
            collective_id=0, has_side_effects=True, vmem_limit_bytes=60 << 20
        ),
        name="fused",
    )(sizes, rows, owners, blocks, adj, occ, vir, three.reshape(count, BS, groups, SUB, naux))


def tile_kernel(
    n_aux, own, sizes, rows, owners, blocks, occ_ref, vir_ref, adj_ref, t_ref, occ_out, vir_out, vir_acc
):
    t = pl.program_id(0)
    pairs = BS * BS
    naux = adj_ref.shape[0]

    @pl.when(t == 0)
    def _():
        occ_out[...] = jnp.zeros_like(occ_out)
        vir_acc[...] = jnp.zeros_like(vir_acc)

    row, owner, block = rows[t], owners[t], blocks[t]
    size = sizes[row]
    lane = iota((1, pairs), 1)
    inside = (lane // BS < size) & (lane % BS < size)
    occ_all = occ_ref[...].astype(F32)
    occ_row = jnp.sum(jnp.where(iota(occ_all.shape, 0) == row, occ_all, 0.0), axis=0, keepdims=True)
    occ_row = jnp.where(inside, occ_row, 0.0)
    home = owner * n_aux + block // own
    vir_all = vir_ref[home].astype(F32)
    vir_row = jnp.sum(jnp.where(iota(vir_all.shape, 0) == block % own, vir_all, 0.0), axis=0, keepdims=True)
    diag = iota((BS, pairs), 1) // BS == iota((BS, pairs), 0)
    fold_minor = (iota((pairs, 128), 0) % BS == iota((pairs, 128), 1) % BS).astype(BF16)
    fold_major = (iota((pairs, 128), 0) // BS == iota((pairs, 128), 1) % BS).astype(BF16)
    spread = (iota((128, pairs), 0) == iota((128, pairs), 1) // BS).astype(BF16)
    repeat = pairs // 128

    def square(flat):
        return jnp.dot(jnp.where(diag, flat, 0.0).astype(BF16), fold_minor, preferred_element_type=F32)

    occ_rep = jnp.dot(square(occ_row).astype(BF16), spread, preferred_element_type=F32)
    vir_rep = jnp.concatenate([square(vir_row)] * repeat, axis=1)

    nt = (((1,), (1,)), ((), ()))
    acc = jnp.zeros((BS, pairs), F32)
    lines = []
    for first in range(0, pairs, CHUNK):
        part = lax.dot_general(t_ref[0, first : first + CHUNK, :], adj_ref[...], nt, preferred_element_type=F32)
        gram = lax.dot_general(part.astype(BF16), t_ref[0], nt, preferred_element_type=F32)
        for at in range(CHUNK // BS):
            i = first // BS + at
            block_i = gram[at * BS : (at + 1) * BS, :]
            acc = acc + block_i * occ_rep[i : i + 1, :]
            lines.append(jnp.sum(block_i * vir_rep, axis=0, keepdims=True))
    zmat = jnp.concatenate(lines, axis=0)

    def flatten(mat, fold):
        high = mat.astype(BF16)
        low = (mat - high.astype(F32)).astype(BF16)
        both = jnp.dot(high, fold, preferred_element_type=F32) + jnp.dot(low, fold, preferred_element_type=F32)
        wide = jnp.concatenate([both] * repeat, axis=1)
        return jnp.sum(jnp.where(diag, wide, 0.0), axis=0, keepdims=True)

    occ_flat = flatten(zmat, fold_major)
    vir_flat = flatten(acc, fold_minor)
    slot = iota((own, pairs), 0)
    occ_out[row // own] = occ_out[row // own] + jnp.where(slot == row % own, occ_flat, 0.0)
    vir_acc[home] = vir_acc[home] + jnp.where(slot == block % own, vir_flat, 0.0)

    @pl.when(t == pl.num_programs(0) - 1)
    def _():
        vir_out[...] = vir_acc[...].astype(vir_out.dtype)


def tiles(sizes, rows, owners, blocks, occ, vir, adj, three, n_dev, n_aux):
    count, pairs, naux = three.shape
    own = occ.shape[0] // n_aux
    smem = pl.BlockSpec(memory_space=pltpu.SMEM)
    vmem = pl.BlockSpec(memory_space=pltpu.VMEM)
    return pl.pallas_call(
        functools.partial(tile_kernel, n_aux, own),
        grid=(count,),
        out_shape=(
            jax.ShapeDtypeStruct((n_aux, own, pairs), F32),
            jax.ShapeDtypeStruct((n_dev, own, pairs), BF16),
        ),
        in_specs=[smem] * 4 + [vmem] * 3 + [pl.BlockSpec((1, pairs, naux), lambda t: (t, 0, 0))],
        out_specs=(vmem, vmem),
        scratch_shapes=[pltpu.VMEM((n_dev, own, pairs), F32)],
        compiler_params=pltpu.CompilerParams(vmem_limit_bytes=48 * 1024 * 1024),
        name="tiles",
    )(sizes, rows, owners, blocks, occ, vir, adj, three)


def exchange_kernel(
    n_blk, n_aux, norm, sizes, occ_ref, vir_ref, occ_out, vir_out, occ_got, vir_got, occ_sems, vir_sems
):
    n_dev = n_blk * n_aux
    b = lax.axis_index("blk")
    a = lax.axis_index("aux")
    me = b * n_aux + a
    barrier = pltpu.get_barrier_semaphore()

    def greet(k, carry):
        p = lax.rem(me + k, n_dev)
        pl.semaphore_signal(barrier, inc=1, device_id=(p // n_aux, p % n_aux), device_id_type=MESH)
        return carry

    lax.fori_loop(1, n_dev, greet, 0)
    pl.semaphore_wait(barrier, n_dev - 1)

    trade(n_blk, n_aux, norm, sizes, occ_ref, vir_ref, occ_out, vir_out, occ_got, vir_got, occ_sems, vir_sems)


def trade(n_blk, n_aux, norm, sizes, occ_ref, vir_ref, occ_out, vir_out, occ_got, vir_got, occ_sems, vir_sems):
    n_dev = n_blk * n_aux
    b = lax.axis_index("blk")
    a = lax.axis_index("aux")
    me = b * n_aux + a
    own, pairs = occ_out.shape

    def vir_copy(k, source):
        p = lax.rem(me + k, n_dev)
        return pltpu.make_async_remote_copy(
            src_ref=vir_ref.at[p],
            dst_ref=vir_got.at[source],
            send_sem=vir_sems.at[0, k],
            recv_sem=vir_sems.at[1, source],
            device_id=(p // n_aux, p % n_aux),
            device_id_type=MESH,
        )

    def occ_copy(k, source):
        q = lax.rem(a + k, n_aux)
        return pltpu.make_async_remote_copy(
            src_ref=occ_ref.at[q],
            dst_ref=occ_got.at[source],
            send_sem=occ_sems.at[0, k],
            recv_sem=occ_sems.at[1, source],
            device_id=(b, q),
            device_id_type=MESH,
        )

    def start_vir(k, carry):
        vir_copy(k, me).start()
        return carry

    def start_occ(k, carry):
        occ_copy(k, a).start()
        return carry

    lax.fori_loop(1, n_dev, start_vir, 0)
    lax.fori_loop(1, n_aux, start_occ, 0)

    def take_vir(k, total):
        source = lax.rem(me + k, n_dev)
        vir_copy(k, source).wait_recv()
        return total + vir_got[source].astype(F32)

    def take_occ(k, total):
        source = lax.rem(a + k, n_aux)
        occ_copy(k, source).wait_recv()
        return total + occ_got[source]

    occ_sum = lax.fori_loop(1, n_aux, take_occ, occ_ref[a])
    vir_sum = lax.fori_loop(1, n_dev, take_vir, vir_ref[me].astype(F32))
    lane = iota((1, pairs), 1)
    for r in range(own):
        size = sizes[a * own + r]
        scale = jnp.where((lane // BS < size) & (lane % BS < size), norm, 0.0).astype(F32)
        occ_out[r : r + 1, :] = occ_sum[r : r + 1, :] * scale
        vir_out[r : r + 1, :] = vir_sum[r : r + 1, :] * scale

    def end_vir(k, carry):
        vir_copy(k, me).wait_send()
        return carry

    def end_occ(k, carry):
        occ_copy(k, a).wait_send()
        return carry

    lax.fori_loop(1, n_dev, end_vir, 0)
    lax.fori_loop(1, n_aux, end_occ, 0)


def exchange(sizes, occ, vir, n_blk, n_aux, norm):
    n_dev, own, pairs = vir.shape
    vmem = pl.BlockSpec(memory_space=pltpu.VMEM)
    out = jax.ShapeDtypeStruct((own, pairs), F32)
    return pl.pallas_call(
        functools.partial(exchange_kernel, n_blk, n_aux, norm),
        out_shape=(out, out),
        in_specs=[pl.BlockSpec(memory_space=pltpu.SMEM), vmem, vmem],
        out_specs=(vmem, vmem),
        scratch_shapes=[
            pltpu.VMEM(occ.shape, occ.dtype),
            pltpu.VMEM(vir.shape, vir.dtype),
            pltpu.SemaphoreType.DMA((2, n_aux)),
            pltpu.SemaphoreType.DMA((2, n_dev)),
        ],
        compiler_params=pltpu.CompilerParams(collective_id=1, has_side_effects=True),
        name="exchange",
    )(sizes, occ, vir)


def shards(
    n_blk, n_aux, adjoint, three_centre, occ_density, vir_density, block_sizes, tile_rows, col_owner, col_block
):
    n_dev = n_blk * n_aux
    count = three_centre.shape[0]
    naux = three_centre.shape[3]
    own = occ_density.shape[0] // n_aux
    depth = adjoint.shape[0]
    three = three_centre.reshape(count, BS * BS, naux)
    if n_aux == 4 and n_blk == 8:
        both = fused(
            block_sizes, tile_rows, col_owner.reshape(count), col_block, adjoint, occ_density, vir_density,
            three_centre, n_blk, n_aux, naux ** -0.5,
        )
        return both[0], both[1]
    aux_here = lax.axis_index("aux")
    own_sizes = lax.dynamic_slice_in_dim(block_sizes, aux_here * own, own, 0)
    own_vir = lax.dynamic_slice_in_dim(vir_density, aux_here * own, own, 0)
    lane = jnp.arange(BS * BS, dtype=jnp.int32)[None, :]
    inside = (lane // BS < own_sizes[:, None]) & (lane % BS < own_sizes[:, None])
    own_vir = jnp.where(inside, own_vir, jnp.zeros_like(own_vir))
    got = lax.all_gather(jnp.concatenate((adjoint, own_vir), axis=0), ("blk", "aux"), axis=0)
    adj = got[:, :depth, :].reshape(naux, naux)
    vir = got[:, depth:, :]
    occ_terms, vir_terms = tiles(
        block_sizes, tile_rows, col_owner.reshape(count), col_block, occ_density, vir, adj,
        three, n_dev, n_aux,
    )
    return exchange(block_sizes, occ_terms, vir_terms, n_blk, n_aux, naux ** -0.5)


def solution(mesh):
    in_specs = (
        P(("blk", "aux"), None),
        P(("blk", "aux"), None, None, None),
        P("blk", None),
        P("blk", None),
        P("blk"),
        P(("blk", "aux")),
        P(("blk", "aux"), None),
        P(("blk", "aux")),
    )
    out_specs = (P(("blk", "aux"), None), P(("blk", "aux"), None))
    body = functools.partial(shards, mesh.shape["blk"], mesh.shape["aux"])
    return jax.shard_map(body, mesh=mesh, in_specs=in_specs, out_specs=out_specs, check_vma=False)
```

```python
import functools

import jax
import jax.numpy as jnp
from jax import lax
from jax.experimental import pallas as pl
from jax.experimental.pallas import tpu as pltpu
from jax.sharding import PartitionSpec as P

BS = 32
SUB = 8
CHUNK = 256
MESH = pl.DeviceIdType.MESH
F32 = jnp.float32
BF16 = jnp.bfloat16


def iota(shape, dim):
    return lax.broadcasted_iota(jnp.int32, shape, dim)


def dot(left, right):
    return jnp.dot(left, right, preferred_element_type=F32)


def dot_nt(left, right):
    return lax.dot_general(left, right, (((1,), (1,)), ((), ())), preferred_element_type=F32)


def fold(rows, lanes, row_key, lane_key):
    return (row_key(iota((rows, lanes), 0)) == lane_key(iota((rows, lanes), 1))).astype(BF16)


def exact(mat, folding):
    high = mat.astype(BF16)
    low = (mat - high.astype(F32)).astype(BF16)
    return dot(high, folding) + dot(low, folding)


def minor(index):
    return index % BS


def inner(index):
    return index // (SUB * SUB) * SUB + index % SUB


def outer(index):
    return index // SUB


def fused_kernel(
    n_blk, n_aux, norm,
    sizes_hbm, rows_hbm, owners_hbm, blocks_hbm, adj_hbm, occ_hbm, vir_hbm, t_hbm,
    out_ref,
    sizes, rows, owners, blocks, occ_ref, vir_ref, got, vgot, tbuf, cbuf, rbuf, ybuf, vir_acc, vir_send, vir_got, occ_send, occ_got,
    in_sem, t_sem, near_sem, recv_sem, send_sem, v_sem, trade_sem,
):
    n_dev = n_blk * n_aux
    depth = n_blk // 2
    count, groups, _, _, naux = tbuf.shape
    pairs = BS * BS
    wide = BS * SUB
    own = out_ref.shape[1]
    arows = adj_hbm.shape[0]
    span = naux // depth
    per_plane = n_dev // depth
    b = lax.axis_index("blk")
    a = lax.axis_index("aux")
    z, y, x, c = b // 2, b % 2, a // 2, a % 2
    col, sides, corner, mates = range(4)
    over_x = (b, (1 - x) * 2 + c)
    over_y = (z * 2 + 1 - y, a)
    across = (z * 2 + 1 - y, (1 - x) * 2 + c)
    mate = (b, x * 2 + 1 - c)
    above, below = (b + 2, a), (b - 2, a)
    has_up, has_down = z < depth - 1, z > 0
    inner_plane = has_up & has_down
    me = b * n_aux + a

    def ident(xx, yy, zz, cc):
        return ((zz * 2 + yy) * 2 + xx) * 2 + cc

    def stand(xx, yy, cc):
        return (yy * 2 + xx) * 2 + cc

    barrier = pltpu.get_barrier_semaphore()

    def tell(sem, device):
        pl.semaphore_signal(sem, inc=1, device_id=device, device_id_type=MESH)

    for device in (over_x, over_y, across, mate):
        tell(barrier, device)
    pl.when(has_up)(lambda: tell(barrier, above))
    pl.when(has_down)(lambda: tell(barrier, below))

    pairs_in = (
        (vir_hbm, vir_ref), (sizes_hbm, sizes), (adj_hbm, got.at[me]),
        (rows_hbm, rows), (occ_hbm, occ_ref), (owners_hbm, owners), (blocks_hbm, blocks),
    )
    fetches = [pltpu.make_async_copy(src, dst, in_sem.at[i]) for i, (src, dst) in enumerate(pairs_in)]
    for fetch in fetches:
        fetch.start()

    lane = iota((1, pairs), 1)
    diag = iota((BS, pairs), 1) // BS == iota((BS, pairs), 0)

    def live(size):
        return (lane // BS < size) & (lane % BS < size)

    def pick(all_rows, at):
        return jnp.sum(jnp.where(iota(all_rows.shape, 0) == at, all_rows, 0.0), axis=0, keepdims=True)

    for fetch in fetches:
        fetch.wait()
    for t in range(count):
        for g in range(groups):
            pltpu.make_async_copy(t_hbm.at[t, :, g], tbuf.at[t, g], t_sem.at[t]).start()
    vir_all = vir_ref[...].astype(F32)
    mine = [jnp.where(live(sizes[a * own + r]), pick(vir_all, a * own + r), 0.0) for r in range(own)]
    vgot[stand(x, y, c), z] = jnp.concatenate(mine, axis=0).astype(BF16)

    pl.semaphore_wait(barrier, 4 + has_up.astype(jnp.int32) + has_down.astype(jnp.int32))

    def send(block, device, kind, zz):
        ref = got.at[block]
        pltpu.make_async_remote_copy(
            src_ref=ref,
            dst_ref=ref,
            send_sem=send_sem,
            recv_sem=recv_sem.at[kind, zz],
            device_id=device,
            device_id_type=MESH,
        ).start()

    def arrive(kind, zz, number):
        part = got.at[pl.ds(0, number)]
        pltpu.make_async_copy(part, part, recv_sem.at[kind, zz]).wait()

    v_col, v_sides, v_mates, v_sent_col, v_sent = range(5)

    def send_v(ref, device, kind):
        pltpu.make_async_remote_copy(
            src_ref=ref,
            dst_ref=ref,
            send_sem=v_sem.at[v_sent_col if kind == v_col else v_sent],
            recv_sem=v_sem.at[kind],
            device_id=device,
            device_id_type=MESH,
        ).start()

    def spread_v(hop):
        mine_v = vgot.at[stand(x, y, c), z]
        pl.when(z + hop < depth)(lambda: send_v(mine_v, (b + 2 * hop, a), v_col))
        pl.when(z - hop >= 0)(lambda: send_v(mine_v, (b - 2 * hop, a), v_col))

    def wait_v(ref, kind):
        pltpu.make_async_copy(ref, ref, v_sem.at[kind]).wait()

    def relay_v_col():
        wait_v(vgot.at[0, pl.ds(0, depth - 1)], v_col)
        column = vgot.at[stand(x, y, c)]
        for device in (across, near_one, near_two):
            send_v(column, device, v_sides)
        send_v(column, mate, v_mates)

    def relay_v_sides():
        wait_v(vgot.at[pl.ds(0, 3)], v_sides)
        for xx, yy in ((1 - x, y), (x, 1 - y), (1 - x, 1 - y)):
            send_v(vgot.at[stand(xx, yy, c)], mate, v_mates)

    def turn(even, odd):
        return tuple(jnp.where(c == 0, i, j) for i, j in zip(even, odd))

    near_one, near_two = turn(over_x, over_y), turn(over_y, over_x)
    spread_v(1)
    send(me, across, corner, z)
    send(me, near_one, sides, z)
    send(me, near_two, sides, z)
    pl.when(has_up)(lambda: send(me, above, col, z))
    pl.when(has_down)(lambda: send(me, below, col, z))
    send(me, mate, mates, z)

    def report(hop):
        pl.when(has_down & (z + hop < depth))(lambda: tell(near_sem.at[0], below))
        pl.when(has_up & (z - hop >= 0))(lambda: tell(near_sem.at[1], above))

    def reach(hop):
        pl.when(z + hop + 1 < depth)(lambda: pl.semaphore_wait(near_sem.at[0], 1))
        pl.when(z - hop - 1 >= 0)(lambda: pl.semaphore_wait(near_sem.at[1], 1))

    def send_far(hop):
        pl.when(z + hop < depth)(lambda: send(me, (b + 2 * hop, a), col, z))
        pl.when(z - hop >= 0)(lambda: send(me, (b - 2 * hop, a), col, z))

    def relay_col(zz):
        block = ident(x, y, zz, c)
        arrive(col, zz, 1)
        pl.when((zz == z - 1) & has_up)(lambda: send(block, above, col, zz))
        pl.when((zz == z + 1) & has_down)(lambda: send(block, below, col, zz))
        send(block, across, corner, zz)
        send(block, near_one, sides, zz)
        send(block, near_two, sides, zz)
        send(block, mate, mates, zz)

    def relay_sides(zz):
        arrive(sides, zz, 2)
        send(ident(1 - x, y, zz, c), mate, mates, zz)
        send(ident(x, 1 - y, zz, c), mate, mates, zz)

    def relay_corner(zz):
        arrive(corner, zz, 1)
        send(ident(1 - x, 1 - y, zz, c), mate, mates, zz)

    def relay_outer(zz):
        pl.when(jnp.logical_not(inner_plane))(lambda: relay_col(zz))

    def ready(zz):
        arrive(mates, zz, 4)

    low = z < depth // 2
    zl = jnp.where(low, z, depth - 1 - z)

    def plane(k):
        near = zl + k // 2 if k % 2 == 0 else zl - (k + 1) // 2
        at = jnp.where(k <= 2 * zl, near, k)
        return jnp.where(low, at, depth - 1 - at)

    order = [plane(k) for k in range(depth)]

    report(1)
    occ_all = occ_ref[...].astype(F32)
    parts = []
    for t in range(count):
        row = jnp.where(live(sizes[rows[t]]), pick(occ_all, rows[t]), 0.0)
        parts.append(jnp.where(diag, row, 0.0))
    square = dot(jnp.concatenate(parts, axis=0).astype(BF16), fold(pairs, wide, minor, outer))
    same_sub = iota((wide, wide), 0) % SUB == iota((wide, wide), 1) % SUB

    def rotate(t):
        spread = jnp.broadcast_to(square[t * BS : (t + 1) * BS][:, None, :], (BS, SUB, wide)).reshape(wide, wide)
        left = jnp.where(same_sub, spread, 0.0).astype(BF16)
        pltpu.make_async_copy(tbuf.at[t], tbuf.at[t], t_sem.at[t]).wait()
        for g in range(groups):
            new = dot(left, tbuf[t, g].reshape(wide, naux)).astype(BF16)
            for zz in range(depth):
                rbuf[t, zz, g] = new[:, zz * span : (zz + 1) * span].reshape(BS, SUB, span)

    def contract(k, t):
        zz = order[k]
        part = got[pl.ds(zz * per_plane, per_plane)].reshape(span, naux)
        for first in range(0, groups, groups // 2):
            rows_of = pl.ds(first, groups // 2)
            new = dot_nt(tbuf[t, rows_of].reshape(pairs // 2, naux), part).astype(BF16)
            cbuf[t, zz, rows_of] = new.reshape(groups // 2, BS, SUB, span)

    def column_term(k, t):
        zz = order[k]
        acc = jnp.zeros((wide, wide), F32) if k == 0 else vir_acc[t]
        for at in range(0, BS, SUB):
            left = cbuf[t, zz, :, at : at + SUB].reshape(wide, span)
            acc = acc + dot_nt(left, rbuf[t, zz, :, at : at + SUB].reshape(wide, span))
        return acc

    reach(1)
    report(2)
    spread_v(2)
    rotate(0)
    reach(2)
    spread_v(3)
    rotate(1)
    relay_col(order[1])
    pl.when(inner_plane)(lambda: relay_col(order[2]))
    rotate(2)
    rotate(3)
    send_far(3)
    relay_sides(z)
    relay_corner(z)
    ready(z)
    same_row = iota((SUB, SUB, wide), 0) == iota((SUB, SUB, wide), 2) % (SUB * SUB) // SUB
    square_v = []

    def prepare():
        wait_v(vgot.at[pl.ds(0, 4)], v_mates)
        parts = []
        for t in range(count):
            slot = blocks[t] // own
            near = vgot[stand(slot // 2, owners[t] % 2, slot % 2), owners[t] // 2]
            parts.append(jnp.where(diag, pick(near.astype(F32), blocks[t] % own), 0.0))
        square_v.append(dot(jnp.concatenate(parts, axis=0).astype(BF16), fold(pairs, wide, minor, inner)))

    def expand(tiles_here):
        for t in tiles_here:
            spread = square_v[0][t * BS : (t + 1) * BS].reshape(groups, 1, SUB, wide)
            spread = jnp.broadcast_to(spread, (groups, SUB, SUB, wide))
            left = jnp.where(same_row, spread, 0.0).reshape(wide, wide).astype(BF16)
            for at in range(0, BS, SUB):
                new = dot(left, tbuf[t, :, at : at + SUB].reshape(wide, naux)).astype(BF16)
                ybuf[t, :, at : at + SUB] = new.reshape(groups, SUB, SUB, naux)

    events = {
        (0, 1): [(lambda zz: relay_v_col(), 1), (relay_sides, 1), (relay_outer, 2), (relay_corner, 1)],
        (1, 0): [(relay_col, 3), (ready, 1)],
        (1, 1): [(lambda zz: relay_v_sides(), 2)],
        (2, 0): [
            (lambda zz: prepare(), 2), (lambda zz: expand((0, 1)), 2), (relay_sides, 2), (relay_corner, 2),
            (lambda zz: expand((2, 3)), 2), (ready, 2),
        ],
        (2, 1): [(relay_sides, 3), (relay_corner, 3)],
        (3, 0): [(ready, 3)],
    }
    for k in range(depth):
        for part in range(2):
            for event, which in events.get((k, part), []):
                event(order[which])
            tiles_here = range(part * count // 2, (part + 1) * count // 2)
            for t in tiles_here:
                contract(k, t)
            for t in tiles_here:
                vir_acc[t] = column_term(k, t)

    lanes_of = iota((SUB, 128), 1) // BS

    def compact(square):
        total = jnp.zeros((SUB, 128), F32)
        for g in range(groups):
            total = jnp.where(lanes_of == g, square[g * SUB : (g + 1) * SUB], total)
        return total

    parts = []
    for t in range(count):
        acc = jnp.where(same_row, vir_acc[t].reshape(groups, SUB, SUB, wide), 0.0)
        parts.append(jnp.sum(acc, axis=1).reshape(BS, wide))
    both = exact(jnp.concatenate(parts, axis=0), fold(wide, 128, inner, minor))
    terms = [compact(both[t * BS : (t + 1) * BS]) for t in range(count)]
    for p in range(n_dev):
        slots = []
        for r in range(own):
            total = jnp.zeros((SUB, 128), F32)
            for t in range(count):
                here = owners[t] * (n_aux * own) + blocks[t] == p * own + r
                total = total + jnp.where(here, terms[t], 0.0)
            slots.append(total)
        vir_send[p] = jnp.concatenate(slots, axis=0).astype(BF16)
    vir_got[me] = vir_send[me]

    def send_vir(p):
        pltpu.make_async_remote_copy(
            src_ref=vir_send.at[p],
            dst_ref=vir_got.at[me],
            send_sem=trade_sem.at[0],
            recv_sem=trade_sem.at[1],
            device_id=(p // n_aux, p % n_aux),
            device_id_type=MESH,
        ).start()

    parts = []
    for t in range(count):
        if t == 0:
            for k in reversed(range(depth)):
                for i in range(0 if k else 1, per_plane):
                    send_vir(order[k] * per_plane + lax.rem(me + i, per_plane))
        acc = jnp.zeros((wide, wide), F32)
        for g in range(groups):
            left = jnp.concatenate([cbuf[t, zz, g].reshape(wide, span) for zz in range(depth)], axis=1)
            acc = acc + dot_nt(left, ybuf[t, g].reshape(wide, naux))
        parts.append(jnp.where(same_sub, acc, 0.0))
    both = exact(jnp.concatenate(parts, axis=0), fold(wide, 128, outer, minor)).reshape(count, groups, SUB, SUB, 128)
    terms = []
    for t in range(count):
        total = jnp.zeros((SUB, SUB, 128), F32)
        for g in range(groups):
            total = jnp.where(lanes_of == g, both[t, g], total)
        terms.append(jnp.sum(total, axis=1))
    for q in range(n_aux):
        slots = []
        for r in range(own):
            total = jnp.zeros((SUB, 128), F32)
            for t in range(count):
                total = total + jnp.where(rows[t] == q * own + r, terms[t], 0.0)
            slots.append(total)
        occ_send[q] = jnp.concatenate(slots, axis=0)
    occ_got[a] = occ_send[a]
    for k in range(1, n_aux):
        q = lax.rem(a + k, n_aux)
        pltpu.make_async_remote_copy(
            src_ref=occ_send.at[q],
            dst_ref=occ_got.at[a],
            send_sem=trade_sem.at[2],
            recv_sem=trade_sem.at[3],
            device_id=(b, q),
            device_id_type=MESH,
        ).start()

    def done(ref, sem):
        pltpu.make_async_copy(ref, ref, sem).wait()

    done(vir_got.at[pl.ds(0, n_dev - 1)], trade_sem.at[1])
    vir_sum = jnp.sum(vir_got[...].astype(F32), axis=0)
    done(occ_got.at[pl.ds(0, n_aux - 1)], trade_sem.at[3])
    occ_sum = jnp.sum(occ_got[...], axis=0)

    sums = jnp.concatenate([occ_sum, vir_sum], axis=0)
    lanes_all = iota(sums.shape, 1) // BS
    parts = [jnp.where(lanes_all == g, sums, 0.0) for g in range(groups)]
    both = exact(jnp.concatenate(parts, axis=0), fold(128, 128, minor, minor))
    both = both.reshape(groups, 2 * own, SUB, 128)
    per_tile = 128 // BS
    lines = []
    for m in range(pairs // 128):
        first = m * per_tile
        here = iota((SUB, 128), 0) == first % SUB + lanes_of
        lines.append(jnp.sum(jnp.where(here, both[first // SUB], 0.0), axis=1))
    flat = jnp.concatenate(lines, axis=1)
    for r in range(own):
        scale = jnp.where(live(sizes[a * own + r]), norm, 0.0).astype(F32)
        out_ref[0, r : r + 1, :] = flat[r : r + 1, :] * scale
        out_ref[1, r : r + 1, :] = flat[own + r : own + r + 1, :] * scale

    done(vir_send.at[pl.ds(0, n_dev - 1)], trade_sem.at[0])
    done(occ_send.at[pl.ds(0, n_aux - 1)], trade_sem.at[2])
    done(vgot.at[0, pl.ds(0, depth - 1)], v_sem.at[v_sent_col])
    done(vgot.at[pl.ds(0, 7)], v_sem.at[v_sent])
    pl.when(inner_plane)(lambda: done(got.at[pl.ds(0, 7 * depth + 4)], send_sem))
    pl.when(jnp.logical_not(inner_plane))(lambda: done(got.at[pl.ds(0, 7 * depth + 2)], send_sem))


def fused(sizes, rows, owners, blocks, adj, occ, vir, three, n_blk, n_aux, norm):
    n_dev = n_blk * n_aux
    count, naux = three.shape[0], three.shape[3]
    own = occ.shape[0] // n_aux
    groups = BS // SUB
    vmem = pl.BlockSpec(memory_space=pltpu.VMEM)
    hbm = pl.BlockSpec(memory_space=pltpu.HBM)
    tile = pltpu.VMEM((count, groups, BS, SUB, naux), BF16)
    by_plane = pltpu.VMEM((count, n_blk // 2, groups, BS, SUB, naux // (n_blk // 2)), BF16)
    return pl.pallas_call(
        functools.partial(fused_kernel, n_blk, n_aux, norm),
        out_shape=pltpu.VMEM((2, own, BS * BS), F32),
        in_specs=[hbm] * 8,
        out_specs=vmem,
        scratch_shapes=[
            *(pltpu.SMEM(scalars.shape, scalars.dtype) for scalars in (sizes, rows, owners, blocks)),
            pltpu.VMEM(occ.shape, BF16),
            pltpu.VMEM(vir.shape, BF16),
            pltpu.VMEM((n_dev, adj.shape[0], naux), BF16),
            pltpu.VMEM((2 * n_aux, n_blk // 2, own, naux), BF16),
            tile,
            by_plane,
            by_plane,
            tile,
            pltpu.VMEM((count, BS * SUB, BS * SUB), F32),
            pltpu.VMEM((n_dev, own * SUB, 128), BF16),
            pltpu.VMEM((n_dev, own * SUB, 128), BF16),
            pltpu.VMEM((n_aux, own * SUB, 128), F32),
            pltpu.VMEM((n_aux, own * SUB, 128), F32),
            pltpu.SemaphoreType.DMA((7,)),
            pltpu.SemaphoreType.DMA((count,)),
            pltpu.SemaphoreType.REGULAR((2,)),
            pltpu.SemaphoreType.DMA((4, n_blk // 2)),
            pltpu.SemaphoreType.DMA,
            pltpu.SemaphoreType.DMA((5,)),
            pltpu.SemaphoreType.DMA((4,)),
        ],
        compiler_params=pltpu.CompilerParams(
            collective_id=0, has_side_effects=True, vmem_limit_bytes=60 << 20
        ),
        name="fused",
    )(sizes, rows, owners, blocks, adj, occ, vir, three.reshape(count, BS, groups, SUB, naux))


def tile_kernel(
    n_aux, own, sizes, rows, owners, blocks, occ_ref, vir_ref, adj_ref, t_ref, occ_out, vir_out, vir_acc
):
    t = pl.program_id(0)
    pairs = BS * BS
    naux = adj_ref.shape[0]

    @pl.when(t == 0)
    def _():
        occ_out[...] = jnp.zeros_like(occ_out)
        vir_acc[...] = jnp.zeros_like(vir_acc)

    row, owner, block = rows[t], owners[t], blocks[t]
    size = sizes[row]
    lane = iota((1, pairs), 1)
    inside = (lane // BS < size) & (lane % BS < size)
    occ_all = occ_ref[...].astype(F32)
    occ_row = jnp.sum(jnp.where(iota(occ_all.shape, 0) == row, occ_all, 0.0), axis=0, keepdims=True)
    occ_row = jnp.where(inside, occ_row, 0.0)
    home = owner * n_aux + block // own
    vir_all = vir_ref[home].astype(F32)
    vir_row = jnp.sum(jnp.where(iota(vir_all.shape, 0) == block % own, vir_all, 0.0), axis=0, keepdims=True)
    diag = iota((BS, pairs), 1) // BS == iota((BS, pairs), 0)
    fold_minor = (iota((pairs, 128), 0) % BS == iota((pairs, 128), 1) % BS).astype(BF16)
    fold_major = (iota((pairs, 128), 0) // BS == iota((pairs, 128), 1) % BS).astype(BF16)
    spread = (iota((128, pairs), 0) == iota((128, pairs), 1) // BS).astype(BF16)
    repeat = pairs // 128

    def square(flat):
        return jnp.dot(jnp.where(diag, flat, 0.0).astype(BF16), fold_minor, preferred_element_type=F32)

    occ_rep = jnp.dot(square(occ_row).astype(BF16), spread, preferred_element_type=F32)
    vir_rep = jnp.concatenate([square(vir_row)] * repeat, axis=1)

    nt = (((1,), (1,)), ((), ()))
    acc = jnp.zeros((BS, pairs), F32)
    lines = []
    for first in range(0, pairs, CHUNK):
        part = lax.dot_general(t_ref[0, first : first + CHUNK, :], adj_ref[...], nt, preferred_element_type=F32)
        gram = lax.dot_general(part.astype(BF16), t_ref[0], nt, preferred_element_type=F32)
        for at in range(CHUNK // BS):
            i = first // BS + at
            block_i = gram[at * BS : (at + 1) * BS, :]
            acc = acc + block_i * occ_rep[i : i + 1, :]
            lines.append(jnp.sum(block_i * vir_rep, axis=0, keepdims=True))
    zmat = jnp.concatenate(lines, axis=0)

    def flatten(mat, fold):
        high = mat.astype(BF16)
        low = (mat - high.astype(F32)).astype(BF16)
        both = jnp.dot(high, fold, preferred_element_type=F32) + jnp.dot(low, fold, preferred_element_type=F32)
        wide = jnp.concatenate([both] * repeat, axis=1)
        return jnp.sum(jnp.where(diag, wide, 0.0), axis=0, keepdims=True)

    occ_flat = flatten(zmat, fold_major)
    vir_flat = flatten(acc, fold_minor)
    slot = iota((own, pairs), 0)
    occ_out[row // own] = occ_out[row // own] + jnp.where(slot == row % own, occ_flat, 0.0)
    vir_acc[home] = vir_acc[home] + jnp.where(slot == block % own, vir_flat, 0.0)

    @pl.when(t == pl.num_programs(0) - 1)
    def _():
        vir_out[...] = vir_acc[...].astype(vir_out.dtype)


def tiles(sizes, rows, owners, blocks, occ, vir, adj, three, n_dev, n_aux):
    count, pairs, naux = three.shape
    own = occ.shape[0] // n_aux
    smem = pl.BlockSpec(memory_space=pltpu.SMEM)
    vmem = pl.BlockSpec(memory_space=pltpu.VMEM)
    return pl.pallas_call(
        functools.partial(tile_kernel, n_aux, own),
        grid=(count,),
        out_shape=(
            jax.ShapeDtypeStruct((n_aux, own, pairs), F32),
            jax.ShapeDtypeStruct((n_dev, own, pairs), BF16),
        ),
        in_specs=[smem] * 4 + [vmem] * 3 + [pl.BlockSpec((1, pairs, naux), lambda t: (t, 0, 0))],
        out_specs=(vmem, vmem),
        scratch_shapes=[pltpu.VMEM((n_dev, own, pairs), F32)],
        compiler_params=pltpu.CompilerParams(vmem_limit_bytes=48 * 1024 * 1024),
        name="tiles",
    )(sizes, rows, owners, blocks, occ, vir, adj, three)


def exchange_kernel(
    n_blk, n_aux, norm, sizes, occ_ref, vir_ref, occ_out, vir_out, occ_got, vir_got, occ_sems, vir_sems
):
    n_dev = n_blk * n_aux
    b = lax.axis_index("blk")
    a = lax.axis_index("aux")
    me = b * n_aux + a
    barrier = pltpu.get_barrier_semaphore()

    def greet(k, carry):
        p = lax.rem(me + k, n_dev)
        pl.semaphore_signal(barrier, inc=1, device_id=(p // n_aux, p % n_aux), device_id_type=MESH)
        return carry

    lax.fori_loop(1, n_dev, greet, 0)
    pl.semaphore_wait(barrier, n_dev - 1)

    trade(n_blk, n_aux, norm, sizes, occ_ref, vir_ref, occ_out, vir_out, occ_got, vir_got, occ_sems, vir_sems)


def trade(n_blk, n_aux, norm, sizes, occ_ref, vir_ref, occ_out, vir_out, occ_got, vir_got, occ_sems, vir_sems):
    n_dev = n_blk * n_aux
    b = lax.axis_index("blk")
    a = lax.axis_index("aux")
    me = b * n_aux + a
    own, pairs = occ_out.shape

    def vir_copy(k, source):
        p = lax.rem(me + k, n_dev)
        return pltpu.make_async_remote_copy(
            src_ref=vir_ref.at[p],
            dst_ref=vir_got.at[source],
            send_sem=vir_sems.at[0, k],
            recv_sem=vir_sems.at[1, source],
            device_id=(p // n_aux, p % n_aux),
            device_id_type=MESH,
        )

    def occ_copy(k, source):
        q = lax.rem(a + k, n_aux)
        return pltpu.make_async_remote_copy(
            src_ref=occ_ref.at[q],
            dst_ref=occ_got.at[source],
            send_sem=occ_sems.at[0, k],
            recv_sem=occ_sems.at[1, source],
            device_id=(b, q),
            device_id_type=MESH,
        )

    def start_vir(k, carry):
        vir_copy(k, me).start()
        return carry

    def start_occ(k, carry):
        occ_copy(k, a).start()
        return carry

    lax.fori_loop(1, n_dev, start_vir, 0)
    lax.fori_loop(1, n_aux, start_occ, 0)

    def take_vir(k, total):
        source = lax.rem(me + k, n_dev)
        vir_copy(k, source).wait_recv()
        return total + vir_got[source].astype(F32)

    def take_occ(k, total):
        source = lax.rem(a + k, n_aux)
        occ_copy(k, source).wait_recv()
        return total + occ_got[source]

    occ_sum = lax.fori_loop(1, n_aux, take_occ, occ_ref[a])
    vir_sum = lax.fori_loop(1, n_dev, take_vir, vir_ref[me].astype(F32))
    lane = iota((1, pairs), 1)
    for r in range(own):
        size = sizes[a * own + r]
        scale = jnp.where((lane // BS < size) & (lane % BS < size), norm, 0.0).astype(F32)
        occ_out[r : r + 1, :] = occ_sum[r : r + 1, :] * scale
        vir_out[r : r + 1, :] = vir_sum[r : r + 1, :] * scale

    def end_vir(k, carry):
        vir_copy(k, me).wait_send()
        return carry

    def end_occ(k, carry):
        occ_copy(k, a).wait_send()
        return carry

    lax.fori_loop(1, n_dev, end_vir, 0)
    lax.fori_loop(1, n_aux, end_occ, 0)


def exchange(sizes, occ, vir, n_blk, n_aux, norm):
    n_dev, own, pairs = vir.shape
    vmem = pl.BlockSpec(memory_space=pltpu.VMEM)
    out = jax.ShapeDtypeStruct((own, pairs), F32)
    return pl.pallas_call(
        functools.partial(exchange_kernel, n_blk, n_aux, norm),
        out_shape=(out, out),
        in_specs=[pl.BlockSpec(memory_space=pltpu.SMEM), vmem, vmem],
        out_specs=(vmem, vmem),
        scratch_shapes=[
            pltpu.VMEM(occ.shape, occ.dtype),
            pltpu.VMEM(vir.shape, vir.dtype),
            pltpu.SemaphoreType.DMA((2, n_aux)),
            pltpu.SemaphoreType.DMA((2, n_dev)),
        ],
        compiler_params=pltpu.CompilerParams(collective_id=1, has_side_effects=True),
        name="exchange",
    )(sizes, occ, vir)


def shards(
    n_blk, n_aux, adjoint, three_centre, occ_density, vir_density, block_sizes, tile_rows, col_owner, col_block
):
    n_dev = n_blk * n_aux
    count = three_centre.shape[0]
    naux = three_centre.shape[3]
    own = occ_density.shape[0] // n_aux
    depth = adjoint.shape[0]
    three = three_centre.reshape(count, BS * BS, naux)
    if n_aux == 4 and n_blk == 8:
        both = fused(
            block_sizes, tile_rows, col_owner.reshape(count), col_block, adjoint, occ_density, vir_density,
            three_centre, n_blk, n_aux, naux ** -0.5,
        )
        return both[0], both[1]
    aux_here = lax.axis_index("aux")
    own_sizes = lax.dynamic_slice_in_dim(block_sizes, aux_here * own, own, 0)
    own_vir = lax.dynamic_slice_in_dim(vir_density, aux_here * own, own, 0)
    lane = jnp.arange(BS * BS, dtype=jnp.int32)[None, :]
    inside = (lane // BS < own_sizes[:, None]) & (lane % BS < own_sizes[:, None])
    own_vir = jnp.where(inside, own_vir, jnp.zeros_like(own_vir))
    got = lax.all_gather(jnp.concatenate((adjoint, own_vir), axis=0), ("blk", "aux"), axis=0)
    adj = got[:, :depth, :].reshape(naux, naux)
    vir = got[:, depth:, :]
    occ_terms, vir_terms = tiles(
        block_sizes, tile_rows, col_owner.reshape(count), col_block, occ_density, vir, adj,
        three, n_dev, n_aux,
    )
    return exchange(block_sizes, occ_terms, vir_terms, n_blk, n_aux, naux ** -0.5)


def solution(mesh):
    in_specs = (
        P(("blk", "aux"), None),
        P(("blk", "aux"), None, None, None),
        P("blk", None),
        P("blk", None),
        P("blk"),
        P(("blk", "aux")),
        P(("blk", "aux"), None),
        P(("blk", "aux")),
    )
    out_specs = (P(("blk", "aux"), None), P(("blk", "aux"), None))
    body = functools.partial(shards, mesh.shape["blk"], mesh.shape["aux"])
    return jax.shard_map(body, mesh=mesh, in_specs=in_specs, out_specs=out_specs, check_vma=False)
```

```python
import functools

import jax
import jax.numpy as jnp
from jax import lax
from jax.experimental import pallas as pl
from jax.experimental.pallas import tpu as pltpu
from jax.sharding import PartitionSpec as P

BS = 32
SUB = 8
CHUNK = 256
MESH = pl.DeviceIdType.MESH
F32 = jnp.float32
BF16 = jnp.bfloat16


def iota(shape, dim):
    return lax.broadcasted_iota(jnp.int32, shape, dim)


def dot(left, right):
    return jnp.dot(left, right, preferred_element_type=F32)


def dot_nt(left, right):
    return lax.dot_general(left, right, (((1,), (1,)), ((), ())), preferred_element_type=F32)


def fold(rows, lanes, row_key, lane_key):
    return (row_key(iota((rows, lanes), 0)) == lane_key(iota((rows, lanes), 1))).astype(BF16)


def exact(mat, folding):
    high = mat.astype(BF16)
    low = (mat - high.astype(F32)).astype(BF16)
    return dot(high, folding) + dot(low, folding)


def minor(index):
    return index % BS


def inner(index):
    return index // (SUB * SUB) * SUB + index % SUB


def outer(index):
    return index // SUB


def fused_kernel(
    n_blk, n_aux, norm,
    sizes_hbm, rows_hbm, owners_hbm, blocks_hbm, adj_hbm, occ_hbm, vir_hbm, t_hbm,
    out_ref,
    sizes, rows, owners, blocks, occ_ref, vir_ref, got, vgot, tbuf, cbuf, rbuf, ybuf, vir_acc, vir_send, vir_got, occ_send, occ_got,
    in_sem, t_sem, near_sem, recv_sem, send_sem, v_sem, trade_sem,
):
    n_dev = n_blk * n_aux
    depth = n_blk // 2
    count, groups, _, _, naux = tbuf.shape
    pairs = BS * BS
    wide = BS * SUB
    own = out_ref.shape[1]
    arows = adj_hbm.shape[0]
    span = naux // depth
    per_plane = n_dev // depth
    b = lax.axis_index("blk")
    a = lax.axis_index("aux")
    z, y, x, c = b // 2, b % 2, a // 2, a % 2
    col, sides, corner, mates = range(4)
    over_x = (b, (1 - x) * 2 + c)
    over_y = (z * 2 + 1 - y, a)
    across = (z * 2 + 1 - y, (1 - x) * 2 + c)
    mate = (b, x * 2 + 1 - c)
    above, below = (b + 2, a), (b - 2, a)
    has_up, has_down = z < depth - 1, z > 0
    inner_plane = has_up & has_down
    me = b * n_aux + a

    def ident(xx, yy, zz, cc):
        return ((zz * 2 + yy) * 2 + xx) * 2 + cc

    def stand(xx, yy, cc):
        return (yy * 2 + xx) * 2 + cc

    barrier = pltpu.get_barrier_semaphore()

    def tell(sem, device):
        pl.semaphore_signal(sem, inc=1, device_id=device, device_id_type=MESH)

    for device in (over_x, over_y, across, mate):
        tell(barrier, device)
    pl.when(has_up)(lambda: tell(barrier, above))
    pl.when(has_down)(lambda: tell(barrier, below))

    pairs_in = (
        (vir_hbm, vir_ref), (sizes_hbm, sizes), (adj_hbm, got.at[me]),
        (rows_hbm, rows), (occ_hbm, occ_ref), (owners_hbm, owners), (blocks_hbm, blocks),
    )
    fetches = [pltpu.make_async_copy(src, dst, in_sem.at[i]) for i, (src, dst) in enumerate(pairs_in)]
    for fetch in fetches:
        fetch.start()

    lane = iota((1, pairs), 1)
    diag = iota((BS, pairs), 1) // BS == iota((BS, pairs), 0)

    def live(size):
        return (lane // BS < size) & (lane % BS < size)

    def pick(all_rows, at):
        return jnp.sum(jnp.where(iota(all_rows.shape, 0) == at, all_rows, 0.0), axis=0, keepdims=True)

    for fetch in fetches:
        fetch.wait()
    for t in range(count):
        for g in range(groups):
            pltpu.make_async_copy(t_hbm.at[t, :, g], tbuf.at[t, g], t_sem.at[t]).start()
    vir_all = vir_ref[...].astype(F32)
    mine = [jnp.where(live(sizes[a * own + r]), pick(vir_all, a * own + r), 0.0) for r in range(own)]
    vgot[stand(x, y, c), z] = jnp.concatenate(mine, axis=0).astype(BF16)

    pl.semaphore_wait(barrier, 4 + has_up.astype(jnp.int32) + has_down.astype(jnp.int32))

    def send(block, device, kind, zz):
        ref = got.at[block]
        pltpu.make_async_remote_copy(
            src_ref=ref,
            dst_ref=ref,
            send_sem=send_sem,
            recv_sem=recv_sem.at[kind, zz],
            device_id=device,
            device_id_type=MESH,
        ).start()

    def arrive(kind, zz, number):
        part = got.at[pl.ds(0, number)]
        pltpu.make_async_copy(part, part, recv_sem.at[kind, zz]).wait()

    v_col, v_sides, v_mates, v_sent_col, v_sent = range(5)

    def send_v(ref, device, kind):
        pltpu.make_async_remote_copy(
            src_ref=ref,
            dst_ref=ref,
            send_sem=v_sem.at[v_sent_col if kind == v_col else v_sent],
            recv_sem=v_sem.at[kind],
            device_id=device,
            device_id_type=MESH,
        ).start()

    def spread_v(hop):
        mine_v = vgot.at[stand(x, y, c), z]
        pl.when(z + hop < depth)(lambda: send_v(mine_v, (b + 2 * hop, a), v_col))
        pl.when(z - hop >= 0)(lambda: send_v(mine_v, (b - 2 * hop, a), v_col))

    def wait_v(ref, kind):
        pltpu.make_async_copy(ref, ref, v_sem.at[kind]).wait()

    def relay_v_col():
        wait_v(vgot.at[0, pl.ds(0, depth - 1)], v_col)
        column = vgot.at[stand(x, y, c)]
        for device in (across, near_one, near_two):
            send_v(column, device, v_sides)
        send_v(column, mate, v_mates)

    def relay_v_sides():
        wait_v(vgot.at[pl.ds(0, 3)], v_sides)
        for xx, yy in ((1 - x, y), (x, 1 - y), (1 - x, 1 - y)):
            send_v(vgot.at[stand(xx, yy, c)], mate, v_mates)

    def turn(even, odd):
        return tuple(jnp.where(c == 0, i, j) for i, j in zip(even, odd))

    near_one, near_two = turn(over_x, over_y), turn(over_y, over_x)
    spread_v(1)
    send(me, across, corner, z)
    send(me, near_one, sides, z)
    send(me, near_two, sides, z)
    pl.when(has_up)(lambda: send(me, above, col, z))
    pl.when(has_down)(lambda: send(me, below, col, z))
    send(me, mate, mates, z)

    def report(hop):
        pl.when(has_down & (z + hop < depth))(lambda: tell(near_sem.at[0], below))
        pl.when(has_up & (z - hop >= 0))(lambda: tell(near_sem.at[1], above))

    def reach(hop):
        pl.when(z + hop + 1 < depth)(lambda: pl.semaphore_wait(near_sem.at[0], 1))
        pl.when(z - hop - 1 >= 0)(lambda: pl.semaphore_wait(near_sem.at[1], 1))

    def send_far(hop):
        pl.when(z + hop < depth)(lambda: send(me, (b + 2 * hop, a), col, z))
        pl.when(z - hop >= 0)(lambda: send(me, (b - 2 * hop, a), col, z))

    def relay_col(zz):
        block = ident(x, y, zz, c)
        arrive(col, zz, 1)
        pl.when((zz == z - 1) & has_up)(lambda: send(block, above, col, zz))
        pl.when((zz == z + 1) & has_down)(lambda: send(block, below, col, zz))
        send(block, across, corner, zz)
        send(block, near_one, sides, zz)
        send(block, near_two, sides, zz)
        send(block, mate, mates, zz)

    def relay_sides(zz):
        arrive(sides, zz, 2)
        send(ident(1 - x, y, zz, c), mate, mates, zz)
        send(ident(x, 1 - y, zz, c), mate, mates, zz)

    def relay_corner(zz):
        arrive(corner, zz, 1)
        send(ident(1 - x, 1 - y, zz, c), mate, mates, zz)

    def relay_outer(zz):
        pl.when(jnp.logical_not(inner_plane))(lambda: relay_col(zz))

    def ready(zz):
        arrive(mates, zz, 4)

    low = z < depth // 2
    zl = jnp.where(low, z, depth - 1 - z)

    def plane(k):
        near = zl + k // 2 if k % 2 == 0 else zl - (k + 1) // 2
        at = jnp.where(k <= 2 * zl, near, k)
        return jnp.where(low, at, depth - 1 - at)

    order = [plane(k) for k in range(depth)]

    report(1)
    occ_all = occ_ref[...].astype(F32)
    parts = []
    for t in range(count):
        row = jnp.where(live(sizes[rows[t]]), pick(occ_all, rows[t]), 0.0)
        parts.append(jnp.where(diag, row, 0.0))
    square = dot(jnp.concatenate(parts, axis=0).astype(BF16), fold(pairs, wide, minor, outer))
    same_sub = iota((wide, wide), 0) % SUB == iota((wide, wide), 1) % SUB

    def rotate(t):
        spread = jnp.broadcast_to(square[t * BS : (t + 1) * BS][:, None, :], (BS, SUB, wide)).reshape(wide, wide)
        left = jnp.where(same_sub, spread, 0.0).astype(BF16)
        pltpu.make_async_copy(tbuf.at[t], tbuf.at[t], t_sem.at[t]).wait()
        for g in range(groups):
            new = dot(left, tbuf[t, g].reshape(wide, naux)).astype(BF16)
            for zz in range(depth):
                rbuf[t, zz, g] = new[:, zz * span : (zz + 1) * span].reshape(BS, SUB, span)

    def contract(k, t):
        zz = order[k]
        part = got[pl.ds(zz * per_plane, per_plane)].reshape(span, naux)
        for first in range(0, groups, groups // 2):
            rows_of = pl.ds(first, groups // 2)
            new = dot_nt(tbuf[t, rows_of].reshape(pairs // 2, naux), part).astype(BF16)
            cbuf[t, zz, rows_of] = new.reshape(groups // 2, BS, SUB, span)

    def column_term(k, t):
        zz = order[k]
        acc = jnp.zeros((wide, wide), F32) if k == 0 else vir_acc[t]
        for at in range(0, BS, SUB):
            left = cbuf[t, zz, :, at : at + SUB].reshape(wide, span)
            acc = acc + dot_nt(left, rbuf[t, zz, :, at : at + SUB].reshape(wide, span))
        return acc

    reach(1)
    report(2)
    spread_v(2)
    rotate(0)
    reach(2)
    spread_v(3)
    rotate(1)
    relay_col(order[1])
    pl.when(inner_plane)(lambda: relay_col(order[2]))
    rotate(2)
    rotate(3)
    send_far(3)
    relay_sides(z)
    relay_corner(z)
    ready(z)
    same_row = iota((SUB, SUB, wide), 0) == iota((SUB, SUB, wide), 2) % (SUB * SUB) // SUB
    square_v = []

    def prepare():
        wait_v(vgot.at[pl.ds(0, 4)], v_mates)
        parts = []
        for t in range(count):
            slot = blocks[t] // own
            near = vgot[stand(slot // 2, owners[t] % 2, slot % 2), owners[t] // 2]
            parts.append(jnp.where(diag, pick(near.astype(F32), blocks[t] % own), 0.0))
        square_v.append(dot(jnp.concatenate(parts, axis=0).astype(BF16), fold(pairs, wide, minor, inner)))

    def expand(tiles_here):
        for t in tiles_here:
            spread = square_v[0][t * BS : (t + 1) * BS].reshape(groups, 1, SUB, wide)
            spread = jnp.broadcast_to(spread, (groups, SUB, SUB, wide))
            left = jnp.where(same_row, spread, 0.0).reshape(wide, wide).astype(BF16)
            for at in range(0, BS, SUB):
                new = dot(left, tbuf[t, :, at : at + SUB].reshape(wide, naux)).astype(BF16)
                ybuf[t, :, at : at + SUB] = new.reshape(groups, SUB, SUB, naux)

    events = {
        (0, 1): [(lambda zz: relay_v_col(), 1), (relay_sides, 1), (relay_outer, 2), (relay_corner, 1)],
        (1, 0): [(relay_col, 3), (ready, 1)],
        (1, 1): [(lambda zz: relay_v_sides(), 2)],
        (2, 0): [
            (lambda zz: prepare(), 2), (lambda zz: expand((0, 1)), 2), (relay_sides, 2), (relay_corner, 2),
            (lambda zz: expand((2, 3)), 2), (ready, 2),
        ],
        (2, 1): [(relay_sides, 3), (relay_corner, 3)],
        (3, 0): [(ready, 3)],
    }
    for k in range(depth):
        for part in range(2):
            for event, which in events.get((k, part), []):
                event(order[which])
            tiles_here = range(part * count // 2, (part + 1) * count // 2)
            for t in tiles_here:
                contract(k, t)
            for t in tiles_here:
                vir_acc[t] = column_term(k, t)

    lanes_of = iota((SUB, 128), 1) // BS

    def compact(square):
        total = jnp.zeros((SUB, 128), F32)
        for g in range(groups):
            total = jnp.where(lanes_of == g, square[g * SUB : (g + 1) * SUB], total)
        return total

    parts = []
    for t in range(count):
        acc = jnp.where(same_row, vir_acc[t].reshape(groups, SUB, SUB, wide), 0.0)
        parts.append(jnp.sum(acc, axis=1).reshape(BS, wide))
    both = exact(jnp.concatenate(parts, axis=0), fold(wide, 128, inner, minor))
    terms = [compact(both[t * BS : (t + 1) * BS]) for t in range(count)]
    for p in range(n_dev):
        slots = []
        for r in range(own):
            total = jnp.zeros((SUB, 128), F32)
            for t in range(count):
                here = owners[t] * (n_aux * own) + blocks[t] == p * own + r
                total = total + jnp.where(here, terms[t], 0.0)
            slots.append(total)
        vir_send[p] = jnp.concatenate(slots, axis=0).astype(BF16)
    vir_got[me] = vir_send[me]

    def send_vir(p):
        pltpu.make_async_remote_copy(
            src_ref=vir_send.at[p],
            dst_ref=vir_got.at[me],
            send_sem=trade_sem.at[0],
            recv_sem=trade_sem.at[1],
            device_id=(p // n_aux, p % n_aux),
            device_id_type=MESH,
        ).start()

    parts = []
    for t in range(count):
        if t == 0:
            for k in reversed(range(depth)):
                for i in range(0 if k else 1, per_plane):
                    send_vir(order[k] * per_plane + lax.rem(me + i, per_plane))
        acc = jnp.zeros((wide, wide), F32)
        for g in range(groups):
            left = jnp.concatenate([cbuf[t, zz, g].reshape(wide, span) for zz in range(depth)], axis=1)
            acc = acc + dot_nt(left, ybuf[t, g].reshape(wide, naux))
        parts.append(jnp.where(same_sub, acc, 0.0))
    both = exact(jnp.concatenate(parts, axis=0), fold(wide, 128, outer, minor)).reshape(count, groups, SUB, SUB, 128)
    terms = []
    for t in range(count):
        total = jnp.zeros((SUB, SUB, 128), F32)
        for g in range(groups):
            total = jnp.where(lanes_of == g, both[t, g], total)
        terms.append(jnp.sum(total, axis=1))
    for q in range(n_aux):
        slots = []
        for r in range(own):
            total = jnp.zeros((SUB, 128), F32)
            for t in range(count):
                total = total + jnp.where(rows[t] == q * own + r, terms[t], 0.0)
            slots.append(total)
        occ_send[q] = jnp.concatenate(slots, axis=0)
    occ_got[a] = occ_send[a]
    for k in range(1, n_aux):
        q = lax.rem(a + k, n_aux)
        pltpu.make_async_remote_copy(
            src_ref=occ_send.at[q],
            dst_ref=occ_got.at[a],
            send_sem=trade_sem.at[2],
            recv_sem=trade_sem.at[3],
            device_id=(b, q),
            device_id_type=MESH,
        ).start()

    def done(ref, sem):
        pltpu.make_async_copy(ref, ref, sem).wait()

    per_tile = 128 // BS
    scales = [jnp.where(live(sizes[a * own + r]), norm, 0.0).astype(F32) for r in range(own)]

    def write(which, sums):
        lanes_all = iota(sums.shape, 1) // BS
        parts = [jnp.where(lanes_all == g, sums, 0.0) for g in range(groups)]
        both = exact(jnp.concatenate(parts, axis=0), fold(128, 128, minor, minor)).reshape(groups, own, SUB, 128)
        lines = []
        for m in range(pairs // 128):
            first = m * per_tile
            here = iota((SUB, 128), 0) == first % SUB + lanes_of
            lines.append(jnp.sum(jnp.where(here, both[first // SUB], 0.0), axis=1))
        flat = jnp.concatenate(lines, axis=1)
        for r in range(own):
            out_ref[which, r : r + 1, :] = flat[r : r + 1, :] * scales[r]

    done(occ_got.at[pl.ds(0, n_aux - 1)], trade_sem.at[3])
    write(0, jnp.sum(occ_got[...], axis=0))
    done(vir_got.at[pl.ds(0, n_dev - 1)], trade_sem.at[1])
    write(1, jnp.sum(vir_got[...].astype(F32), axis=0))

    done(vir_send.at[pl.ds(0, n_dev - 1)], trade_sem.at[0])
    done(occ_send.at[pl.ds(0, n_aux - 1)], trade_sem.at[2])
    done(vgot.at[0, pl.ds(0, depth - 1)], v_sem.at[v_sent_col])
    done(vgot.at[pl.ds(0, 7)], v_sem.at[v_sent])
    pl.when(inner_plane)(lambda: done(got.at[pl.ds(0, 7 * depth + 4)], send_sem))
    pl.when(jnp.logical_not(inner_plane))(lambda: done(got.at[pl.ds(0, 7 * depth + 2)], send_sem))


def fused(sizes, rows, owners, blocks, adj, occ, vir, three, n_blk, n_aux, norm):
    n_dev = n_blk * n_aux
    count, naux = three.shape[0], three.shape[3]
    own = occ.shape[0] // n_aux
    groups = BS // SUB
    vmem = pl.BlockSpec(memory_space=pltpu.VMEM)
    hbm = pl.BlockSpec(memory_space=pltpu.HBM)
    tile = pltpu.VMEM((count, groups, BS, SUB, naux), BF16)
    by_plane = pltpu.VMEM((count, n_blk // 2, groups, BS, SUB, naux // (n_blk // 2)), BF16)
    return pl.pallas_call(
        functools.partial(fused_kernel, n_blk, n_aux, norm),
        out_shape=pltpu.VMEM((2, own, BS * BS), F32),
        in_specs=[hbm] * 8,
        out_specs=vmem,
        scratch_shapes=[
            *(pltpu.SMEM(scalars.shape, scalars.dtype) for scalars in (sizes, rows, owners, blocks)),
            pltpu.VMEM(occ.shape, BF16),
            pltpu.VMEM(vir.shape, BF16),
            pltpu.VMEM((n_dev, adj.shape[0], naux), BF16),
            pltpu.VMEM((2 * n_aux, n_blk // 2, own, naux), BF16),
            tile,
            by_plane,
            by_plane,
            tile,
            pltpu.VMEM((count, BS * SUB, BS * SUB), F32),
            pltpu.VMEM((n_dev, own * SUB, 128), BF16),
            pltpu.VMEM((n_dev, own * SUB, 128), BF16),
            pltpu.VMEM((n_aux, own * SUB, 128), F32),
            pltpu.VMEM((n_aux, own * SUB, 128), F32),
            pltpu.SemaphoreType.DMA((7,)),
            pltpu.SemaphoreType.DMA((count,)),
            pltpu.SemaphoreType.REGULAR((2,)),
            pltpu.SemaphoreType.DMA((4, n_blk // 2)),
            pltpu.SemaphoreType.DMA,
            pltpu.SemaphoreType.DMA((5,)),
            pltpu.SemaphoreType.DMA((4,)),
        ],
        compiler_params=pltpu.CompilerParams(
            collective_id=0, has_side_effects=True, vmem_limit_bytes=60 << 20
        ),
        name="fused",
    )(sizes, rows, owners, blocks, adj, occ, vir, three.reshape(count, BS, groups, SUB, naux))


def tile_kernel(
    n_aux, own, sizes, rows, owners, blocks, occ_ref, vir_ref, adj_ref, t_ref, occ_out, vir_out, vir_acc
):
    t = pl.program_id(0)
    pairs = BS * BS
    naux = adj_ref.shape[0]

    @pl.when(t == 0)
    def _():
        occ_out[...] = jnp.zeros_like(occ_out)
        vir_acc[...] = jnp.zeros_like(vir_acc)

    row, owner, block = rows[t], owners[t], blocks[t]
    size = sizes[row]
    lane = iota((1, pairs), 1)
    inside = (lane // BS < size) & (lane % BS < size)
    occ_all = occ_ref[...].astype(F32)
    occ_row = jnp.sum(jnp.where(iota(occ_all.shape, 0) == row, occ_all, 0.0), axis=0, keepdims=True)
    occ_row = jnp.where(inside, occ_row, 0.0)
    home = owner * n_aux + block // own
    vir_all = vir_ref[home].astype(F32)
    vir_row = jnp.sum(jnp.where(iota(vir_all.shape, 0) == block % own, vir_all, 0.0), axis=0, keepdims=True)
    diag = iota((BS, pairs), 1) // BS == iota((BS, pairs), 0)
    fold_minor = (iota((pairs, 128), 0) % BS == iota((pairs, 128), 1) % BS).astype(BF16)
    fold_major = (iota((pairs, 128), 0) // BS == iota((pairs, 128), 1) % BS).astype(BF16)
    spread = (iota((128, pairs), 0) == iota((128, pairs), 1) // BS).astype(BF16)
    repeat = pairs // 128

    def square(flat):
        return jnp.dot(jnp.where(diag, flat, 0.0).astype(BF16), fold_minor, preferred_element_type=F32)

    occ_rep = jnp.dot(square(occ_row).astype(BF16), spread, preferred_element_type=F32)
    vir_rep = jnp.concatenate([square(vir_row)] * repeat, axis=1)

    nt = (((1,), (1,)), ((), ()))
    acc = jnp.zeros((BS, pairs), F32)
    lines = []
    for first in range(0, pairs, CHUNK):
        part = lax.dot_general(t_ref[0, first : first + CHUNK, :], adj_ref[...], nt, preferred_element_type=F32)
        gram = lax.dot_general(part.astype(BF16), t_ref[0], nt, preferred_element_type=F32)
        for at in range(CHUNK // BS):
            i = first // BS + at
            block_i = gram[at * BS : (at + 1) * BS, :]
            acc = acc + block_i * occ_rep[i : i + 1, :]
            lines.append(jnp.sum(block_i * vir_rep, axis=0, keepdims=True))
    zmat = jnp.concatenate(lines, axis=0)

    def flatten(mat, fold):
        high = mat.astype(BF16)
        low = (mat - high.astype(F32)).astype(BF16)
        both = jnp.dot(high, fold, preferred_element_type=F32) + jnp.dot(low, fold, preferred_element_type=F32)
        wide = jnp.concatenate([both] * repeat, axis=1)
        return jnp.sum(jnp.where(diag, wide, 0.0), axis=0, keepdims=True)

    occ_flat = flatten(zmat, fold_major)
    vir_flat = flatten(acc, fold_minor)
    slot = iota((own, pairs), 0)
    occ_out[row // own] = occ_out[row // own] + jnp.where(slot == row % own, occ_flat, 0.0)
    vir_acc[home] = vir_acc[home] + jnp.where(slot == block % own, vir_flat, 0.0)

    @pl.when(t == pl.num_programs(0) - 1)
    def _():
        vir_out[...] = vir_acc[...].astype(vir_out.dtype)


def tiles(sizes, rows, owners, blocks, occ, vir, adj, three, n_dev, n_aux):
    count, pairs, naux = three.shape
    own = occ.shape[0] // n_aux
    smem = pl.BlockSpec(memory_space=pltpu.SMEM)
    vmem = pl.BlockSpec(memory_space=pltpu.VMEM)
    return pl.pallas_call(
        functools.partial(tile_kernel, n_aux, own),
        grid=(count,),
        out_shape=(
            jax.ShapeDtypeStruct((n_aux, own, pairs), F32),
            jax.ShapeDtypeStruct((n_dev, own, pairs), BF16),
        ),
        in_specs=[smem] * 4 + [vmem] * 3 + [pl.BlockSpec((1, pairs, naux), lambda t: (t, 0, 0))],
        out_specs=(vmem, vmem),
        scratch_shapes=[pltpu.VMEM((n_dev, own, pairs), F32)],
        compiler_params=pltpu.CompilerParams(vmem_limit_bytes=48 * 1024 * 1024),
        name="tiles",
    )(sizes, rows, owners, blocks, occ, vir, adj, three)


def exchange_kernel(
    n_blk, n_aux, norm, sizes, occ_ref, vir_ref, occ_out, vir_out, occ_got, vir_got, occ_sems, vir_sems
):
    n_dev = n_blk * n_aux
    b = lax.axis_index("blk")
    a = lax.axis_index("aux")
    me = b * n_aux + a
    barrier = pltpu.get_barrier_semaphore()

    def greet(k, carry):
        p = lax.rem(me + k, n_dev)
        pl.semaphore_signal(barrier, inc=1, device_id=(p // n_aux, p % n_aux), device_id_type=MESH)
        return carry

    lax.fori_loop(1, n_dev, greet, 0)
    pl.semaphore_wait(barrier, n_dev - 1)

    trade(n_blk, n_aux, norm, sizes, occ_ref, vir_ref, occ_out, vir_out, occ_got, vir_got, occ_sems, vir_sems)


def trade(n_blk, n_aux, norm, sizes, occ_ref, vir_ref, occ_out, vir_out, occ_got, vir_got, occ_sems, vir_sems):
    n_dev = n_blk * n_aux
    b = lax.axis_index("blk")
    a = lax.axis_index("aux")
    me = b * n_aux + a
    own, pairs = occ_out.shape

    def vir_copy(k, source):
        p = lax.rem(me + k, n_dev)
        return pltpu.make_async_remote_copy(
            src_ref=vir_ref.at[p],
            dst_ref=vir_got.at[source],
            send_sem=vir_sems.at[0, k],
            recv_sem=vir_sems.at[1, source],
            device_id=(p // n_aux, p % n_aux),
            device_id_type=MESH,
        )

    def occ_copy(k, source):
        q = lax.rem(a + k, n_aux)
        return pltpu.make_async_remote_copy(
            src_ref=occ_ref.at[q],
            dst_ref=occ_got.at[source],
            send_sem=occ_sems.at[0, k],
            recv_sem=occ_sems.at[1, source],
            device_id=(b, q),
            device_id_type=MESH,
        )

    def start_vir(k, carry):
        vir_copy(k, me).start()
        return carry

    def start_occ(k, carry):
        occ_copy(k, a).start()
        return carry

    lax.fori_loop(1, n_dev, start_vir, 0)
    lax.fori_loop(1, n_aux, start_occ, 0)

    def take_vir(k, total):
        source = lax.rem(me + k, n_dev)
        vir_copy(k, source).wait_recv()
        return total + vir_got[source].astype(F32)

    def take_occ(k, total):
        source = lax.rem(a + k, n_aux)
        occ_copy(k, source).wait_recv()
        return total + occ_got[source]

    occ_sum = lax.fori_loop(1, n_aux, take_occ, occ_ref[a])
    vir_sum = lax.fori_loop(1, n_dev, take_vir, vir_ref[me].astype(F32))
    lane = iota((1, pairs), 1)
    for r in range(own):
        size = sizes[a * own + r]
        scale = jnp.where((lane // BS < size) & (lane % BS < size), norm, 0.0).astype(F32)
        occ_out[r : r + 1, :] = occ_sum[r : r + 1, :] * scale
        vir_out[r : r + 1, :] = vir_sum[r : r + 1, :] * scale

    def end_vir(k, carry):
        vir_copy(k, me).wait_send()
        return carry

    def end_occ(k, carry):
        occ_copy(k, a).wait_send()
        return carry

    lax.fori_loop(1, n_dev, end_vir, 0)
    lax.fori_loop(1, n_aux, end_occ, 0)


def exchange(sizes, occ, vir, n_blk, n_aux, norm):
    n_dev, own, pairs = vir.shape
    vmem = pl.BlockSpec(memory_space=pltpu.VMEM)
    out = jax.ShapeDtypeStruct((own, pairs), F32)
    return pl.pallas_call(
        functools.partial(exchange_kernel, n_blk, n_aux, norm),
        out_shape=(out, out),
        in_specs=[pl.BlockSpec(memory_space=pltpu.SMEM), vmem, vmem],
        out_specs=(vmem, vmem),
        scratch_shapes=[
            pltpu.VMEM(occ.shape, occ.dtype),
            pltpu.VMEM(vir.shape, vir.dtype),
            pltpu.SemaphoreType.DMA((2, n_aux)),
            pltpu.SemaphoreType.DMA((2, n_dev)),
        ],
        compiler_params=pltpu.CompilerParams(collective_id=1, has_side_effects=True),
        name="exchange",
    )(sizes, occ, vir)


def shards(
    n_blk, n_aux, adjoint, three_centre, occ_density, vir_density, block_sizes, tile_rows, col_owner, col_block
):
    n_dev = n_blk * n_aux
    count = three_centre.shape[0]
    naux = three_centre.shape[3]
    own = occ_density.shape[0] // n_aux
    depth = adjoint.shape[0]
    three = three_centre.reshape(count, BS * BS, naux)
    if n_aux == 4 and n_blk == 8:
        both = fused(
            block_sizes, tile_rows, col_owner.reshape(count), col_block, adjoint, occ_density, vir_density,
            three_centre, n_blk, n_aux, naux ** -0.5,
        )
        return both[0], both[1]
    aux_here = lax.axis_index("aux")
    own_sizes = lax.dynamic_slice_in_dim(block_sizes, aux_here * own, own, 0)
    own_vir = lax.dynamic_slice_in_dim(vir_density, aux_here * own, own, 0)
    lane = jnp.arange(BS * BS, dtype=jnp.int32)[None, :]
    inside = (lane // BS < own_sizes[:, None]) & (lane % BS < own_sizes[:, None])
    own_vir = jnp.where(inside, own_vir, jnp.zeros_like(own_vir))
    got = lax.all_gather(jnp.concatenate((adjoint, own_vir), axis=0), ("blk", "aux"), axis=0)
    adj = got[:, :depth, :].reshape(naux, naux)
    vir = got[:, depth:, :]
    occ_terms, vir_terms = tiles(
        block_sizes, tile_rows, col_owner.reshape(count), col_block, occ_density, vir, adj,
        three, n_dev, n_aux,
    )
    return exchange(block_sizes, occ_terms, vir_terms, n_blk, n_aux, naux ** -0.5)


def solution(mesh):
    in_specs = (
        P(("blk", "aux"), None),
        P(("blk", "aux"), None, None, None),
        P("blk", None),
        P("blk", None),
        P("blk"),
        P(("blk", "aux")),
        P(("blk", "aux"), None),
        P(("blk", "aux")),
    )
    out_specs = (P(("blk", "aux"), None), P(("blk", "aux"), None))
    body = functools.partial(shards, mesh.shape["blk"], mesh.shape["aux"])
    return jax.shard_map(body, mesh=mesh, in_specs=in_specs, out_specs=out_specs, check_vma=False)
```
